256 devices in a mesh: phase: 8 (over z_lo, x), ctx: 32 (over y, z_hi, core).
Axes of the slice: x: 4, y: 4, z: 8 (z_hi: 4, z_lo: 2; z = z_hi * 2 + z_lo), core: 2. Of those that a mesh axis runs over, the one named last changes fastest.
Arguments:
- inputs: bfloat16 [1, 4096, 2048], P(None, 'ctx'), may hold values from -6 to 6
- segment_ids: int32 [1, 4096], P(None, 'ctx'), may hold values from 0 to 15, never falling along the last dimension, each value on 1 to 768 neighbouring positions
- w_query: bfloat16 [8, 2048, 1024], P('phase'), may hold values from -1 to 1
- w_keyval: bfloat16 [8, 2048, 2048], P('phase', 'ctx'), may hold values from -16 to 16
- w_out: bfloat16 [8, 1024, 2048], P('phase'), may hold values from -0.1875 to 0.1875
Outputs:
- section_out: bfloat16 [8, 1, 4096, 2048], P('phase', None, 'ctx')
The draws below stay inside these ranges and needn't reach their ends.
Inputs may be any that keep to these rules, and one draw needn't show every extreme that they name: `segment_ids`: ids never fall along the tokens of a micro-batch; each trajectory is a run of 1 to 768 tokens and one run has exactly 768.
All inputs are finite; a program needn't handle non-finite values.
Results may differ from the reference program's by a relative error of at most 0.015.
Values may be sent and summed in bfloat16 or wider, within the bound.
A program may use at most 64 MiB of HBM per device.

```python
import math
import jax
import jax.numpy as jnp
import numpy as np
from jax import lax

D = 2048
HEADS = 8
HEAD = 128
WINDOW = 4
TOK_DEV = 128
MB = 1
LAYERS = 8
TOKENS = 4096
SEGS = 16
SEG_MOST = 768
N_CTX = 32


def shared_query(key):
    base = jax.random.normal(jax.random.fold_in(key, 11), (LAYERS, D, HEADS * HEAD), jnp.float32)
    return base / math.sqrt(D)


def draw_w_query(key, part):
    return shared_query(key).astype(jnp.bfloat16)


def draw_w_keyval(key, part):
    head_width = HEADS * HEAD
    fresh = jax.random.normal(jax.random.fold_in(key, 23), (LAYERS, D, 2 * head_width), jnp.float32) / math.sqrt(D)
    return fresh.astype(jnp.bfloat16)


def block_scale(own_key, shape, pieces, low, largest):
    def one(position, blocks):
        heights = jax.random.uniform(jax.random.fold_in(jax.random.fold_in(own_key, 6), position), (blocks,), jnp.float32, low / len(pieces), largest / len(pieces))
        return jnp.repeat(jnp.exp(heights), shape[position] // blocks).reshape((-1,) + (1,) * (len(shape) - position - 1))

    factor_of = one(*pieces[0])
    for cut in pieces[1:]:
        factor_of = factor_of * one(*cut)
    return factor_of


def split_up(count, total, limit, lean):
    portions = [(1 << 20) // math.isqrt(rank ** lean) + 1 for rank in range(2, count + 1)]
    surplus, given = total - limit - (count - 1), [1] * (count - 1)
    while surplus > 0:
        candidates = [i for i in range(count - 1) if given[i] < limit]
        whole, budget = sum([portions[i] for i in candidates]), surplus
        for i in candidates:
            more = min(limit - given[i], max(1, budget * portions[i] // whole), surplus)
            given[i] = given[i] + more
            surplus = surplus - more
    return np.array([limit] + given)


def uneven(rng, amount, total, limit, slope):
    if amount == 2:
        one = jax.random.randint(rng, (), max(1, total - limit), min(limit, total - 1) + 1)
        return jnp.stack([one, total - one])
    lengths = jnp.asarray(split_up(amount, total, limit, slope), jnp.int32)
    pairs = (amount - 1) // 2
    giver, receiver = lengths[1:1 + 2 * pairs:2], lengths[2:2 + 2 * pairs:2]
    room = jnp.minimum(giver - 1, limit - receiver)
    passed = jax.random.randint(jax.random.fold_in(rng, 1), (pairs,), 0, 1 << 20) % (room + 1)
    lengths = lengths.at[1:1 + 2 * pairs:2].set(giver - passed).at[2:2 + 2 * pairs:2].set(receiver + passed)
    return lengths[jax.random.permutation(jax.random.fold_in(rng, 2), amount)]


def bell_draw(own_key, dims, deviation, reach, split=(), kind=jnp.bfloat16):
    drawn = jax.random.normal(own_key, dims, jnp.float32) * deviation
    if len(split) > 0:
        drawn = block_scale(own_key, dims, split, -0.22, 0.18) * drawn
    return jnp.clip(drawn, min=-reach, max=reach).astype(kind)


def setup_inputs(seed: int = 0) -> dict:
    splits = jax.random.split(jax.random.key(seed), 6)
    inputs = bell_draw(splits[0], (MB, TOKENS, D), 1.0, 6.0, ((1, 32),))
    segment_ids = jax.vmap(lambda own: jnp.searchsorted(jnp.cumsum(uneven(own, SEGS, TOKENS, SEG_MOST, 0)), jnp.arange(TOKENS), side="right"))(jax.random.split(splits[1], MB)).reshape((MB, TOKENS)).astype(jnp.int32)
    w_query = draw_w_query(jax.random.fold_in(splits[5], 71), 0)
    w_keyval = draw_w_keyval(jax.random.fold_in(splits[5], 71), 0)
    w_out = bell_draw(splits[4], (LAYERS, HEADS * HEAD, D), (HEADS * HEAD) ** -0.5, 0.1875, ((0, 8),))
    return dict(inputs=inputs, segment_ids=segment_ids, w_query=w_query, w_keyval=w_keyval, w_out=w_out)


def rms_rows(values):
    widened = values.astype(jnp.float32)
    return (widened * lax.rsqrt(lax.optimization_barrier(jnp.mean(widened * widened, axis=-1, keepdims=True)) + 1e-05)).astype(jnp.bfloat16)

def segment_begin(segments):
    places = jnp.arange(segments.shape[0], dtype=jnp.int32)
    earlier = jnp.concatenate([jnp.full((1,), -1, jnp.int32), segments[:-1]])
    boundary = jnp.where(segments != earlier, places, jnp.zeros_like(places))
    return lax.cummax(boundary, axis=0)

def layer_pass(stream, segments, query_w, keyval_w, out_w):
    normed = rms_rows(stream)
    queries = jnp.dot(normed, query_w, preferred_element_type=jnp.float32).astype(jnp.bfloat16)
    keyvals = jnp.dot(normed, keyval_w, preferred_element_type=jnp.float32).astype(jnp.bfloat16)
    queries = lax.optimization_barrier(queries)
    keyvals = lax.optimization_barrier(keyvals)
    begins = segment_begin(segments)
    head_width = HEADS * HEAD
    padded = jnp.concatenate([jnp.zeros(((WINDOW - 1) * TOK_DEV, 2 * head_width), jnp.bfloat16), keyvals], axis=0)
    score_scale = 1.0 / math.sqrt(HEAD)

    def query_block(block_index):
        first_pos = (block_index * TOK_DEV).astype(jnp.int32)
        query_part = lax.dynamic_slice_in_dim(queries, first_pos, TOK_DEV, 0).reshape(TOK_DEV, HEADS, HEAD).astype(jnp.float32)
        key_rows = lax.dynamic_slice_in_dim(padded, first_pos, WINDOW * TOK_DEV, 0)
        key_part = key_rows[:, :head_width].reshape(-1, HEADS, HEAD).astype(jnp.float32)
        value_part = key_rows[:, head_width:].reshape(-1, HEADS, HEAD).astype(jnp.float32)
        scores = jnp.einsum('qhd,khd->hqk', query_part, key_part) * score_scale
        query_pos = first_pos + jnp.arange(TOK_DEV, dtype=jnp.int32)
        key_pos = first_pos - (WINDOW - 1) * TOK_DEV + jnp.arange(WINDOW * TOK_DEV, dtype=jnp.int32)
        begin_part = lax.dynamic_slice_in_dim(begins, first_pos, TOK_DEV, 0)
        allowed = (key_pos[None, :] <= query_pos[:, None]) & (key_pos[None, :] >= begin_part[:, None])
        scores = jnp.where(allowed[None], scores, -jnp.inf)
        row_top = lax.optimization_barrier(jnp.max(scores, axis=2, keepdims=True))
        weights = jnp.exp(scores - row_top)
        weights = (weights / lax.optimization_barrier(jnp.sum(weights, axis=2, keepdims=True))).astype(jnp.bfloat16)
        weights = lax.optimization_barrier(weights)
        blended = jnp.einsum('hqk,khd->qhd', weights.astype(jnp.float32), value_part)
        return blended.astype(jnp.bfloat16).reshape(TOK_DEV, head_width)
    blocks = lax.map(query_block, jnp.arange(N_CTX, dtype=jnp.int32))
    heads_out = blocks.reshape(TOKENS, head_width)
    update = jnp.dot(heads_out, out_w, preferred_element_type=jnp.float32)
    return (stream.astype(jnp.float32) + update).astype(jnp.bfloat16)

def reference(inputs, segment_ids, w_query, w_keyval, w_out):
    layers_out = []
    for layer_index in range(LAYERS):
        batch_out = []
        for batch_index in range(MB):
            if layer_index == 0:
                stream = inputs[batch_index]
            else:
                stream = layers_out[-1][batch_index]
            batch_out.append(layer_pass(stream, segment_ids[batch_index], w_query[layer_index], w_keyval[layer_index], w_out[layer_index]))
        layers_out.append(jnp.stack(batch_out))
    return jnp.stack(layers_out)
```

```python
import functools
import math

import jax
import jax.numpy as jnp
from jax import lax
from jax.experimental import pallas as pl
from jax.experimental.pallas import tpu as pltpu
from jax.sharding import PartitionSpec as P

MESH = pl.DeviceIdType.MESH
HEAD = 128
BLK = 128
RING = 4


def kernel(
    phases, chips, x_in, seg_in, wq_in, wkv_in, wo_in, out_ref,
    x_v, acc, wq_v, wkv_v, wo_v, wop_v, q_v, kv_v, bl_v, blo_v, bls_v, seg_v, bias_v,
    ssem, rsem, lsem, go_sem,
):
    width = x_v.shape[1]
    rows_dev = wkv_in.shape[0]
    rows_chip = 2 * rows_dev
    ph = lax.axis_index("phase")
    c = lax.axis_index("ctx")
    p = c // 2
    j = c % 2
    y = p // RING
    z = p % RING
    sib = c + 1 - 2 * j

    def at(phase, chip):
        return {"phase": phase, "ctx": chip * 2 + j}

    sibling = {"phase": ph, "ctx": sib}

    def chip_at(dy, dz):
        return ((y + dy + RING) % RING) * RING + (z + dz + RING) % RING

    y_next, y_prev = at(ph, chip_at(1, 0)), at(ph, chip_at(-1, 0))
    z_next, z_prev = at(ph, chip_at(0, 1)), at(ph, chip_at(0, -1))
    next1, next2 = at(ph, jnp.minimum(p + 1, chips - 1)), at(ph, jnp.minimum(p + 2, chips - 1))
    last1, last2 = at(ph, jnp.maximum(p - 1, 0)), at(ph, jnp.maximum(p - 2, 0))
    ph_next, ph_prev = at(jnp.minimum(ph + 1, phases - 1), p), at(jnp.maximum(ph - 1, 0), p)
    ph_over, ph_under = at(jnp.minimum(ph + RING, phases - 1), p), at(jnp.maximum(ph - RING, 0), p)
    has_next1, has_next2 = p + 1 < chips, p + 2 < chips
    has_last1, has_last2 = p >= 1, p >= 2
    is_first, is_last = ph == 0, ph == phases - 1
    has_over, has_under = ph + RING < phases, ph >= RING

    barrier = pltpu.get_barrier_semaphore()
    for device in (sibling, y_next, y_prev, z_next, z_prev):
        pl.semaphore_signal(barrier, inc=1, device_id=device, device_id_type=MESH)
    count = jnp.int32(5)
    for device, there in (
        (next1, has_next1), (next2, has_next2), (last1, has_last1), (last2, has_last2),
        (ph_next, ph + 1 < phases), (ph_prev, ph > 0), (ph_over, has_over), (ph_under, has_under),
    ):
        @pl.when(there)
        def _(device=device):
            pl.semaphore_signal(barrier, inc=1, device_id=device, device_id_type=MESH)

        count = count + there.astype(jnp.int32)
    pl.semaphore_wait(barrier, count)

    pending = []
    slots = iter(range(ssem.shape[0]))

    def copy(src, dst, slot, device):
        return pltpu.make_async_remote_copy(
            src_ref=src, dst_ref=dst, send_sem=ssem.at[slot], recv_sem=rsem.at[slot],
            device_id=device, device_id_type=MESH,
        )

    def send(src, dst, slot, device, when=None):
        made = copy(src, dst, slot, device)
        if when is None:
            made.start()
        else:
            pl.when(when)(made.start)
        pending.append((made, when))
        return made

    def recv(dst, slot):
        copy(dst, dst, slot, sibling).wait_recv()

    def run(when, body):
        pl.when(when)(body)

    local = []

    def load(src, dst):
        made = pltpu.make_async_copy(src, dst, lsem.at[len(local)])
        made.start()
        local.append(made)
        return made

    def columns(core, tile):
        start = core * 4 * HEAD + (tile // 2) * 2 * HEAD + (tile % 2) * 8 * HEAD
        return pl.ds(pl.multiple_of(start, 2 * HEAD), 2 * HEAD)

    own_rows = pl.ds(pl.multiple_of(c * rows_dev, rows_dev), rows_dev)
    shard_loads = [load(wkv_in.at[:, columns(j, t)], wkv_v.at[t, own_rows, :]) for t in range(4)]
    seg_load = load(seg_in, seg_v.at[3 + j])
    mine = pl.ds(pl.multiple_of(j * BLK, BLK), BLK)
    theirs = pl.ds(pl.multiple_of((1 - j) * BLK, BLK), BLK)
    wq_loads = [
        load(wq_in.at[:, pl.ds(pl.multiple_of(j * 4 * HEAD + t * 2 * HEAD, 2 * HEAD), 2 * HEAD)], wq_v.at[t])
        for t in range(2)
    ]
    wo_load = load(wo_in, wo_v)

    sib_rows = pl.ds(pl.multiple_of(sib * rows_dev, rows_dev), rows_dev)
    shard_slots = [next(slots) for _ in range(4)]
    seg_slots = [next(slots) for _ in range(3)]

    pl.when(has_under)(lambda: pl.semaphore_wait(go_sem, 1))
    for t in range(4):
        send(wkv_in.at[:, columns(1 - j, t)], wkv_v.at[t, own_rows, :], shard_slots[t], sibling)
    send(seg_in, seg_v.at[3 + j], seg_slots[0], sibling)

    wop_slots = [next(slots) for _ in range(4)]
    for k in range(4):
        send(wo_in.at[4 * j + k], wop_v.at[4 * j + k], wop_slots[k], ph_next, ph + 1 < phases)
    x_slot = next(slots)
    x_prev_slot = next(slots)
    x_load = pltpu.make_async_copy(x_in, x_v.at[mine], lsem.at[len(local)])
    x_direct = copy(x_in, x_v.at[mine], x_slot, sibling)

    @pl.when(ph < 2)
    def _():
        x_load.start()
        x_direct.start()

    for made in shard_loads:
        made.wait()
    for t in range(4):
        recv(wkv_v.at[t, sib_rows, :], shard_slots[t])

    def slab(chip, first, count_):
        return wkv_v.at[pl.ds(first, count_), pl.ds(pl.multiple_of(chip * rows_chip, rows_chip), rows_chip), :]

    sets = []
    for s in range(2):
        sets.append(dict(
            tile=2 * s,
            prim=(y_next, y_prev) if s == 0 else (z_next, z_prev),
            sec=(z_next, z_prev) if s == 0 else (y_next, y_prev),
            chip=(lambda a, b: chip_at(a, b)) if s == 0 else (lambda a, b: chip_at(b, a)),
            pslot=[next(slots) for _ in range(4)],
            sslot={dp: [next(slots) for _ in range(4)] for dp in (0, -1, 1, 2)},
        ))

    def ring_send(g, ring, slot, dp):
        piece = slab(g["chip"](dp, 0), g["tile"], 2)
        send(piece, piece, slot[0], ring[0])
        send(piece, piece, slot[1], ring[1])

    def ring_forward(g, ring, slot, before, after):
        piece = slab(before, g["tile"], 2)
        recv(piece, slot[0])
        half = slab(before, g["tile"], 1)
        send(half, half, slot[2], ring[0])
        piece = slab(after, g["tile"], 2)
        recv(piece, slot[1])
        half = slab(after, g["tile"] + 1, 1)
        send(half, half, slot[3], ring[1])

    def ring_end(g, slot, far):
        recv(slab(far, g["tile"], 1), slot[2])
        recv(slab(far, g["tile"] + 1, 1), slot[3])

    for g in sets:
        ring_send(g, g["prim"], g["pslot"], 0)
        ring_send(g, g["sec"], g["sslot"][0], 0)
    for g in sets:
        ring_forward(g, g["prim"], g["pslot"], g["chip"](-1, 0), g["chip"](1, 0))
        ring_send(g, g["sec"], g["sslot"][-1], -1)
        ring_send(g, g["sec"], g["sslot"][1], 1)
    for g in sets:
        ring_forward(g, g["sec"], g["sslot"][0], g["chip"](0, -1), g["chip"](0, 1))
    for g in sets:
        ring_end(g, g["pslot"], g["chip"](2, 0))
        ring_send(g, g["sec"], g["sslot"][2], 2)
    for dp in (-1, 1, 2):
        for g in sets:
            ring_forward(g, g["sec"], g["sslot"][dp], g["chip"](dp, -1), g["chip"](dp, 1))

    seg_load.wait()
    recv(seg_v.at[4 - j], seg_slots[0])
    send(seg_v.at[pl.ds(3, 2)], seg_v.at[pl.ds(1, 2)], seg_slots[1], next1, has_next1)
    send(seg_v.at[4], seg_v.at[0], seg_slots[2], next2, has_next2)

    @pl.when(jnp.logical_not(has_last1))
    def _():
        seg_v[1:3] = jnp.full((2,) + seg_v.shape[1:], -1.0, jnp.float32)
        kv_v[:, :, BLK:3 * BLK, :] = jnp.zeros((4, 2, 2 * BLK, HEAD), jnp.bfloat16)

    @pl.when(jnp.logical_not(has_last2))
    def _():
        seg_v[0] = jnp.full(seg_v.shape[1:], -1.0, jnp.float32)
        kv_v[:, :, 0:BLK, :] = jnp.zeros((4, 2, BLK, HEAD), jnp.bfloat16)

    run(has_last1, lambda: recv(seg_v.at[pl.ds(1, 2)], seg_slots[1]))
    run(has_last2, lambda: recv(seg_v.at[0], seg_slots[2]))

    row_id = lax.broadcasted_iota(jnp.int32, (BLK, BLK), 0)
    col_id = lax.broadcasted_iota(jnp.int32, (BLK, BLK), 1)
    causal = col_id <= row_id
    for i in range(2):
        asking = jnp.transpose(jnp.broadcast_to(seg_v[3 + i, 0:1, :], (BLK, BLK)))
        for b in range(4):
            asked = jnp.broadcast_to(seg_v[i + b, 0:1, :], (BLK, BLK))
            ok = asking == asked
            if b == 3:
                ok = ok & causal
            bias_v[i, :, b * BLK:(b + 1) * BLK] = jnp.where(ok, 0.0, -1e30).astype(jnp.float32)

    for dp in (0, -1, 1, 2):
        for g in sets:
            ring_end(g, g["sslot"][dp], g["chip"](dp, 2))
    for made in wq_loads:
        made.wait()
    wo_load.wait()

    @pl.when(has_over)
    def _():
        pl.semaphore_signal(go_sem, inc=1, device_id=ph_over, device_id_type=MESH)

    wop_relay = [next(slots) for _ in range(4)]
    relays = []
    for k in range(4):
        relays.append(copy(wop_v.at[4 * j + k], wop_v.at[4 * j + k], wop_relay[k], sibling))
    x_relay = copy(x_v.at[mine], x_v.at[mine], x_slot, sibling)

    @pl.when(ph > 0)
    def _():
        for k in range(4):
            recv(wop_v.at[4 * j + k], wop_slots[k])
            relays[k].start()

    @pl.when(ph < 2)
    def _():
        x_load.wait()
        x_direct.wait_send()

    @pl.when(ph >= 2)
    def _():
        recv(x_v.at[mine], x_prev_slot)
        x_relay.start()
        x_relay.wait_send()

    recv(x_v.at[theirs], x_slot)

    bl_slots = [next(slots) for _ in range(4)]
    bl_relay_slots = [next(slots) for _ in range(4)]
    bl_relays = [copy(bl_v.at[4 * j + h], bl_v.at[4 * j + h], bl_relay_slots[h], sibling) for h in range(4)]
    step = 512 if width % 512 == 0 else width

    @pl.when(ph > 0)
    def _():
        for k in range(4):
            recv(wop_v.at[4 * (1 - j) + k], wop_relay[k])
        for h in range(4):
            recv(bl_v.at[4 * j + h], bl_slots[h])
            bl_relays[h].start()
            recv(bl_v.at[4 * (1 - j) + h], bl_relay_slots[h])
            lhs = jnp.concatenate([bl_v[h], bl_v[4 + h]], axis=1)
            for n in range(0, width, step):
                rhs = jnp.concatenate([wop_v[h, :, n:n + step], wop_v[4 + h, :, n:n + step]], axis=0)
                part = jnp.dot(lhs, rhs, preferred_element_type=jnp.float32)
                if h == 0:
                    acc[:, n:n + step] = part
                elif h < 3:
                    acc[:, n:n + step] += part
                else:
                    total = x_v[:, n:n + step].astype(jnp.float32) + (acc[:, n:n + step] + part)
                    x_v[:, n:n + step] = total.astype(jnp.bfloat16)

    send(x_v.at[mine], x_v.at[mine], x_prev_slot, ph_next, (ph > 0) & (ph + 1 < phases))

    square = jnp.zeros((2 * BLK, 1), jnp.float32)
    for n in range(0, width, step):
        part = x_v[:, n:n + step].astype(jnp.float32)
        square = square + jnp.sum(part * part, axis=1, keepdims=True)
    scale_rows = lax.rsqrt(square * (1.0 / width) + 1e-05)

    halo_slots = [[next(slots), next(slots)] for _ in range(4)]
    stream = x_v[...]

    def project(weights):
        return (jnp.dot(stream, weights, preferred_element_type=jnp.float32) * scale_rows).astype(jnp.bfloat16)

    for t in range(2):
        for kind in range(2):
            made = project(wkv_v[2 * t + kind])
            kv_v[2 * t, kind, 3 * BLK:5 * BLK, :] = made[:, :HEAD]
            kv_v[2 * t + 1, kind, 3 * BLK:5 * BLK, :] = made[:, HEAD:]
        for h in (2 * t, 2 * t + 1):
            send(kv_v.at[h, :, pl.ds(3 * BLK, 2 * BLK), :], kv_v.at[h, :, pl.ds(BLK, 2 * BLK), :],
                 halo_slots[h][0], next1, has_next1)
            send(kv_v.at[h, :, pl.ds(4 * BLK, BLK), :], kv_v.at[h, :, pl.ds(0, BLK), :],
                 halo_slots[h][1], next2, has_next2)
    for t in range(2):
        made = project(wq_v[t])
        q_v[2 * t] = made[:, :HEAD]
        q_v[2 * t + 1] = made[:, HEAD:]

    bls_slots = [next(slots) for _ in range(4)]
    for h in range(4):
        run(has_last1, lambda h=h: recv(kv_v.at[h, :, pl.ds(BLK, 2 * BLK), :], halo_slots[h][0]))
        run(has_last2, lambda h=h: recv(kv_v.at[h, :, pl.ds(0, BLK), :], halo_slots[h][1]))
        for i in range(2):
            keys = kv_v[h, 0, i * BLK:(i + 4) * BLK, :]
            values = kv_v[h, 1, i * BLK:(i + 4) * BLK, :]
            scores = lax.dot_general(
                q_v[h, i * BLK:(i + 1) * BLK, :], keys, (((1,), (1,)), ((), ())),
                preferred_element_type=jnp.float32,
            )
            scores = scores * (1.0 / math.sqrt(HEAD)) + bias_v[i]
            top = jnp.max(scores, axis=1, keepdims=True)
            weights = jnp.exp(scores - top)
            total = jnp.sum(weights, axis=1, keepdims=True)
            mixed = jnp.dot(weights.astype(jnp.bfloat16), values, preferred_element_type=jnp.float32)
            blo_v[h, i * BLK:(i + 1) * BLK, :] = (mixed / total).astype(jnp.bfloat16)
        send(blo_v.at[h], bl_v.at[4 * j + h], bl_slots[h], ph_next, ph + 1 < phases)
        send(blo_v.at[h, theirs, :], bls_v.at[h], bls_slots[h], sibling)

    for h in range(4):
        recv(bls_v.at[h], bls_slots[h])
    own = jnp.concatenate([blo_v[h, mine, :] for h in range(4)], axis=1)
    other = jnp.concatenate([bls_v[h] for h in range(4)], axis=1)
    for n in range(0, width, step):
        first = wo_v[pl.ds(4 * j, 4), :, n:n + step].reshape(4 * HEAD, step)
        second = wo_v[pl.ds(4 * (1 - j), 4), :, n:n + step].reshape(4 * HEAD, step)
        update = jnp.dot(own, first, preferred_element_type=jnp.float32)
        update = update + jnp.dot(other, second, preferred_element_type=jnp.float32)
        out_ref[:, n:n + step] = (x_v[mine, n:n + step].astype(jnp.float32) + update).astype(jnp.bfloat16)

    for made, when in pending:
        if when is None:
            made.wait_send()
        else:
            pl.when(when)(made.wait_send)

    @pl.when(ph > 0)
    def _():
        for made in relays + bl_relays:
            made.wait_send()


def solution(mesh):
    phases, devices = mesh.shape["phase"], mesh.shape["ctx"]
    chips = devices // 2

    def local(inputs, segment_ids, w_query, w_keyval, w_out):
        width = inputs.shape[2]
        rows_dev = w_keyval.shape[1]
        seg = jnp.broadcast_to(segment_ids.astype(jnp.float32), (8, BLK))
        any_space = pl.BlockSpec(memory_space=pl.ANY)
        n_slots = 96
        made = pl.pallas_call(
            functools.partial(kernel, phases, chips),
            out_shape=jax.ShapeDtypeStruct((BLK, width), jnp.bfloat16),
            in_specs=[any_space] * 5,
            out_specs=pl.BlockSpec(memory_space=pltpu.VMEM),
            scratch_shapes=[
                pltpu.VMEM((2 * BLK, width), jnp.bfloat16),
                pltpu.VMEM((2 * BLK, width), jnp.float32),
                pltpu.VMEM((2, width, 2 * HEAD), jnp.bfloat16),
                pltpu.VMEM((4, width, 2 * HEAD), jnp.bfloat16),
                pltpu.VMEM((8, HEAD, width), jnp.bfloat16),
                pltpu.VMEM((8, HEAD, width), jnp.bfloat16),
                pltpu.VMEM((4, 2 * BLK, HEAD), jnp.bfloat16),
                pltpu.VMEM((4, 2, 5 * BLK, HEAD), jnp.bfloat16),
                pltpu.VMEM((8, 2 * BLK, HEAD), jnp.bfloat16),
                pltpu.VMEM((4, 2 * BLK, HEAD), jnp.bfloat16),
                pltpu.VMEM((4, BLK, HEAD), jnp.bfloat16),
                pltpu.VMEM((5, 8, BLK), jnp.float32),
                pltpu.VMEM((2, BLK, 4 * BLK), jnp.float32),
                pltpu.SemaphoreType.DMA((n_slots,)),
                pltpu.SemaphoreType.DMA((n_slots,)),
                pltpu.SemaphoreType.DMA((16,)),
                pltpu.SemaphoreType.REGULAR,
            ],
            compiler_params=pltpu.CompilerParams(
                collective_id=0, has_side_effects=True, vmem_limit_bytes=56 * 1024 * 1024
            ),
        )(
            inputs.reshape(BLK, width), seg, w_query.reshape(width, -1),
            w_keyval.reshape(rows_dev, -1), w_out.reshape(8, HEAD, width),
        )
        return made.reshape(1, 1, BLK, width)

    placed = (
        P(None, "ctx", None),
        P(None, "ctx"),
        P("phase", None, None),
        P("phase", "ctx", None),
        P("phase", None, None),
    )
    return jax.shard_map(
        local, mesh=mesh, in_specs=placed, out_specs=P("phase", None, "ctx", None), check_vma=False
    )
```

```python
import functools
import math

import jax
import jax.numpy as jnp
from jax import lax
from jax.experimental import pallas as pl
from jax.experimental.pallas import tpu as pltpu
from jax.sharding import PartitionSpec as P

MESH = pl.DeviceIdType.MESH
HEAD = 128
BLK = 128
RING = 4


def kernel(
    phases, chips, x_in, seg_in, wq_in, wkv_in, wo_in, out_ref,
    x_v, acc, wq_v, wkv_v, wo_v, wop_v, q_v, kv_v, bl_v, blo_v, bls_v, seg_v, bias_v, rel_v,
    ssem, rsem, lsem, go_sem,
):
    width = x_v.shape[1]
    rows_dev = wkv_in.shape[0]
    rows_chip = 2 * rows_dev
    ph = lax.axis_index("phase")
    c = lax.axis_index("ctx")
    p = c // 2
    j = c % 2
    y = p // RING
    z = p % RING
    sib = c + 1 - 2 * j

    def at(phase, chip):
        return {"phase": phase, "ctx": chip * 2 + j}

    sibling = {"phase": ph, "ctx": sib}

    def chip_at(dy, dz):
        return ((y + dy + RING) % RING) * RING + (z + dz + RING) % RING

    y_next, y_prev = at(ph, chip_at(1, 0)), at(ph, chip_at(-1, 0))
    z_next, z_prev = at(ph, chip_at(0, 1)), at(ph, chip_at(0, -1))
    next1, next2 = at(ph, jnp.minimum(p + 1, chips - 1)), at(ph, jnp.minimum(p + 2, chips - 1))
    last1, last2 = at(ph, jnp.maximum(p - 1, 0)), at(ph, jnp.maximum(p - 2, 0))
    ph_next, ph_prev = at(jnp.minimum(ph + 1, phases - 1), p), at(jnp.maximum(ph - 1, 0), p)
    ph_over, ph_under = at(jnp.minimum(ph + RING, phases - 1), p), at(jnp.maximum(ph - RING, 0), p)
    has_next1, has_next2 = p + 1 < chips, p + 2 < chips
    has_last1, has_last2 = p >= 1, p >= 2
    is_first, is_last = ph == 0, ph == phases - 1
    has_over, has_under = ph + RING < phases, ph >= RING
    late_helper = ph % RING < RING - 1
    helper = jnp.where(ph % RING > 0, ph - 1, ph + RING - 1)
    helped = jnp.where(late_helper, ph + 1, ph - RING + 1)
    turn_out, turn_in = ph == RING - 1, ph == RING

    barrier = pltpu.get_barrier_semaphore()
    for device in (sibling, y_next, y_prev, z_next, z_prev, at(helper, p), at(helped, p)):
        pl.semaphore_signal(barrier, inc=1, device_id=device, device_id_type=MESH)
    count = jnp.int32(7)
    for device, there in (
        (next1, has_next1), (next2, has_next2), (last1, has_last1), (last2, has_last2),
        (ph_next, ph + 1 < phases), (ph_prev, ph > 0), (ph_over, has_over), (ph_under, has_under),
        (at(helped, jnp.minimum(p + 1, chips - 1)), has_next1), (at(helped, jnp.minimum(p + 2, chips - 1)), has_next2),
        (at(helper, jnp.maximum(p - 1, 0)), has_last1), (at(helper, jnp.maximum(p - 2, 0)), has_last2),
        (at(jnp.minimum(ph + 1, phases - 1), chip_at(0, -1)), turn_out),
        (at(jnp.maximum(ph - 1, 0), chip_at(0, 1)), turn_in),
    ):
        @pl.when(there)
        def _(device=device):
            pl.semaphore_signal(barrier, inc=1, device_id=device, device_id_type=MESH)

        count = count + there.astype(jnp.int32)
    pl.semaphore_wait(barrier, count)

    pending = []
    slots = iter(range(ssem.shape[0]))

    def copy(src, dst, slot, device):
        return pltpu.make_async_remote_copy(
            src_ref=src, dst_ref=dst, send_sem=ssem.at[slot], recv_sem=rsem.at[slot],
            device_id=device, device_id_type=MESH,
        )

    def send(src, dst, slot, device, when=None):
        made = copy(src, dst, slot, device)
        if when is None:
            made.start()
        else:
            pl.when(when)(made.start)
        pending.append((made, when))
        return made

    def recv(dst, slot):
        copy(dst, dst, slot, sibling).wait_recv()

    def run(when, body):
        pl.when(when)(body)

    local = []

    def load(src, dst):
        made = pltpu.make_async_copy(src, dst, lsem.at[len(local)])
        made.start()
        local.append(made)
        return made

    def columns(core, tile):
        start = core * 4 * HEAD + (tile // 2) * 2 * HEAD + (tile % 2) * 8 * HEAD
        return pl.ds(pl.multiple_of(start, 2 * HEAD), 2 * HEAD)

    own_rows = pl.ds(pl.multiple_of(c * rows_dev, rows_dev), rows_dev)
    shard_loads = [load(wkv_in.at[:, columns(j, t)], wkv_v.at[t, own_rows, :]) for t in range(4)]
    seg_load = load(seg_in, seg_v.at[3 + j])
    mine = pl.ds(pl.multiple_of(j * BLK, BLK), BLK)
    theirs = pl.ds(pl.multiple_of((1 - j) * BLK, BLK), BLK)
    wq_loads = [
        load(wq_in.at[:, pl.ds(pl.multiple_of(j * 4 * HEAD + t * 2 * HEAD, 2 * HEAD), 2 * HEAD)], wq_v.at[t])
        for t in range(2)
    ]
    wo_load = load(wo_in, wo_v)

    sib_rows = pl.ds(pl.multiple_of(sib * rows_dev, rows_dev), rows_dev)
    shard_slots = [next(slots) for _ in range(4)]
    seg_slots = [next(slots) for _ in range(3)]

    for t in range(4):
        send(wkv_in.at[:, columns(1 - j, t)], wkv_v.at[t, own_rows, :], shard_slots[t], sibling)
    send(seg_in, seg_v.at[3 + j], seg_slots[0], sibling)

    wop_slots = [next(slots) for _ in range(4)]

    def send_wop(when, devices):
        for k in range(4):
            send(wo_in.at[4 * j + k], wop_v.at[4 * j + k], wop_slots[k], devices[k // 2], when)

    send_wop(is_first, (ph_next, ph_next))
    x_slot = next(slots)
    x_prev_slot = next(slots)
    x_load = pltpu.make_async_copy(x_in, x_v.at[mine], lsem.at[len(local)])
    x_direct = copy(x_in, x_v.at[mine], x_slot, sibling)

    @pl.when(ph < 2)
    def _():
        x_load.start()
        x_direct.start()

    for made in shard_loads:
        made.wait()
    for t in range(4):
        recv(wkv_v.at[t, sib_rows, :], shard_slots[t])

    def slab(chip, first, count_):
        return wkv_v.at[pl.ds(first, count_), pl.ds(pl.multiple_of(chip * rows_chip, rows_chip), rows_chip), :]

    sets = []
    for s in range(2):
        sets.append(dict(
            tile=2 * s,
            prim=(y_next, y_prev) if s == 0 else (z_next, z_prev),
            sec=(z_next, z_prev) if s == 0 else (y_next, y_prev),
            chip=(lambda a, b: chip_at(a, b)) if s == 0 else (lambda a, b: chip_at(b, a)),
            pslot=[next(slots) for _ in range(4)],
            sslot={dp: [next(slots) for _ in range(4)] for dp in (0, -1, 1, 2)},
        ))

    def ring_send(g, ring, slot, dp):
        piece = slab(g["chip"](dp, 0), g["tile"], 2)
        send(piece, piece, slot[0], ring[0])
        send(piece, piece, slot[1], ring[1])

    def ring_forward(g, ring, slot, before, after):
        piece = slab(before, g["tile"], 2)
        recv(piece, slot[0])
        half = slab(before, g["tile"], 1)
        send(half, half, slot[2], ring[0])
        piece = slab(after, g["tile"], 2)
        recv(piece, slot[1])
        half = slab(after, g["tile"] + 1, 1)
        send(half, half, slot[3], ring[1])

    def ring_end(g, slot, far):
        recv(slab(far, g["tile"], 1), slot[2])
        recv(slab(far, g["tile"] + 1, 1), slot[3])

    pl.when(has_under)(lambda: pl.semaphore_wait(go_sem, 1))
    for g in sets:
        ring_send(g, g["prim"], g["pslot"], 0)
        ring_send(g, g["sec"], g["sslot"][0], 0)
    for g in sets:
        ring_forward(g, g["prim"], g["pslot"], g["chip"](-1, 0), g["chip"](1, 0))
        ring_send(g, g["sec"], g["sslot"][-1], -1)
        ring_send(g, g["sec"], g["sslot"][1], 1)
    for g in sets:
        ring_forward(g, g["sec"], g["sslot"][0], g["chip"](0, -1), g["chip"](0, 1))
    for g in sets:
        ring_end(g, g["pslot"], g["chip"](2, 0))
        ring_send(g, g["sec"], g["sslot"][2], 2)
    for dp in (-1, 1, 2):
        for g in sets:
            ring_forward(g, g["sec"], g["sslot"][dp], g["chip"](dp, -1), g["chip"](dp, 1))

    seg_load.wait()
    recv(seg_v.at[4 - j], seg_slots[0])
    send(seg_v.at[pl.ds(3, 2)], seg_v.at[pl.ds(1, 2)], seg_slots[1], next1, has_next1)
    send(seg_v.at[4], seg_v.at[0], seg_slots[2], next2, has_next2)

    @pl.when(jnp.logical_not(has_last1))
    def _():
        seg_v[1:3] = jnp.full((2,) + seg_v.shape[1:], -1.0, jnp.float32)
        kv_v[:, :, BLK:3 * BLK, :] = jnp.zeros((4, 2, 2 * BLK, HEAD), jnp.bfloat16)

    @pl.when(jnp.logical_not(has_last2))
    def _():
        seg_v[0] = jnp.full(seg_v.shape[1:], -1.0, jnp.float32)
        kv_v[:, :, 0:BLK, :] = jnp.zeros((4, 2, BLK, HEAD), jnp.bfloat16)

    run(has_last1, lambda: recv(seg_v.at[pl.ds(1, 2)], seg_slots[1]))
    run(has_last2, lambda: recv(seg_v.at[0], seg_slots[2]))

    row_id = lax.broadcasted_iota(jnp.int32, (BLK, BLK), 0)
    col_id = lax.broadcasted_iota(jnp.int32, (BLK, BLK), 1)
    causal = col_id <= row_id
    for i in range(2):
        asking = jnp.transpose(jnp.broadcast_to(seg_v[3 + i, 0:1, :], (BLK, BLK)))
        for b in range(4):
            asked = jnp.broadcast_to(seg_v[i + b, 0:1, :], (BLK, BLK))
            ok = asking == asked
            if b == 3:
                ok = ok & causal
            bias_v[i, :, b * BLK:(b + 1) * BLK] = jnp.where(ok, 0.0, -1e30).astype(jnp.float32)

    for dp in (0, -1, 1, 2):
        for g in sets:
            ring_end(g, g["sslot"][dp], g["chip"](dp, 2))
    for made in wq_loads:
        made.wait()
    wo_load.wait()

    halo_slots = [[next(slots) for _ in range(4)] for _ in range(4)]
    rel_slots = [next(slots) for _ in range(4)]
    rel_copies = []
    for h in range(4):
        rel_copies.append((copy(rel_v.at[h], kv_v.at[h, 1, pl.ds(BLK, 2 * BLK), :], halo_slots[h][2],
                                at(helped, jnp.minimum(p + 1, chips - 1))), has_next1))
        rel_copies.append((copy(rel_v.at[h, pl.ds(BLK, BLK), :], kv_v.at[h, 1, pl.ds(0, BLK), :], halo_slots[h][3],
                                at(helped, jnp.minimum(p + 2, chips - 1))), has_next2))

    def help_halo():
        @pl.when(has_next1)
        def _():
            for h in range(4):
                recv(rel_v.at[h], rel_slots[h])
                rel_copies[2 * h][0].start()
                pl.when(has_next2)(rel_copies[2 * h + 1][0].start)

        @pl.when(has_over)
        def _():
            pl.semaphore_signal(go_sem, inc=1, device_id=ph_over, device_id_type=MESH)

    pl.when(jnp.logical_not(late_helper))(help_halo)
    send_wop((ph > 0) & (ph + 1 < phases) & jnp.logical_not(turn_out), (ph_next, ph_next))
    send_wop(turn_out, (ph_next, at(jnp.minimum(ph + 1, phases - 1), chip_at(0, -1))))

    wop_relay = [next(slots) for _ in range(4)]
    relays = []
    for k in range(4):
        relays.append(copy(wop_v.at[4 * j + k], wop_v.at[4 * j + k], wop_relay[k], sibling))
    x_relay = copy(x_v.at[mine], x_v.at[mine], x_slot, sibling)

    @pl.when(ph > 0)
    def _():
        for k in range(4):
            recv(wop_v.at[4 * j + k], wop_slots[k])
            relays[k].start()

    @pl.when(ph < 2)
    def _():
        x_load.wait()
        x_direct.wait_send()

    @pl.when(ph >= 2)
    def _():
        recv(x_v.at[mine], x_prev_slot)
        x_relay.start()
        x_relay.wait_send()

    recv(x_v.at[theirs], x_slot)

    bl_slots = [next(slots) for _ in range(4)]
    bl_relay_slots = [next(slots) for _ in range(4)]
    bl_relays = [copy(bl_v.at[4 * j + h], bl_v.at[4 * j + h], bl_relay_slots[h], sibling) for h in range(4)]
    step = 512 if width % 512 == 0 else width

    @pl.when(ph > 0)
    def _():
        for k in range(4):
            recv(wop_v.at[4 * (1 - j) + k], wop_relay[k])
        for h in range(4):
            recv(bl_v.at[4 * j + h], bl_slots[h])
            bl_relays[h].start()
            recv(bl_v.at[4 * (1 - j) + h], bl_relay_slots[h])
            lhs = jnp.concatenate([bl_v[h], bl_v[4 + h]], axis=1)
            for n in range(0, width, step):
                rhs = jnp.concatenate([wop_v[h, :, n:n + step], wop_v[4 + h, :, n:n + step]], axis=0)
                part = jnp.dot(lhs, rhs, preferred_element_type=jnp.float32)
                if h == 0:
                    acc[:, n:n + step] = part
                elif h < 3:
                    acc[:, n:n + step] += part
                else:
                    total = x_v[:, n:n + step].astype(jnp.float32) + (acc[:, n:n + step] + part)
                    x_v[:, n:n + step] = total.astype(jnp.bfloat16)

    send(x_v.at[mine], x_v.at[mine], x_prev_slot, ph_next, (ph > 0) & (ph + 1 < phases))

    square = jnp.zeros((2 * BLK, 1), jnp.float32)
    for n in range(0, width, step):
        part = x_v[:, n:n + step].astype(jnp.float32)
        square = square + jnp.sum(part * part, axis=1, keepdims=True)
    scale_rows = lax.rsqrt(square * (1.0 / width) + 1e-05)

    stream = x_v[...]

    def project(weights):
        return (jnp.dot(stream, weights, preferred_element_type=jnp.float32) * scale_rows).astype(jnp.bfloat16)

    for t in range(2):
        for kind in range(2):
            made = project(wkv_v[2 * t + kind])
            kv_v[2 * t, kind, 3 * BLK:5 * BLK, :] = made[:, :HEAD]
            kv_v[2 * t + 1, kind, 3 * BLK:5 * BLK, :] = made[:, HEAD:]
        for h in (2 * t, 2 * t + 1):
            send(kv_v.at[h, 1, pl.ds(3 * BLK, 2 * BLK), :], rel_v.at[h], rel_slots[h], at(helper, p), has_next1)
            send(kv_v.at[h, 0, pl.ds(3 * BLK, 2 * BLK), :], kv_v.at[h, 0, pl.ds(BLK, 2 * BLK), :],
                 halo_slots[h][0], next1, has_next1)
            send(kv_v.at[h, 0, pl.ds(4 * BLK, BLK), :], kv_v.at[h, 0, pl.ds(0, BLK), :],
                 halo_slots[h][1], next2, has_next2)
    for t in range(2):
        made = project(wq_v[t])
        q_v[2 * t] = made[:, :HEAD]
        q_v[2 * t + 1] = made[:, HEAD:]

    bls_slots = [next(slots) for _ in range(4)]
    for h in range(4):
        for kind in range(2):
            run(has_last1, lambda h=h, kind=kind: recv(kv_v.at[h, kind, pl.ds(BLK, 2 * BLK), :], halo_slots[h][2 * kind]))
            run(has_last2, lambda h=h, kind=kind: recv(kv_v.at[h, kind, pl.ds(0, BLK), :], halo_slots[h][2 * kind + 1]))
        for i in range(2):
            keys = kv_v[h, 0, i * BLK:(i + 4) * BLK, :]
            values = kv_v[h, 1, i * BLK:(i + 4) * BLK, :]
            scores = lax.dot_general(
                q_v[h, i * BLK:(i + 1) * BLK, :], keys, (((1,), (1,)), ((), ())),
                preferred_element_type=jnp.float32,
            )
            scores = scores * (1.0 / math.sqrt(HEAD)) + bias_v[i]
            top = jnp.max(scores, axis=1, keepdims=True)
            weights = jnp.exp(scores - top)
            total = jnp.sum(weights, axis=1, keepdims=True)
            mixed = jnp.dot(weights.astype(jnp.bfloat16), values, preferred_element_type=jnp.float32)
            blo_v[h, i * BLK:(i + 1) * BLK, :] = (mixed / total).astype(jnp.bfloat16)
        send(blo_v.at[h], bl_v.at[4 * j + h], bl_slots[h], ph_next, ph + 1 < phases)
        send(blo_v.at[h, theirs, :], bls_v.at[h], bls_slots[h], sibling)

    for h in range(4):
        recv(bls_v.at[h], bls_slots[h])
    own = jnp.concatenate([blo_v[h, mine, :] for h in range(4)], axis=1)
    other = jnp.concatenate([bls_v[h] for h in range(4)], axis=1)
    for n in range(0, width, step):
        first = wo_v[pl.ds(4 * j, 4), :, n:n + step].reshape(4 * HEAD, step)
        second = wo_v[pl.ds(4 * (1 - j), 4), :, n:n + step].reshape(4 * HEAD, step)
        update = jnp.dot(own, first, preferred_element_type=jnp.float32)
        update = update + jnp.dot(other, second, preferred_element_type=jnp.float32)
        out_ref[:, n:n + step] = (x_v[mine, n:n + step].astype(jnp.float32) + update).astype(jnp.bfloat16)

    pl.when(late_helper)(help_halo)
    for made, when in pending + rel_copies:
        if when is None:
            made.wait_send()
        else:
            pl.when(when)(made.wait_send)

    @pl.when(ph > 0)
    def _():
        for made in relays + bl_relays:
            made.wait_send()


def solution(mesh):
    phases, devices = mesh.shape["phase"], mesh.shape["ctx"]
    chips = devices // 2

    def local(inputs, segment_ids, w_query, w_keyval, w_out):
        width = inputs.shape[2]
        rows_dev = w_keyval.shape[1]
        seg = jnp.broadcast_to(segment_ids.astype(jnp.float32), (8, BLK))
        any_space = pl.BlockSpec(memory_space=pl.ANY)
        n_slots = 128
        made = pl.pallas_call(
            functools.partial(kernel, phases, chips),
            out_shape=jax.ShapeDtypeStruct((BLK, width), jnp.bfloat16),
            in_specs=[any_space] * 5,
            out_specs=pl.BlockSpec(memory_space=pltpu.VMEM),
            scratch_shapes=[
                pltpu.VMEM((2 * BLK, width), jnp.bfloat16),
                pltpu.VMEM((2 * BLK, width), jnp.float32),
                pltpu.VMEM((2, width, 2 * HEAD), jnp.bfloat16),
                pltpu.VMEM((4, width, 2 * HEAD), jnp.bfloat16),
                pltpu.VMEM((8, HEAD, width), jnp.bfloat16),
                pltpu.VMEM((8, HEAD, width), jnp.bfloat16),
                pltpu.VMEM((4, 2 * BLK, HEAD), jnp.bfloat16),
                pltpu.VMEM((4, 2, 5 * BLK, HEAD), jnp.bfloat16),
                pltpu.VMEM((8, 2 * BLK, HEAD), jnp.bfloat16),
                pltpu.VMEM((4, 2 * BLK, HEAD), jnp.bfloat16),
                pltpu.VMEM((4, BLK, HEAD), jnp.bfloat16),
                pltpu.VMEM((5, 8, BLK), jnp.float32),
                pltpu.VMEM((2, BLK, 4 * BLK), jnp.float32),
                pltpu.VMEM((4, 2 * BLK, HEAD), jnp.bfloat16),
                pltpu.SemaphoreType.DMA((n_slots,)),
                pltpu.SemaphoreType.DMA((n_slots,)),
                pltpu.SemaphoreType.DMA((16,)),
                pltpu.SemaphoreType.REGULAR,
            ],
            compiler_params=pltpu.CompilerParams(
                collective_id=0, has_side_effects=True, vmem_limit_bytes=56 * 1024 * 1024
            ),
        )(
            inputs.reshape(BLK, width), seg, w_query.reshape(width, -1),
            w_keyval.reshape(rows_dev, -1), w_out.reshape(8, HEAD, width),
        )
        return made.reshape(1, 1, BLK, width)

    placed = (
        P(None, "ctx", None),
        P(None, "ctx"),
        P("phase", None, None),
        P("phase", "ctx", None),
        P("phase", None, None),
    )
    return jax.shard_map(
        local, mesh=mesh, in_specs=placed, out_specs=P("phase", None, "ctx", None), check_vma=False
    )
```

```python
import functools
import math

import jax
import jax.numpy as jnp
from jax import lax
from jax.experimental import pallas as pl
from jax.experimental.pallas import tpu as pltpu
from jax.sharding import PartitionSpec as P

MESH = pl.DeviceIdType.MESH
HEAD = 128
BLK = 128
RING = 4


def kernel(
    phases, chips, x_in, seg_in, wq_in, wkv_in, wo_in, out_ref,
    x_v, acc, wq_v, wkv_v, wo_v, wop_v, q_v, kv_v, bl_v, blo_v, bls_v, seg_v, bias_v, rel_v, res_v, sq_v,
    ssem, rsem, lsem, go_sem,
):
    width = x_v.shape[1]
    rows_dev = wkv_in.shape[0]
    rows_chip = 2 * rows_dev
    ph = lax.axis_index("phase")
    c = lax.axis_index("ctx")
    p = c // 2
    j = c % 2
    y = p // RING
    z = p % RING
    sib = c + 1 - 2 * j

    def at(phase, chip):
        return {"phase": phase, "ctx": chip * 2 + j}

    sibling = {"phase": ph, "ctx": sib}

    def chip_at(dy, dz):
        return ((y + dy + RING) % RING) * RING + (z + dz + RING) % RING

    y_next, y_prev = at(ph, chip_at(1, 0)), at(ph, chip_at(-1, 0))
    z_next, z_prev = at(ph, chip_at(0, 1)), at(ph, chip_at(0, -1))
    next1, next2 = at(ph, jnp.minimum(p + 1, chips - 1)), at(ph, jnp.minimum(p + 2, chips - 1))
    last1, last2 = at(ph, jnp.maximum(p - 1, 0)), at(ph, jnp.maximum(p - 2, 0))
    ph_next, ph_prev = at(jnp.minimum(ph + 1, phases - 1), p), at(jnp.maximum(ph - 1, 0), p)
    goer = jnp.where(ph < RING + 2, jnp.maximum(ph - RING + 1, 0), ph - RING)
    has_next1, has_next2 = p + 1 < chips, p + 2 < chips
    has_last1, has_last2 = p >= 1, p >= 2
    is_first, is_last = ph == 0, ph == phases - 1
    has_under = ph >= RING
    goes_late, goes_early = (ph == 1) | (ph == 2), (ph == 2) | (ph == 3)
    early_help, late_help = ph == 2 * RING - 1, (ph % RING < RING - 1)
    has_helper, has_helped = ph > 0, ph != RING - 1
    helper = jnp.where(ph == RING, 2 * RING - 1, jnp.maximum(ph - 1, 0))
    helped = jnp.where(early_help, RING, jnp.minimum(ph + 1, phases - 1))
    res_out, res_in = (ph >= 1) & (ph + 1 < phases), ph >= 2
    early_pass, late_pass = ph >= RING + 2, ph < RING
    has_pass = early_pass | late_pass
    up = jnp.where(early_pass, 1, 0)

    def passer(target):
        low = target < RING
        chip = jnp.where(low, chip_at(0, -1), p)
        return at(jnp.where(low, target + RING, target - RING), chip)

    pass_chip = chip_at(0, up)
    pass_phase = jnp.where(early_pass, jnp.maximum(ph - RING, 0), jnp.minimum(ph + RING, phases - 1))
    turn_out, turn_in = ph == RING - 1, ph == RING

    barrier = pltpu.get_barrier_semaphore()
    for device in (sibling, y_next, y_prev, z_next, z_prev):
        pl.semaphore_signal(barrier, inc=1, device_id=device, device_id_type=MESH)
    count = jnp.int32(5)
    for device, there in (
        (next1, has_next1), (next2, has_next2), (last1, has_last1), (last2, has_last2),
        (ph_next, ph + 1 < phases), (ph_prev, ph > 0), (at(goer, p), has_under), (at(ph + RING - 1, p), goes_late), (at(jnp.minimum(ph + RING, phases - 1), p), goes_early),
        (at(helper, p), has_helper), (at(helped, p), has_helped),
        (at(helped, jnp.minimum(p + 1, chips - 1)), has_helped & has_next1),
        (at(helped, jnp.minimum(p + 2, chips - 1)), has_helped & has_next2),
        (at(helper, jnp.maximum(p - 1, 0)), has_helper & has_last1),
        (at(helper, jnp.maximum(p - 2, 0)), has_helper & has_last2),
        (passer(jnp.minimum(ph + 1, phases - 1)), res_out), (passer(ph), res_in),
        (at(jnp.maximum(pass_phase - 1, 0), pass_chip), has_pass), (at(pass_phase, pass_chip), has_pass),
        (at(jnp.minimum(ph + 1, phases - 1), chip_at(0, -1)), turn_out),
        (at(jnp.maximum(ph - 1, 0), chip_at(0, 1)), turn_in),
    ):
        @pl.when(there)
        def _(device=device):
            pl.semaphore_signal(barrier, inc=1, device_id=device, device_id_type=MESH)

        count = count + there.astype(jnp.int32)
    pl.semaphore_wait(barrier, count)

    pending = []
    slots = iter(range(ssem.shape[0]))

    def copy(src, dst, slot, device):
        return pltpu.make_async_remote_copy(
            src_ref=src, dst_ref=dst, send_sem=ssem.at[slot], recv_sem=rsem.at[slot],
            device_id=device, device_id_type=MESH,
        )

    def send(src, dst, slot, device, when=None):
        made = copy(src, dst, slot, device)
        if when is None:
            made.start()
        else:
            pl.when(when)(made.start)
        pending.append((made, when))
        return made

    def recv(dst, slot):
        copy(dst, dst, slot, sibling).wait_recv()

    def run(when, body):
        pl.when(when)(body)

    local = []

    def load(src, dst):
        made = pltpu.make_async_copy(src, dst, lsem.at[len(local)])
        made.start()
        local.append(made)
        return made

    def columns(core, tile):
        start = core * 4 * HEAD + (tile // 2) * 2 * HEAD + (tile % 2) * 8 * HEAD
        return pl.ds(pl.multiple_of(start, 2 * HEAD), 2 * HEAD)

    own_rows = pl.ds(pl.multiple_of(c * rows_dev, rows_dev), rows_dev)
    shard_loads = [load(wkv_in.at[:, columns(j, t)], wkv_v.at[t, own_rows, :]) for t in range(4)]
    seg_load = load(seg_in, seg_v.at[3 + j])
    mine = pl.ds(pl.multiple_of(j * BLK, BLK), BLK)
    theirs = pl.ds(pl.multiple_of((1 - j) * BLK, BLK), BLK)
    wq_loads = [
        load(wq_in.at[:, pl.ds(pl.multiple_of(j * 4 * HEAD + t * 2 * HEAD, 2 * HEAD), 2 * HEAD)], wq_v.at[t])
        for t in range(2)
    ]
    wo_load = load(wo_in, wo_v)

    sib_rows = pl.ds(pl.multiple_of(sib * rows_dev, rows_dev), rows_dev)
    shard_slots = [next(slots) for _ in range(4)]
    seg_slots = [next(slots) for _ in range(3)]

    for t in range(4):
        send(wkv_in.at[:, columns(1 - j, t)], wkv_v.at[t, own_rows, :], shard_slots[t], sibling)
    send(seg_in, seg_v.at[3 + j], seg_slots[0], sibling)

    wop_slots = [next(slots) for _ in range(4)]

    def send_wop(when, devices):
        for k in range(4):
            send(wo_in.at[4 * j + k], wop_v.at[4 * j + k], wop_slots[k], devices[k // 2], when)

    send_wop((ph + 1 < phases) & jnp.logical_not(turn_out), (ph_next, ph_next))
    x_slot = next(slots)
    x_prev_slots = [next(slots) for _ in range(4)]
    x_relay_slots = [next(slots) for _ in range(4)]
    res_slots = [next(slots) for _ in range(4)]
    x_load = pltpu.make_async_copy(x_in, x_v.at[mine], lsem.at[len(local)])
    x_direct = copy(x_in, x_v.at[mine], x_slot, sibling)

    @pl.when(ph < 2)
    def _():
        x_load.start()
        x_direct.start()

    for made in shard_loads:
        made.wait()
    for t in range(4):
        recv(wkv_v.at[t, sib_rows, :], shard_slots[t])

    def slab(chip, first, count_):
        return wkv_v.at[pl.ds(first, count_), pl.ds(pl.multiple_of(chip * rows_chip, rows_chip), rows_chip), :]

    sets = []
    for s in range(2):
        sets.append(dict(
            tile=2 * s,
            prim=(y_next, y_prev) if s == 0 else (z_next, z_prev),
            sec=(z_next, z_prev) if s == 0 else (y_next, y_prev),
            chip=(lambda a, b: chip_at(a, b)) if s == 0 else (lambda a, b: chip_at(b, a)),
            pslot=[next(slots) for _ in range(4)],
            sslot={dp: [next(slots) for _ in range(4)] for dp in (0, -1, 1, 2)},
        ))

    def ring_send(g, ring, slot, dp):
        piece = slab(g["chip"](dp, 0), g["tile"], 2)
        send(piece, piece, slot[0], ring[0])
        send(piece, piece, slot[1], ring[1])

    def ring_forward(g, ring, slot, before, after):
        piece = slab(before, g["tile"], 2)
        recv(piece, slot[0])
        half = slab(before, g["tile"], 1)
        send(half, half, slot[2], ring[0])
        piece = slab(after, g["tile"], 2)
        recv(piece, slot[1])
        half = slab(after, g["tile"] + 1, 1)
        send(half, half, slot[3], ring[1])

    def ring_end(g, slot, far):
        recv(slab(far, g["tile"], 1), slot[2])
        recv(slab(far, g["tile"] + 1, 1), slot[3])

    seg_load.wait()
    recv(seg_v.at[4 - j], seg_slots[0])
    send(seg_v.at[pl.ds(3, 2)], seg_v.at[pl.ds(1, 2)], seg_slots[1], next1, has_next1)
    send(seg_v.at[4], seg_v.at[0], seg_slots[2], next2, has_next2)

    @pl.when(jnp.logical_not(has_last1))
    def _():
        seg_v[1:3] = jnp.full((2,) + seg_v.shape[1:], -1.0, jnp.float32)
        kv_v[:, :, BLK:3 * BLK, :] = jnp.zeros((4, 2, 2 * BLK, HEAD), jnp.bfloat16)

    @pl.when(jnp.logical_not(has_last2))
    def _():
        seg_v[0] = jnp.full(seg_v.shape[1:], -1.0, jnp.float32)
        kv_v[:, :, 0:BLK, :] = jnp.zeros((4, 2, BLK, HEAD), jnp.bfloat16)

    pl.when(has_under)(lambda: pl.semaphore_wait(go_sem, 1))
    for g in sets:
        ring_send(g, g["prim"], g["pslot"], 0)
        ring_send(g, g["sec"], g["sslot"][0], 0)
    run(has_last1, lambda: recv(seg_v.at[pl.ds(1, 2)], seg_slots[1]))
    run(has_last2, lambda: recv(seg_v.at[0], seg_slots[2]))

    row_id = lax.broadcasted_iota(jnp.int32, (BLK, BLK), 0)
    col_id = lax.broadcasted_iota(jnp.int32, (BLK, BLK), 1)
    causal = col_id <= row_id
    for i in range(2):
        asking = jnp.transpose(jnp.broadcast_to(seg_v[3 + i, 0:1, :], (BLK, BLK)))
        for b in range(4):
            asked = jnp.broadcast_to(seg_v[i + b, 0:1, :], (BLK, BLK))
            ok = asking == asked
            if b == 3:
                ok = ok & causal
            bias_v[i, :, b * BLK:(b + 1) * BLK] = jnp.where(ok, 0.0, -1e30).astype(jnp.float32)

    for g in sets:
        ring_forward(g, g["prim"], g["pslot"], g["chip"](-1, 0), g["chip"](1, 0))
        ring_send(g, g["sec"], g["sslot"][-1], -1)
        ring_send(g, g["sec"], g["sslot"][1], 1)
    for g in sets:
        ring_forward(g, g["sec"], g["sslot"][0], g["chip"](0, -1), g["chip"](0, 1))
    for g in sets:
        ring_end(g, g["pslot"], g["chip"](2, 0))
        ring_send(g, g["sec"], g["sslot"][2], 2)
    for dp in (-1, 1, 2):
        for g in sets:
            ring_forward(g, g["sec"], g["sslot"][dp], g["chip"](dp, -1), g["chip"](dp, 1))

    for dp in (0, -1, 1, 2):
        for g in sets:
            ring_end(g, g["sslot"][dp], g["chip"](dp, 2))
    for made in wq_loads:
        made.wait()
    wo_load.wait()

    halo_slots = [[next(slots) for _ in range(4)] for _ in range(4)]
    rel_slots = [next(slots) for _ in range(4)]
    rel_copies = []
    for h in range(4):
        rel_copies.append((copy(rel_v.at[h], kv_v.at[h, 1, pl.ds(BLK, 2 * BLK), :], halo_slots[h][2],
                                at(helped, jnp.minimum(p + 1, chips - 1))), has_helped & has_next1))
        rel_copies.append((copy(rel_v.at[h, pl.ds(BLK, BLK), :], kv_v.at[h, 1, pl.ds(0, BLK), :], halo_slots[h][3],
                                at(helped, jnp.minimum(p + 2, chips - 1))), has_helped & has_next2))

    def help_halo():
        @pl.when(has_next1)
        def _():
            for h in range(4):
                recv(rel_v.at[h], rel_slots[h])
                rel_copies[2 * h][0].start()
                pl.when(has_next2)(rel_copies[2 * h + 1][0].start)

    def go(phase):
        pl.semaphore_signal(go_sem, inc=1, device_id=at(jnp.minimum(phase, phases - 1), p), device_id_type=MESH)

    piece = BLK // 4

    def mine_at(k):
        return x_v.at[pl.ds(pl.multiple_of(j * BLK + k * piece, piece), piece), :]

    def theirs_at(k):
        return x_v.at[pl.ds(pl.multiple_of((1 - j) * BLK + k * piece, piece), piece), :]

    res_copies = [copy(res_v.at[k], mine_at(k), x_prev_slots[k], at(pass_phase, pass_chip)) for k in range(4)]
    pass_all = ph == 0

    def pass_residual():
        @pl.when(pass_all)
        def _():
            for k in range(2):
                recv(res_v.at[k], res_slots[k])
                res_copies[k].start()

        for k in range(2, 4):
            recv(res_v.at[k], res_slots[k])
            res_copies[k].start()

    pl.when(goes_early)(lambda: go(ph + RING))
    pl.when(early_pass)(pass_residual)
    pl.when(early_help)(help_halo)
    send_wop(turn_out, (ph_next, at(jnp.minimum(ph + 1, phases - 1), chip_at(0, -1))))

    wop_relay = [next(slots) for _ in range(4)]
    relays = []
    for k in range(4):
        relays.append(copy(wop_v.at[4 * j + k], wop_v.at[4 * j + k], wop_relay[k], sibling))
    x_relays = [copy(mine_at(k), mine_at(k), x_relay_slots[k], sibling) for k in range(4)]

    @pl.when(ph > 0)
    def _():
        for k in range(4):
            recv(wop_v.at[4 * j + k], wop_slots[k])
            relays[k].start()

    @pl.when(ph < 2)
    def _():
        x_load.wait()
        x_direct.wait_send()
        recv(x_v.at[theirs], x_slot)

    bl_slots = [next(slots) for _ in range(4)]
    bl_relay_slots = [next(slots) for _ in range(4)]
    bl_relays = [copy(bl_v.at[4 * j + h], bl_v.at[4 * j + h], bl_relay_slots[h], sibling) for h in range(4)]
    step = 512 if width % 512 == 0 else width

    def add_squares(n, rounded):
        wide = rounded.astype(jnp.float32)
        wide = wide * wide
        lanes = wide[:, :HEAD]
        for m in range(HEAD, step, HEAD):
            lanes = lanes + wide[:, m:m + HEAD]
        sq_v[...] = lanes if n == 0 else sq_v[...] + lanes


    @pl.when(ph > 0)
    def _():
        for k in range(4):
            recv(wop_v.at[4 * (1 - j) + k], wop_relay[k])
        mine_head, their_head = 4 * j, 4 * (1 - j)
        for h in range(5):
            if h < 4:
                recv(bl_v.at[mine_head + h], bl_slots[h])
                bl_relays[h].start()
            if h == 2:
                @pl.when(ph >= 2)
                def _():
                    for k in range(4):
                        recv(mine_at(k), x_prev_slots[k])
                        x_relays[k].start()

            if h == 4:
                @pl.when(ph >= 2)
                def _():
                    for k in range(4):
                        recv(theirs_at(k), x_relay_slots[k])
                    for k in range(4):
                        x_relays[k].wait_send()

            if h > 0:
                recv(bl_v.at[their_head + h - 1], bl_relay_slots[h - 1])
            heads = ([mine_head + h] if h < 4 else []) + ([their_head + h - 1] if h > 0 else [])
            lhs = jnp.concatenate([bl_v[head] for head in heads], axis=1)
            for n in range(0, width, step):
                rhs = jnp.concatenate([wop_v[head, :, n:n + step] for head in heads], axis=0)
                part = jnp.dot(lhs, rhs, preferred_element_type=jnp.float32)
                if h == 0:
                    acc[:, n:n + step] = part
                elif h < 4:
                    acc[:, n:n + step] += part
                else:
                    total = x_v[:, n:n + step].astype(jnp.float32) + (acc[:, n:n + step] + part)
                    total = total.astype(jnp.bfloat16)
                    x_v[:, n:n + step] = total
                    add_squares(n, total)

    @pl.when(is_first)
    def _():
        for n in range(0, width, step):
            add_squares(n, x_v[:, n:n + step])

    square = jnp.sum(sq_v[...], axis=1, keepdims=True)
    scale_rows = lax.rsqrt(square * (1.0 / width) + 1e-05)

    stream = x_v[...]

    def project(weights):
        return (jnp.dot(stream, weights, preferred_element_type=jnp.float32) * scale_rows).astype(jnp.bfloat16)

    for t in range(2):
        for kind in range(2):
            made = project(wkv_v[2 * t + kind])
            kv_v[2 * t, kind, 3 * BLK:5 * BLK, :] = made[:, :HEAD]
            kv_v[2 * t + 1, kind, 3 * BLK:5 * BLK, :] = made[:, HEAD:]
        for h in (2 * t, 2 * t + 1):
            send(kv_v.at[h, 1, pl.ds(3 * BLK, 2 * BLK), :], rel_v.at[h], rel_slots[h], at(helper, p), has_helper & has_next1)
            send(kv_v.at[h, 1, pl.ds(3 * BLK, 2 * BLK), :], kv_v.at[h, 1, pl.ds(BLK, 2 * BLK), :],
                 halo_slots[h][2], next1, is_first & has_next1)
            send(kv_v.at[h, 1, pl.ds(4 * BLK, BLK), :], kv_v.at[h, 1, pl.ds(0, BLK), :],
                 halo_slots[h][3], next2, is_first & has_next2)
            send(kv_v.at[h, 0, pl.ds(3 * BLK, 2 * BLK), :], kv_v.at[h, 0, pl.ds(BLK, 2 * BLK), :],
                 halo_slots[h][0], next1, has_next1)
            send(kv_v.at[h, 0, pl.ds(4 * BLK, BLK), :], kv_v.at[h, 0, pl.ds(0, BLK), :],
                 halo_slots[h][1], next2, has_next2)
    for t in range(2):
        made = project(wq_v[t])
        q_v[2 * t] = made[:, :HEAD]
        q_v[2 * t + 1] = made[:, HEAD:]

    for k in range(4):
        if k < 2:
            direct, around = res_out & jnp.logical_not(turn_out), turn_out
            send(mine_at(k), mine_at(k), x_prev_slots[k], ph_next, direct)
        else:
            around = res_out
        send(mine_at(k), res_v.at[k], res_slots[k], passer(jnp.minimum(ph + 1, phases - 1)), around)

    bls_slots = [next(slots) for _ in range(4)]
    for h in range(4):
        for kind in range(2):
            run(has_last1, lambda h=h, kind=kind: recv(kv_v.at[h, kind, pl.ds(BLK, 2 * BLK), :], halo_slots[h][2 * kind]))
            run(has_last2, lambda h=h, kind=kind: recv(kv_v.at[h, kind, pl.ds(0, BLK), :], halo_slots[h][2 * kind + 1]))
        for i in range(2):
            keys = kv_v[h, 0, i * BLK:(i + 4) * BLK, :]
            values = kv_v[h, 1, i * BLK:(i + 4) * BLK, :]
            scores = lax.dot_general(
                q_v[h, i * BLK:(i + 1) * BLK, :], keys, (((1,), (1,)), ((), ())),
                preferred_element_type=jnp.float32,
            )
            scores = scores * (1.0 / math.sqrt(HEAD)) + bias_v[i]
            top = jnp.max(scores, axis=1, keepdims=True)
            weights = jnp.exp(scores - top)
            total = jnp.sum(weights, axis=1, keepdims=True)
            mixed = jnp.dot(weights.astype(jnp.bfloat16), values, preferred_element_type=jnp.float32)
            blo_v[h, i * BLK:(i + 1) * BLK, :] = (mixed / total).astype(jnp.bfloat16)
        send(blo_v.at[h], bl_v.at[4 * j + h], bl_slots[h], ph_next, ph + 1 < phases)
        send(blo_v.at[h, theirs, :], bls_v.at[h], bls_slots[h], sibling)

    pl.when(goes_late)(lambda: go(ph + RING - 1))

    for h in range(4):
        recv(bls_v.at[h], bls_slots[h])
    own = jnp.concatenate([blo_v[h, mine, :] for h in range(4)], axis=1)
    other = jnp.concatenate([bls_v[h] for h in range(4)], axis=1)
    for n in range(0, width, step):
        first = wo_v[pl.ds(4 * j, 4), :, n:n + step].reshape(4 * HEAD, step)
        second = wo_v[pl.ds(4 * (1 - j), 4), :, n:n + step].reshape(4 * HEAD, step)
        update = jnp.dot(own, first, preferred_element_type=jnp.float32)
        update = update + jnp.dot(other, second, preferred_element_type=jnp.float32)
        out_ref[:, n:n + step] = (x_v[mine, n:n + step].astype(jnp.float32) + update).astype(jnp.bfloat16)

    pl.when(late_help)(help_halo)
    pl.when(late_pass)(pass_residual)
    for made, when in pending + rel_copies + [(made, has_pass if k > 1 else pass_all) for k, made in enumerate(res_copies)]:
        if when is None:
            made.wait_send()
        else:
            pl.when(when)(made.wait_send)

    @pl.when(ph > 0)
    def _():
        for made in relays + bl_relays:
            made.wait_send()


def solution(mesh):
    phases, devices = mesh.shape["phase"], mesh.shape["ctx"]
    chips = devices // 2

    def local(inputs, segment_ids, w_query, w_keyval, w_out):
        width = inputs.shape[2]
        rows_dev = w_keyval.shape[1]
        seg = jnp.broadcast_to(segment_ids.astype(jnp.float32), (8, BLK))
        any_space = pl.BlockSpec(memory_space=pl.ANY)
        n_slots = 128
        made = pl.pallas_call(
            functools.partial(kernel, phases, chips),
            out_shape=jax.ShapeDtypeStruct((BLK, width), jnp.bfloat16),
            in_specs=[any_space] * 5,
            out_specs=pl.BlockSpec(memory_space=pltpu.VMEM),
            scratch_shapes=[
                pltpu.VMEM((2 * BLK, width), jnp.bfloat16),
                pltpu.VMEM((2 * BLK, width), jnp.float32),
                pltpu.VMEM((2, width, 2 * HEAD), jnp.bfloat16),
                pltpu.VMEM((4, width, 2 * HEAD), jnp.bfloat16),
                pltpu.VMEM((8, HEAD, width), jnp.bfloat16),
                pltpu.VMEM((8, HEAD, width), jnp.bfloat16),
                pltpu.VMEM((4, 2 * BLK, HEAD), jnp.bfloat16),
                pltpu.VMEM((4, 2, 5 * BLK, HEAD), jnp.bfloat16),
                pltpu.VMEM((8, 2 * BLK, HEAD), jnp.bfloat16),
                pltpu.VMEM((4, 2 * BLK, HEAD), jnp.bfloat16),
                pltpu.VMEM((4, BLK, HEAD), jnp.bfloat16),
                pltpu.VMEM((5, 8, BLK), jnp.float32),
                pltpu.VMEM((2, BLK, 4 * BLK), jnp.float32),
                pltpu.VMEM((4, 2 * BLK, HEAD), jnp.bfloat16),
                pltpu.VMEM((4, BLK // 4, width), jnp.bfloat16),
                pltpu.VMEM((2 * BLK, HEAD), jnp.float32),
                pltpu.SemaphoreType.DMA((n_slots,)),
                pltpu.SemaphoreType.DMA((n_slots,)),
                pltpu.SemaphoreType.DMA((16,)),
                pltpu.SemaphoreType.REGULAR,
            ],
            compiler_params=pltpu.CompilerParams(
                collective_id=0, has_side_effects=True, vmem_limit_bytes=56 * 1024 * 1024
            ),
        )(
            inputs.reshape(BLK, width), seg, w_query.reshape(width, -1),
            w_keyval.reshape(rows_dev, -1), w_out.reshape(8, HEAD, width),
        )
        return made.reshape(1, 1, BLK, width)

    placed = (
        P(None, "ctx", None),
        P(None, "ctx"),
        P("phase", None, None),
        P("phase", "ctx", None),
        P("phase", None, None),
    )
    return jax.shard_map(
        local, mesh=mesh, in_specs=placed, out_specs=P("phase", None, "ctx", None), check_vma=False
    )
```

```python
import functools
import math

import jax
import jax.numpy as jnp
from jax import lax
from jax.experimental import pallas as pl
from jax.experimental.pallas import tpu as pltpu
from jax.sharding import PartitionSpec as P

MESH = pl.DeviceIdType.MESH
HEAD = 128
BLK = 128
RING = 4


def kernel(
    phases, chips, x_in, seg_in, wq_in, wkv_in, wo_in, out_ref,
    x_v, acc, wq_v, wkv_v, wo_v, wop_v, q_v, kv_v, bl_v, blo_v, bls_v, seg_v, bias_v, rel_v, far_v, res_v, sq_v, mix_v, top_v, sum_v,
    ssem, rsem, lsem, go_sem,
):
    width = x_v.shape[1]
    rows_dev = wkv_in.shape[0]
    rows_chip = 2 * rows_dev
    ph = lax.axis_index("phase")
    c = lax.axis_index("ctx")
    p = c // 2
    j = c % 2
    y = p // RING
    z = p % RING
    sib = c + 1 - 2 * j

    def at(phase, chip):
        return {"phase": phase, "ctx": chip * 2 + j}

    sibling = {"phase": ph, "ctx": sib}

    def chip_at(dy, dz):
        return ((y + dy + RING) % RING) * RING + (z + dz + RING) % RING

    y_next, y_prev = at(ph, chip_at(1, 0)), at(ph, chip_at(-1, 0))
    z_next, z_prev = at(ph, chip_at(0, 1)), at(ph, chip_at(0, -1))
    next1, next2 = at(ph, jnp.minimum(p + 1, chips - 1)), at(ph, jnp.minimum(p + 2, chips - 1))
    last1, last2 = at(ph, jnp.maximum(p - 1, 0)), at(ph, jnp.maximum(p - 2, 0))
    ph_next, ph_prev = at(jnp.minimum(ph + 1, phases - 1), p), at(jnp.maximum(ph - 1, 0), p)
    goer = jnp.where(ph < RING + 2, jnp.maximum(ph - RING + 1, 0), ph - RING)
    has_next1, has_next2 = p + 1 < chips, p + 2 < chips
    has_last1, has_last2 = p >= 1, p >= 2
    is_first, is_last = ph == 0, ph == phases - 1
    has_under = ph >= RING
    goes_late, goes_early = (ph == 1) | (ph == 2), (ph == 2) | (ph == 3)
    early_help, late_help = ph == 2 * RING - 1, (ph % RING < RING - 1)
    has_helper, has_helped = ph > 0, ph != RING - 1
    helper = jnp.where(ph == RING, 2 * RING - 1, jnp.maximum(ph - 1, 0))
    helped = jnp.where(early_help, RING, jnp.minimum(ph + 1, phases - 1))
    res_out, res_in = (ph >= 1) & (ph + 1 < phases), ph >= 2
    turn_pass = ph == 0
    low, high = ph < RING, ph >= RING
    far_chip = at(jnp.minimum(ph + RING, phases - 1), chip_at(0, -1))
    far_from, far_phase = chip_at(0, 1), jnp.maximum(ph - RING, 0)
    far_to = jnp.minimum(far_from + 2, chips - 1)
    does_far = high & (far_from + 2 < chips)
    two_back = jnp.maximum(p - 2, 0)
    far_back = at(jnp.minimum(ph + RING, phases - 1), (two_back // RING) * RING + (two_back + RING - 1) % RING)
    turn_out, turn_in = ph == RING - 1, ph == RING

    barrier = pltpu.get_barrier_semaphore()
    for device in (sibling, y_next, y_prev, z_next, z_prev):
        pl.semaphore_signal(barrier, inc=1, device_id=device, device_id_type=MESH)
    count = jnp.int32(5)
    for device, there in (
        (next1, has_next1), (next2, has_next2), (last1, has_last1), (last2, has_last2),
        (ph_next, ph + 1 < phases), (ph_prev, ph > 0), (at(goer, p), has_under), (at(ph + RING - 1, p), goes_late), (at(jnp.minimum(ph + RING, phases - 1), p), goes_early),
        (far_chip, low & has_next2), (far_back, low & has_last2),
        (at(far_phase, far_from), does_far), (at(far_phase, far_to), does_far),
        (at(helper, p), has_helper), (at(helped, p), has_helped),
        (at(helped, jnp.minimum(p + 1, chips - 1)), has_helped & has_next1),
        (at(helped, jnp.minimum(p + 2, chips - 1)), has_helped & has_next2),
        (at(helper, jnp.maximum(p - 1, 0)), has_helper & has_last1),
        (at(helper, jnp.maximum(p - 2, 0)), has_helper & has_last2),
        (at(0, p), turn_out | turn_in), (at(RING - 1, p), turn_pass), (at(RING, p), turn_pass),
        (at(jnp.minimum(ph + 1, phases - 1), chip_at(0, -1)), turn_out),
        (at(jnp.maximum(ph - 1, 0), chip_at(0, 1)), turn_in),
    ):
        @pl.when(there)
        def _(device=device):
            pl.semaphore_signal(barrier, inc=1, device_id=device, device_id_type=MESH)

        count = count + there.astype(jnp.int32)
    pl.semaphore_wait(barrier, count)

    pending = []
    slots = iter(range(ssem.shape[0]))

    def copy(src, dst, slot, device):
        return pltpu.make_async_remote_copy(
            src_ref=src, dst_ref=dst, send_sem=ssem.at[slot], recv_sem=rsem.at[slot],
            device_id=device, device_id_type=MESH,
        )

    def send(src, dst, slot, device, when=None):
        made = copy(src, dst, slot, device)
        if when is None:
            made.start()
        else:
            pl.when(when)(made.start)
        pending.append((made, when))
        return made

    def recv(dst, slot):
        copy(dst, dst, slot, sibling).wait_recv()

    def run(when, body):
        pl.when(when)(body)

    local = []

    def load(src, dst):
        made = pltpu.make_async_copy(src, dst, lsem.at[len(local)])
        made.start()
        local.append(made)
        return made

    def columns(core, tile):
        start = core * 4 * HEAD + (tile // 2) * 2 * HEAD + (tile % 2) * 8 * HEAD
        return pl.ds(pl.multiple_of(start, 2 * HEAD), 2 * HEAD)

    own_rows = pl.ds(pl.multiple_of(c * rows_dev, rows_dev), rows_dev)
    shard_loads = [load(wkv_in.at[:, columns(j, t)], wkv_v.at[t, own_rows, :]) for t in range(4)]
    seg_load = load(seg_in, seg_v.at[3 + j])
    mine = pl.ds(pl.multiple_of(j * BLK, BLK), BLK)
    theirs = pl.ds(pl.multiple_of((1 - j) * BLK, BLK), BLK)
    wq_loads = [
        load(wq_in.at[:, pl.ds(pl.multiple_of(j * 4 * HEAD + t * 2 * HEAD, 2 * HEAD), 2 * HEAD)], wq_v.at[t])
        for t in range(2)
    ]
    wo_load = load(wo_in, wo_v)

    halo_slots = [[next(slots) for _ in range(4)] for _ in range(4)]
    rel_slots = [next(slots) for _ in range(4)]
    far_slots = [next(slots) for _ in range(4)]
    helped_high = helped >= RING
    rel_copies = []
    for h in range(4):
        rel_copies.append((copy(rel_v.at[h], kv_v.at[h, 1, pl.ds(BLK, 2 * BLK), :], halo_slots[h][2],
                                at(helped, jnp.minimum(p + 1, chips - 1))),
                           has_helped & has_next1 & (True if h > 0 else jnp.logical_not(helped_high))))
    for h in range(1, 4):
        rel_copies.append((copy(rel_v.at[h, pl.ds(BLK, BLK), :], kv_v.at[h, 1, pl.ds(0, BLK), :], halo_slots[h][3],
                                at(helped, jnp.minimum(p + 2, chips - 1))), has_helped & has_next2 & helped_high))
    far_copies = [
        (copy(far_v.at[h], kv_v.at[h, 1, pl.ds(0, BLK), :], halo_slots[h][3], at(far_phase, far_to)), does_far)
        for h in range(4)
    ]

    def help_halo():
        for h in range(4):
            @pl.when(rel_copies[h][1])
            def _(h=h):
                recv(rel_v.at[h], rel_slots[h])
                rel_copies[h][0].start()

            if h > 0:
                pl.when(rel_copies[h + 3][1])(rel_copies[h + 3][0].start)

    def help_far():
        for h in range(4):
            recv(far_v.at[h], far_slots[h])
            far_copies[h][0].start()

    sib_rows = pl.ds(pl.multiple_of(sib * rows_dev, rows_dev), rows_dev)
    shard_slots = [next(slots) for _ in range(4)]
    seg_slots = [next(slots) for _ in range(3)]

    for t in range(4):
        send(wkv_in.at[:, columns(1 - j, t)], wkv_v.at[t, own_rows, :], shard_slots[t], sibling)
    send(seg_in, seg_v.at[3 + j], seg_slots[0], sibling)

    wop_slots = [next(slots) for _ in range(4)]

    def send_wop(when, devices):
        for k in range(4):
            send(wo_in.at[4 * j + k], wop_v.at[4 * j + k], wop_slots[k], devices[k // 2], when)

    send_wop((ph + 1 < phases) & jnp.logical_not(turn_out), (ph_next, ph_next))
    x_slot = next(slots)
    x_prev_slots = [next(slots) for _ in range(4)]
    x_relay_slots = [next(slots) for _ in range(4)]
    res_slots = [next(slots) for _ in range(4)]
    x_load = pltpu.make_async_copy(x_in, x_v.at[mine], lsem.at[len(local)])
    x_direct = copy(x_in, x_v.at[mine], x_slot, sibling)

    @pl.when(ph < 2)
    def _():
        x_load.start()
        x_direct.start()

    for made in shard_loads:
        made.wait()
    for t in range(4):
        recv(wkv_v.at[t, sib_rows, :], shard_slots[t])

    def slab(chip, first, count_):
        return wkv_v.at[pl.ds(first, count_), pl.ds(pl.multiple_of(chip * rows_chip, rows_chip), rows_chip), :]

    sets = []
    for s in range(2):
        sets.append(dict(
            tile=2 * s,
            prim=(y_next, y_prev) if s == 0 else (z_next, z_prev),
            sec=(z_next, z_prev) if s == 0 else (y_next, y_prev),
            chip=(lambda a, b: chip_at(a, b)) if s == 0 else (lambda a, b: chip_at(b, a)),
            pslot=[next(slots) for _ in range(4)],
            sslot={dp: [next(slots) for _ in range(4)] for dp in (0, -1, 1, 2)},
        ))

    def ring_send(g, ring, slot, dp):
        piece = slab(g["chip"](dp, 0), g["tile"], 2)
        send(piece, piece, slot[0], ring[0])
        send(piece, piece, slot[1], ring[1])

    def ring_forward(g, ring, slot, before, after):
        piece = slab(before, g["tile"], 2)
        recv(piece, slot[0])
        half = slab(before, g["tile"], 1)
        send(half, half, slot[2], ring[0])
        piece = slab(after, g["tile"], 2)
        recv(piece, slot[1])
        half = slab(after, g["tile"] + 1, 1)
        send(half, half, slot[3], ring[1])

    def ring_end(g, slot, far):
        recv(slab(far, g["tile"], 1), slot[2])
        recv(slab(far, g["tile"] + 1, 1), slot[3])

    seg_load.wait()
    recv(seg_v.at[4 - j], seg_slots[0])
    send(seg_v.at[pl.ds(3, 2)], seg_v.at[pl.ds(1, 2)], seg_slots[1], next1, has_next1)
    send(seg_v.at[4], seg_v.at[0], seg_slots[2], next2, has_next2)

    @pl.when(jnp.logical_not(has_last1))
    def _():
        seg_v[1:3] = jnp.full((2,) + seg_v.shape[1:], -1.0, jnp.float32)
        kv_v[:, :, BLK:3 * BLK, :] = jnp.zeros((4, 2, 2 * BLK, HEAD), jnp.bfloat16)

    @pl.when(jnp.logical_not(has_last2))
    def _():
        seg_v[0] = jnp.full(seg_v.shape[1:], -1.0, jnp.float32)
        kv_v[:, :, 0:BLK, :] = jnp.zeros((4, 2, BLK, HEAD), jnp.bfloat16)

    pl.when(does_far & (ph < RING + 2))(help_far)
    pl.when(has_under)(lambda: pl.semaphore_wait(go_sem, 1))
    for g in sets:
        ring_send(g, g["prim"], g["pslot"], 0)
        ring_send(g, g["sec"], g["sslot"][0], 0)
    run(has_last1, lambda: recv(seg_v.at[pl.ds(1, 2)], seg_slots[1]))
    run(has_last2, lambda: recv(seg_v.at[0], seg_slots[2]))

    row_id = lax.broadcasted_iota(jnp.int32, (BLK, BLK), 0)
    col_id = lax.broadcasted_iota(jnp.int32, (BLK, BLK), 1)
    causal = col_id <= row_id
    for i in range(2):
        asking = jnp.transpose(jnp.broadcast_to(seg_v[3 + i, 0:1, :], (BLK, BLK)))
        for b in range(4):
            asked = jnp.broadcast_to(seg_v[i + b, 0:1, :], (BLK, BLK))
            ok = asking == asked
            if b == 3:
                ok = ok & causal
            bias_v[i, :, b * BLK:(b + 1) * BLK] = jnp.where(ok, 0.0, -1e30).astype(jnp.float32)

    for g in sets:
        ring_forward(g, g["prim"], g["pslot"], g["chip"](-1, 0), g["chip"](1, 0))
        ring_send(g, g["sec"], g["sslot"][-1], -1)
        ring_send(g, g["sec"], g["sslot"][1], 1)
    for g in sets:
        ring_forward(g, g["sec"], g["sslot"][0], g["chip"](0, -1), g["chip"](0, 1))
    for g in sets:
        ring_end(g, g["pslot"], g["chip"](2, 0))
        ring_send(g, g["sec"], g["sslot"][2], 2)
    for dp in (-1, 1, 2):
        for g in sets:
            ring_forward(g, g["sec"], g["sslot"][dp], g["chip"](dp, -1), g["chip"](dp, 1))

    for dp in (0, -1, 1, 2):
        for g in sets:
            ring_end(g, g["sslot"][dp], g["chip"](dp, 2))
    for made in wq_loads:
        made.wait()
    wo_load.wait()

    def go(phase):
        pl.semaphore_signal(go_sem, inc=1, device_id=at(jnp.minimum(phase, phases - 1), p), device_id_type=MESH)

    piece = BLK // 4

    def mine_at(k):
        return x_v.at[pl.ds(pl.multiple_of(j * BLK + k * piece, piece), piece), :]

    def theirs_at(k):
        return x_v.at[pl.ds(pl.multiple_of((1 - j) * BLK + k * piece, piece), piece), :]

    res_copies = [copy(res_v.at[k], mine_at(k), x_prev_slots[k], at(RING, p)) for k in range(1, 4)]

    def pass_residual():
        for k in range(1, 4):
            recv(res_v.at[k], res_slots[k])
            res_copies[k - 1].start()

    pl.when(goes_early)(lambda: go(ph + RING))
    pl.when(does_far & (ph >= RING + 2))(help_far)
    pl.when(early_help)(help_halo)
    send_wop(turn_out, (ph_next, at(jnp.minimum(ph + 1, phases - 1), chip_at(0, -1))))

    wop_relay = [next(slots) for _ in range(4)]
    relays = []
    for k in range(4):
        relays.append(copy(wop_v.at[4 * j + k], wop_v.at[4 * j + k], wop_relay[k], sibling))
    x_relays = [copy(mine_at(k), mine_at(k), x_relay_slots[k], sibling) for k in range(4)]

    @pl.when(ph > 0)
    def _():
        for k in range(4):
            recv(wop_v.at[4 * j + k], wop_slots[k])
            relays[k].start()

    @pl.when(ph < 2)
    def _():
        x_load.wait()
        x_direct.wait_send()
        recv(x_v.at[theirs], x_slot)

    bl_slots = [next(slots) for _ in range(4)]
    bl_relay_slots = [next(slots) for _ in range(4)]
    bl_relays = [copy(bl_v.at[4 * j + h], bl_v.at[4 * j + h], bl_relay_slots[h], sibling) for h in range(4)]
    step = 512 if width % 512 == 0 else width

    def add_squares(n, rounded):
        wide = rounded.astype(jnp.float32)
        wide = wide * wide
        lanes = wide[:, :HEAD]
        for m in range(HEAD, step, HEAD):
            lanes = lanes + wide[:, m:m + HEAD]
        sq_v[...] = lanes if n == 0 else sq_v[...] + lanes


    @pl.when(ph > 0)
    def _():
        for k in range(4):
            recv(wop_v.at[4 * (1 - j) + k], wop_relay[k])
        mine_head, their_head = 4 * j, 4 * (1 - j)
        def take(h):
            recv(bl_v.at[mine_head + h], bl_slots[h])
            bl_relays[h].start()

        def project_heads(first):
            heads = [mine_head + first, mine_head + first + 1, their_head + first, their_head + first + 1]
            lhs = jnp.concatenate([bl_v[head] for head in heads], axis=1)
            for n in range(0, width, step):
                rhs = jnp.concatenate([wop_v[head, :, n:n + step] for head in heads], axis=0)
                part = jnp.dot(lhs, rhs, preferred_element_type=jnp.float32)
                if first == 0:
                    acc[:, n:n + step] = part
                else:
                    total = x_v[:, n:n + step].astype(jnp.float32) + (acc[:, n:n + step] + part)
                    total = total.astype(jnp.bfloat16)
                    x_v[:, n:n + step] = total
                    add_squares(n, total)

        take(0)
        take(1)

        @pl.when(ph >= 2)
        def _():
            for k in range(4):
                recv(mine_at(k), x_prev_slots[k])
                x_relays[k].start()

        recv(bl_v.at[their_head], bl_relay_slots[0])
        recv(bl_v.at[their_head + 1], bl_relay_slots[1])
        take(2)
        project_heads(0)
        take(3)
        recv(bl_v.at[their_head + 2], bl_relay_slots[2])
        recv(bl_v.at[their_head + 3], bl_relay_slots[3])

        @pl.when(ph >= 2)
        def _():
            for k in range(4):
                recv(theirs_at(k), x_relay_slots[k])
            for k in range(4):
                x_relays[k].wait_send()

        project_heads(2)

    @pl.when(is_first)
    def _():
        for n in range(0, width, step):
            add_squares(n, x_v[:, n:n + step])

    square = jnp.sum(sq_v[...], axis=1, keepdims=True)
    scale_rows = lax.rsqrt(square * (1.0 / width) + 1e-05)

    for k in range(4):
        send(mine_at(k), mine_at(k), x_prev_slots[k], ph_next, res_out if k == 0 else res_out & jnp.logical_not(turn_out))
        if k > 0:
            send(mine_at(k), res_v.at[k], res_slots[k], at(0, p), turn_out)
    stream = x_v[...]

    def project(weights):
        return (jnp.dot(stream, weights, preferred_element_type=jnp.float32) * scale_rows).astype(jnp.bfloat16)

    for kind in (1, 0):
        for t in range(2):
            made = project(wkv_v[2 * t + kind])
            kv_v[2 * t, kind, 3 * BLK:5 * BLK, :] = made[:, :HEAD]
            kv_v[2 * t + 1, kind, 3 * BLK:5 * BLK, :] = made[:, HEAD:]
            for h in (2 * t, 2 * t + 1):
                both = kv_v.at[h, kind, pl.ds(3 * BLK, 2 * BLK), :]
                odd = kv_v.at[h, kind, pl.ds(4 * BLK, BLK), :]
                to_next1, to_next2 = kv_v.at[h, kind, pl.ds(BLK, 2 * BLK), :], kv_v.at[h, kind, pl.ds(0, BLK), :]
                if kind == 0:
                    send(both, to_next1, halo_slots[h][0], next1, has_next1)
                    send(odd, to_next2, halo_slots[h][1], next2, has_next2 & high)
                    continue
                straight = is_first | high if h < 1 else is_first
                send(both, rel_v.at[h], rel_slots[h], at(helper, p), has_next1 & jnp.logical_not(straight))
                send(both, to_next1, halo_slots[h][2], next1, straight & has_next1)
                if h < 1:
                    send(odd, to_next2, halo_slots[h][3], next2, has_next2 & high)
                send(odd, far_v.at[h], far_slots[h], far_chip, has_next2 & low)
    for t in range(2):
        made = project(wq_v[t])
        q_v[2 * t] = made[:, :HEAD]
        q_v[2 * t + 1] = made[:, HEAD:]

    bls_slots = [next(slots) for _ in range(4)]
    factor = math.log2(math.e) / math.sqrt(HEAD)

    def scored(h, i, keys, first):
        query = q_v[h, i * BLK:(i + 1) * BLK, :]
        scores = lax.dot_general(query, keys, (((1,), (1,)), ((), ())), preferred_element_type=jnp.float32)
        return scores * factor + bias_v[i, :, first:first + keys.shape[0]]

    def mix(weights, values):
        return jnp.dot(weights.astype(jnp.bfloat16), values, preferred_element_type=jnp.float32)

    near = ((0, 3 * BLK, 4 * BLK, 3 * BLK), (1, 3 * BLK, 5 * BLK, 2 * BLK))
    far = ((0, 0, 3 * BLK, 0), (1, BLK, 3 * BLK, 0))
    for h in range(4):
        scores = [scored(h, i, kv_v[h, 0, lo:hi, :], first) for i, lo, hi, first in near]
        tops = [jnp.max(part, axis=1, keepdims=True) for part in scores]
        weights = [jnp.exp2(part - top) for part, top in zip(scores, tops)]
        sums = [jnp.sum(part, axis=1, keepdims=True) for part in weights]
        for (i, lo, hi, _), part, top, total in zip(near, weights, tops, sums):
            rows = slice(i * BLK, (i + 1) * BLK)
            mix_v[h, rows, :] = mix(part, kv_v[h, 1, lo:hi, :])
            top_v[h, rows, :] = jnp.broadcast_to(top, (BLK, HEAD))
            sum_v[h, rows, :] = jnp.broadcast_to(total, (BLK, HEAD))

    for h in range(4):
        run(has_last1 & low, lambda h=h: recv(kv_v.at[h, 0, pl.ds(BLK, 2 * BLK), :], halo_slots[h][0]))
        send(kv_v.at[h, 0, pl.ds(2 * BLK, BLK), :], kv_v.at[h, 0, pl.ds(0, BLK), :], halo_slots[h][1], next1,
             low & has_last1 & has_next1)
    for h in range(4):
        run(has_last1 & high, lambda h=h: recv(kv_v.at[h, 0, pl.ds(BLK, 2 * BLK), :], halo_slots[h][0]))
        run(has_last1, lambda h=h: recv(kv_v.at[h, 1, pl.ds(BLK, 2 * BLK), :], halo_slots[h][2]))
        for kind in range(2):
            run(has_last2, lambda h=h, kind=kind: recv(kv_v.at[h, kind, pl.ds(0, BLK), :], halo_slots[h][2 * kind + 1]))
        scores = [scored(h, i, kv_v[h, 0, lo:hi, :], first) for i, lo, hi, first in far]
        before = [top_v[h, i * BLK:(i + 1) * BLK, :] for i in range(2)]
        tops = [jnp.maximum(jnp.max(part, axis=1, keepdims=True), old) for part, old in zip(scores, before)]
        weights = [
            jnp.exp2(part - jnp.concatenate([top] * (part.shape[1] // HEAD), axis=1)) for part, top in zip(scores, tops)
        ]
        sums = [jnp.sum(part, axis=1, keepdims=True) for part in weights]
        mixed = [mix(part, kv_v[h, 1, lo:hi, :]) for part, (_, lo, hi, _) in zip(weights, far)]
        for i in range(2):
            rows = slice(i * BLK, (i + 1) * BLK)
            shrink = jnp.exp2(before[i] - tops[i])
            total = sum_v[h, rows, :] * shrink + sums[i]
            blo_v[h, rows, :] = ((mix_v[h, rows, :] * shrink + mixed[i]) / total).astype(jnp.bfloat16)
        send(blo_v.at[h], bl_v.at[4 * j + h], bl_slots[h], ph_next, ph + 1 < phases)
        send(blo_v.at[h, theirs, :], bls_v.at[h], bls_slots[h], sibling)

    pl.when(goes_late)(lambda: go(ph + RING - 1))

    for h in range(4):
        recv(bls_v.at[h], bls_slots[h])
    own = jnp.concatenate([blo_v[h, mine, :] for h in range(4)], axis=1)
    other = jnp.concatenate([bls_v[h] for h in range(4)], axis=1)
    for n in range(0, width, step):
        first = wo_v[pl.ds(4 * j, 4), :, n:n + step].reshape(4 * HEAD, step)
        second = wo_v[pl.ds(4 * (1 - j), 4), :, n:n + step].reshape(4 * HEAD, step)
        update = jnp.dot(own, first, preferred_element_type=jnp.float32)
        update = update + jnp.dot(other, second, preferred_element_type=jnp.float32)
        out_ref[:, n:n + step] = (x_v[mine, n:n + step].astype(jnp.float32) + update).astype(jnp.bfloat16)

    pl.when(late_help)(help_halo)
    pl.when(turn_pass)(pass_residual)
    for made, when in pending + rel_copies + far_copies + [(made, turn_pass) for made in res_copies]:
        if when is None:
            made.wait_send()
        else:
            pl.when(when)(made.wait_send)

    @pl.when(ph > 0)
    def _():
        for made in relays + bl_relays:
            made.wait_send()


def solution(mesh):
    phases, devices = mesh.shape["phase"], mesh.shape["ctx"]
    chips = devices // 2

    def local(inputs, segment_ids, w_query, w_keyval, w_out):
        width = inputs.shape[2]
        rows_dev = w_keyval.shape[1]
        seg = jnp.broadcast_to(segment_ids.astype(jnp.float32), (8, BLK))
        any_space = pl.BlockSpec(memory_space=pl.ANY)
        n_slots = 128
        made = pl.pallas_call(
            functools.partial(kernel, phases, chips),
            out_shape=jax.ShapeDtypeStruct((BLK, width), jnp.bfloat16),
            in_specs=[any_space] * 5,
            out_specs=pl.BlockSpec(memory_space=pltpu.VMEM),
            scratch_shapes=[
                pltpu.VMEM((2 * BLK, width), jnp.bfloat16),
                pltpu.VMEM((2 * BLK, width), jnp.float32),
                pltpu.VMEM((2, width, 2 * HEAD), jnp.bfloat16),
                pltpu.VMEM((4, width, 2 * HEAD), jnp.bfloat16),
                pltpu.VMEM((8, HEAD, width), jnp.bfloat16),
                pltpu.VMEM((8, HEAD, width), jnp.bfloat16),
                pltpu.VMEM((4, 2 * BLK, HEAD), jnp.bfloat16),
                pltpu.VMEM((4, 2, 5 * BLK, HEAD), jnp.bfloat16),
                pltpu.VMEM((8, 2 * BLK, HEAD), jnp.bfloat16),
                pltpu.VMEM((4, 2 * BLK, HEAD), jnp.bfloat16),
                pltpu.VMEM((4, BLK, HEAD), jnp.bfloat16),
                pltpu.VMEM((5, 8, BLK), jnp.float32),
                pltpu.VMEM((2, BLK, 4 * BLK), jnp.float32),
                pltpu.VMEM((4, 2 * BLK, HEAD), jnp.bfloat16),
                pltpu.VMEM((4, BLK, HEAD), jnp.bfloat16),
                pltpu.VMEM((4, BLK // 4, width), jnp.bfloat16),
                pltpu.VMEM((2 * BLK, HEAD), jnp.float32),
                pltpu.VMEM((4, 2 * BLK, HEAD), jnp.float32),
                pltpu.VMEM((4, 2 * BLK, HEAD), jnp.float32),
                pltpu.VMEM((4, 2 * BLK, HEAD), jnp.float32),
                pltpu.SemaphoreType.DMA((n_slots,)),
                pltpu.SemaphoreType.DMA((n_slots,)),
                pltpu.SemaphoreType.DMA((16,)),
                pltpu.SemaphoreType.REGULAR,
            ],
            compiler_params=pltpu.CompilerParams(
                collective_id=0, has_side_effects=True, vmem_limit_bytes=56 * 1024 * 1024
            ),
        )(
            inputs.reshape(BLK, width), seg, w_query.reshape(width, -1),
            w_keyval.reshape(rows_dev, -1), w_out.reshape(8, HEAD, width),
        )
        return made.reshape(1, 1, BLK, width)

    placed = (
        P(None, "ctx", None),
        P(None, "ctx"),
        P("phase", None, None),
        P("phase", "ctx", None),
        P("phase", None, None),
    )
    return jax.shard_map(
        local, mesh=mesh, in_specs=placed, out_specs=P("phase", None, "ctx", None), check_vma=False
    )
```

```python
import functools
import math

import jax
import jax.numpy as jnp
from jax import lax
from jax.experimental import pallas as pl
from jax.experimental.pallas import tpu as pltpu
from jax.sharding import PartitionSpec as P

MESH = pl.DeviceIdType.MESH
HEAD = 128
BLK = 128
RING = 4


def kernel(
    phases, chips, x_in, seg_in, wq_in, wkv_in, wo_in, out_ref,
    x_v, acc, wq_v, wkv_v, wo_v, wop_v, q_v, kv_v, bl_v, blo_v, bls_v, seg_v, bias_v, rel_v, far_v, sq_v, mix_v, top_v, sum_v,
    ssem, rsem, lsem, go_sem,
):
    width = x_v.shape[1]
    rows_dev = wkv_in.shape[0]
    rows_chip = 2 * rows_dev
    ph = lax.axis_index("phase")
    c = lax.axis_index("ctx")
    p = c // 2
    j = c % 2
    y = p // RING
    z = p % RING
    sib = c + 1 - 2 * j

    def at(phase, chip):
        return {"phase": phase, "ctx": chip * 2 + j}

    sibling = {"phase": ph, "ctx": sib}

    def chip_at(dy, dz):
        return ((y + dy + RING) % RING) * RING + (z + dz + RING) % RING

    y_next, y_prev = at(ph, chip_at(1, 0)), at(ph, chip_at(-1, 0))
    z_next, z_prev = at(ph, chip_at(0, 1)), at(ph, chip_at(0, -1))
    next1, next2 = at(ph, jnp.minimum(p + 1, chips - 1)), at(ph, jnp.minimum(p + 2, chips - 1))
    last1, last2 = at(ph, jnp.maximum(p - 1, 0)), at(ph, jnp.maximum(p - 2, 0))
    ph_next, ph_prev = at(jnp.minimum(ph + 1, phases - 1), p), at(jnp.maximum(ph - 1, 0), p)
    goer = jnp.where(ph < RING + 2, jnp.maximum(ph - RING + 1, 0), ph - RING)
    has_next1, has_next2 = p + 1 < chips, p + 2 < chips
    has_last1, has_last2 = p >= 1, p >= 2
    is_first, is_last = ph == 0, ph == phases - 1
    has_under = ph >= RING
    goes_late, goes_early = (ph == 1) | (ph == 2), (ph == 2) | (ph == 3)
    early_help, late_help = ph == 2 * RING - 1, (ph % RING < RING - 1)
    has_helper, has_helped = ph > 0, ph != RING - 1
    helper = jnp.where(ph == RING, 2 * RING - 1, jnp.maximum(ph - 1, 0))
    helped = jnp.where(early_help, RING, jnp.minimum(ph + 1, phases - 1))
    row_end = z == RING - 1
    helper_chip = jnp.where(row_end, jnp.minimum(p + RING, chips - 1), p)
    helped_chip = jnp.where(row_end, jnp.maximum(p - RING, 0), p)
    helped_to1, helped_to2 = jnp.minimum(helped_chip + 1, chips - 1), jnp.minimum(helped_chip + 2, chips - 1)
    has_helped = has_helped & (jnp.logical_not(row_end) | (p >= RING))
    helped1, helped2 = has_helped & (helped_chip + 1 < chips), has_helped & (helped_chip + 2 < chips)

    def helper_of(chip):
        chip = jnp.maximum(chip, 0)
        return at(helper, jnp.where(chip % RING == RING - 1, jnp.minimum(chip + RING, chips - 1), chip))

    res_out, res_in = ph + 2 < phases, ph >= 2
    ph_next2, ph_prev2 = at(jnp.minimum(ph + 2, phases - 1), p), at(jnp.maximum(ph - 2, 0), p)
    low, high = ph < RING, ph >= RING
    def far_of(chip):
        chip = jnp.clip(chip, 0, chips - 1)
        crossing = chip % RING >= 2
        row = jnp.minimum(chip // RING + jnp.where(crossing, 1, 0), RING - 1)
        return at(jnp.minimum(ph + RING, phases - 1), row * RING + (chip % RING + RING - 1) % RING)

    far_chip, far_back = far_of(p), far_of(p - 2)
    far_z = (z + 1) % RING
    far_row = y - jnp.where(far_z >= 2, 1, 0)
    far_from, far_phase = jnp.maximum(far_row, 0) * RING + far_z, jnp.maximum(ph - RING, 0)
    far_to = jnp.minimum(far_from + 2, chips - 1)
    does_far = high & (far_row >= 0) & (far_from + 2 < chips)
    turn_out, turn_in = ph == RING - 1, ph == RING

    barrier = pltpu.get_barrier_semaphore()
    for device in (sibling, y_next, y_prev, z_next, z_prev):
        pl.semaphore_signal(barrier, inc=1, device_id=device, device_id_type=MESH)
    count = jnp.int32(5)
    for device, there in (
        (next1, has_next1), (next2, has_next2), (last1, has_last1), (last2, has_last2),
        (ph_next, ph + 1 < phases), (ph_prev, ph > 0), (at(goer, p), has_under), (at(ph + RING - 1, p), goes_late), (at(jnp.minimum(ph + RING, phases - 1), p), goes_early),
        (far_chip, low & has_next2), (far_back, low & has_last2),
        (at(far_phase, far_from), does_far), (at(far_phase, far_to), does_far),
        (helper_of(p), has_helper & has_next1), (at(helped, helped_chip), helped1),
        (at(helped, helped_to1), helped1), (at(helped, helped_to2), helped2),
        (helper_of(p - 1), has_helper & has_last1), (helper_of(p - 2), has_helper & has_last2),
        (ph_next2, res_out), (ph_prev2, res_in),
        (at(jnp.minimum(ph + 1, phases - 1), chip_at(0, -1)), turn_out),
        (at(jnp.maximum(ph - 1, 0), chip_at(0, 1)), turn_in),
    ):
        @pl.when(there)
        def _(device=device):
            pl.semaphore_signal(barrier, inc=1, device_id=device, device_id_type=MESH)

        count = count + there.astype(jnp.int32)
    pl.semaphore_wait(barrier, count)

    pending = []
    slots = iter(range(ssem.shape[0]))

    def copy(src, dst, slot, device):
        return pltpu.make_async_remote_copy(
            src_ref=src, dst_ref=dst, send_sem=ssem.at[slot], recv_sem=rsem.at[slot],
            device_id=device, device_id_type=MESH,
        )

    def send(src, dst, slot, device, when=None):
        made = copy(src, dst, slot, device)
        if when is None:
            made.start()
        else:
            pl.when(when)(made.start)
        pending.append((made, when))
        return made

    def recv(dst, slot):
        copy(dst, dst, slot, sibling).wait_recv()

    def run(when, body):
        pl.when(when)(body)

    local = []

    def load(src, dst):
        made = pltpu.make_async_copy(src, dst, lsem.at[len(local)])
        made.start()
        local.append(made)
        return made

    def columns(core, tile):
        start = core * 4 * HEAD + (tile // 2) * 2 * HEAD + (tile % 2) * 8 * HEAD
        return pl.ds(pl.multiple_of(start, 2 * HEAD), 2 * HEAD)

    own_rows = pl.ds(pl.multiple_of(c * rows_dev, rows_dev), rows_dev)
    shard_loads = [load(wkv_in.at[:, columns(j, t)], wkv_v.at[t, own_rows, :]) for t in range(4)]
    seg_load = load(seg_in, seg_v.at[3 + j])
    mine = pl.ds(pl.multiple_of(j * BLK, BLK), BLK)
    theirs = pl.ds(pl.multiple_of((1 - j) * BLK, BLK), BLK)
    wq_loads = [
        load(wq_in.at[:, pl.ds(pl.multiple_of(j * 4 * HEAD + t * 2 * HEAD, 2 * HEAD), 2 * HEAD)], wq_v.at[t])
        for t in range(2)
    ]
    wo_load = load(wo_in, wo_v)

    halo_slots = [[next(slots) for _ in range(4)] for _ in range(4)]
    rel_slots = [[next(slots), next(slots)] for _ in range(4)]
    late_slots = [next(slots) for _ in range(4)]
    far_slots = [next(slots) for _ in range(4)]
    helped_high = helped >= RING
    rel_copies = []
    for h in range(4):
        needed = helped1 & (True if h > 0 else jnp.logical_not(helped_high))
        for b, slot in enumerate((halo_slots[h][2], late_slots[h])):
            rel_copies.append((copy(rel_v.at[h, pl.ds(b * BLK, BLK), :], kv_v.at[h, 1, pl.ds((b + 1) * BLK, BLK), :],
                                    slot, at(helped, helped_to1)), needed))
    for h in range(1, 4):
        rel_copies.append((copy(rel_v.at[h, pl.ds(BLK, BLK), :], kv_v.at[h, 1, pl.ds(0, BLK), :], halo_slots[h][3],
                                at(helped, helped_to2)), helped2 & helped_high))
    far_copies = [
        (copy(far_v.at[h], kv_v.at[h, 1, pl.ds(0, BLK), :], halo_slots[h][3], at(far_phase, far_to)), does_far)
        for h in range(4)
    ]

    def help_halo():
        for h in range(4):
            @pl.when(rel_copies[2 * h][1])
            def _(h=h):
                for b in range(2):
                    recv(rel_v.at[h, pl.ds(b * BLK, BLK), :], rel_slots[h][b])
                    rel_copies[2 * h + b][0].start()

            if h > 0:
                pl.when(rel_copies[h + 7][1])(rel_copies[h + 7][0].start)

    def help_far():
        for h in range(4):
            recv(far_v.at[h], far_slots[h])
            far_copies[h][0].start()

    sib_rows = pl.ds(pl.multiple_of(sib * rows_dev, rows_dev), rows_dev)
    shard_slots = [next(slots) for _ in range(4)]
    seg_slots = [next(slots) for _ in range(3)]

    for t in range(4):
        send(wkv_in.at[:, columns(1 - j, t)], wkv_v.at[t, own_rows, :], shard_slots[t], sibling)
    send(seg_in, seg_v.at[3 + j], seg_slots[0], sibling)

    wop_slots = [next(slots) for _ in range(4)]

    def send_wop(when, devices):
        for k in range(4):
            send(wo_in.at[4 * j + k], wop_v.at[4 * j + k], wop_slots[k], devices[k // 2], when)

    send_wop((ph + 1 < phases) & jnp.logical_not(turn_out), (ph_next, ph_next))
    x_slot = next(slots)
    x_prev_slots = [next(slots) for _ in range(4)]
    x_relay_slots = [next(slots) for _ in range(4)]
    x_load = pltpu.make_async_copy(x_in, x_v.at[mine], lsem.at[len(local)])
    x_direct = copy(x_in, x_v.at[mine], x_slot, sibling)

    @pl.when(ph < 2)
    def _():
        x_load.start()
        x_direct.start()

    for made in shard_loads:
        made.wait()
    for t in range(4):
        recv(wkv_v.at[t, sib_rows, :], shard_slots[t])

    def slab(chip, first, count_):
        return wkv_v.at[pl.ds(first, count_), pl.ds(pl.multiple_of(chip * rows_chip, rows_chip), rows_chip), :]

    sets = []
    for s in range(2):
        sets.append(dict(
            tile=2 * s,
            prim=(y_next, y_prev) if s == 0 else (z_next, z_prev),
            sec=(z_next, z_prev) if s == 0 else (y_next, y_prev),
            chip=(lambda a, b: chip_at(a, b)) if s == 0 else (lambda a, b: chip_at(b, a)),
            pslot=[next(slots) for _ in range(4)],
            sslot={dp: [next(slots) for _ in range(4)] for dp in (0, -1, 1, 2)},
        ))

    def ring_send(g, ring, slot, dp):
        piece = slab(g["chip"](dp, 0), g["tile"], 2)
        send(piece, piece, slot[0], ring[0])
        send(piece, piece, slot[1], ring[1])

    def ring_forward(g, ring, slot, before, after):
        piece = slab(before, g["tile"], 2)
        recv(piece, slot[0])
        half = slab(before, g["tile"], 1)
        send(half, half, slot[2], ring[0])
        piece = slab(after, g["tile"], 2)
        recv(piece, slot[1])
        half = slab(after, g["tile"] + 1, 1)
        send(half, half, slot[3], ring[1])

    def ring_end(g, slot, far):
        recv(slab(far, g["tile"], 1), slot[2])
        recv(slab(far, g["tile"] + 1, 1), slot[3])

    seg_load.wait()
    recv(seg_v.at[4 - j], seg_slots[0])
    send(seg_v.at[pl.ds(3, 2)], seg_v.at[pl.ds(1, 2)], seg_slots[1], next1, has_next1)
    send(seg_v.at[4], seg_v.at[0], seg_slots[2], next2, has_next2)

    @pl.when(jnp.logical_not(has_last1))
    def _():
        seg_v[1:3] = jnp.full((2,) + seg_v.shape[1:], -1.0, jnp.float32)
        kv_v[:, :, BLK:3 * BLK, :] = jnp.zeros((4, 2, 2 * BLK, HEAD), jnp.bfloat16)

    @pl.when(jnp.logical_not(has_last2))
    def _():
        seg_v[0] = jnp.full(seg_v.shape[1:], -1.0, jnp.float32)
        kv_v[:, :, 0:BLK, :] = jnp.zeros((4, 2, BLK, HEAD), jnp.bfloat16)

    pl.when(does_far & (ph < RING + 2))(help_far)
    pl.when(has_under)(lambda: pl.semaphore_wait(go_sem, 1))
    for g in sets:
        ring_send(g, g["prim"], g["pslot"], 0)
        ring_send(g, g["sec"], g["sslot"][0], 0)
    run(has_last1, lambda: recv(seg_v.at[pl.ds(1, 2)], seg_slots[1]))
    run(has_last2, lambda: recv(seg_v.at[0], seg_slots[2]))

    row_id = lax.broadcasted_iota(jnp.int32, (BLK, BLK), 0)
    col_id = lax.broadcasted_iota(jnp.int32, (BLK, BLK), 1)
    causal = col_id <= row_id
    for i in range(2):
        asking = jnp.transpose(jnp.broadcast_to(seg_v[3 + i, 0:1, :], (BLK, BLK)))
        for b in range(4):
            asked = jnp.broadcast_to(seg_v[i + b, 0:1, :], (BLK, BLK))
            ok = asking == asked
            if b == 3:
                ok = ok & causal
            bias_v[i, :, b * BLK:(b + 1) * BLK] = jnp.where(ok, 0.0, -1e30).astype(jnp.float32)

    for g in sets:
        ring_forward(g, g["prim"], g["pslot"], g["chip"](-1, 0), g["chip"](1, 0))
        ring_send(g, g["sec"], g["sslot"][-1], -1)
        ring_send(g, g["sec"], g["sslot"][1], 1)
    for g in sets:
        ring_forward(g, g["sec"], g["sslot"][0], g["chip"](0, -1), g["chip"](0, 1))
    for g in sets:
        ring_end(g, g["pslot"], g["chip"](2, 0))
        ring_send(g, g["sec"], g["sslot"][2], 2)
    for dp in (-1, 1, 2):
        for g in sets:
            ring_forward(g, g["sec"], g["sslot"][dp], g["chip"](dp, -1), g["chip"](dp, 1))

    for dp in (0, -1, 1, 2):
        for g in sets:
            ring_end(g, g["sslot"][dp], g["chip"](dp, 2))
    for made in wq_loads:
        made.wait()
    wo_load.wait()

    def go(phase):
        pl.semaphore_signal(go_sem, inc=1, device_id=at(jnp.minimum(phase, phases - 1), p), device_id_type=MESH)

    piece = width // 4

    def mine_at(k):
        return x_v.at[mine, pl.ds(k * piece, piece)]

    def theirs_at(k):
        return x_v.at[theirs, pl.ds(k * piece, piece)]

    pl.when(goes_early)(lambda: go(ph + RING))
    pl.when(does_far & (ph >= RING + 2))(help_far)
    pl.when(early_help)(help_halo)
    send_wop(turn_out, (ph_next, at(jnp.minimum(ph + 1, phases - 1), chip_at(0, -1))))

    wop_relay = [next(slots) for _ in range(4)]
    relays = []
    for k in range(4):
        relays.append(copy(wop_v.at[4 * j + k], wop_v.at[4 * j + k], wop_relay[k], sibling))
    x_relays = [copy(mine_at(k), mine_at(k), x_relay_slots[k], sibling) for k in range(4)]

    def take_wop(first):
        for k in (first, first + 1):
            recv(wop_v.at[4 * j + k], wop_slots[k])
            relays[k].start()

    def get_wop(first):
        for k in (first, first + 1):
            recv(wop_v.at[4 * (1 - j) + k], wop_relay[k])

    pl.when(ph > 0)(lambda: take_wop(0))
    pl.when(ph > 1)(lambda: take_wop(2))
    pl.when(ph > 0)(lambda: get_wop(0))
    pl.when(ph > 1)(lambda: get_wop(2))

    @pl.when(ph < 2)
    def _():
        x_load.wait()
        x_direct.wait_send()
        recv(x_v.at[theirs], x_slot)

    bl_slots = [next(slots) for _ in range(4)]
    bl_relay_slots = [next(slots) for _ in range(4)]
    bl_relays = [copy(bl_v.at[4 * j + h], bl_v.at[4 * j + h], bl_relay_slots[h], sibling) for h in range(4)]
    step = 512 if width % 512 == 0 else width

    def add_squares(n, rounded):
        wide = rounded.astype(jnp.float32)
        wide = wide * wide
        lanes = wide[:, :HEAD]
        for m in range(HEAD, step, HEAD):
            lanes = lanes + wide[:, m:m + HEAD]
        sq_v[...] = lanes if n == 0 else sq_v[...] + lanes


    @pl.when(ph > 0)
    def _():
        mine_head, their_head = 4 * j, 4 * (1 - j)
        def take(h):
            recv(bl_v.at[mine_head + h], bl_slots[h])
            bl_relays[h].start()

        def project_heads(first):
            heads = [mine_head + first, mine_head + first + 1, their_head + first, their_head + first + 1]
            lhs = jnp.concatenate([bl_v[head] for head in heads], axis=1)
            for n in range(0, width, step):
                rhs = jnp.concatenate([wop_v[head, :, n:n + step] for head in heads], axis=0)
                part = jnp.dot(lhs, rhs, preferred_element_type=jnp.float32)
                if first == 0:
                    acc[:, n:n + step] = part
                else:
                    total = x_v[:, n:n + step].astype(jnp.float32) + (acc[:, n:n + step] + part)
                    total = total.astype(jnp.bfloat16)
                    x_v[:, n:n + step] = total
                    add_squares(n, total)

        take(0)
        take(1)

        @pl.when(ph >= 2)
        def _():
            for k in range(4):
                recv(mine_at(k), x_prev_slots[k])
                x_relays[k].start()

        pl.when(ph == 1)(lambda: take_wop(2))
        recv(bl_v.at[their_head], bl_relay_slots[0])
        recv(bl_v.at[their_head + 1], bl_relay_slots[1])
        take(2)
        project_heads(0)
        take(3)
        pl.when(ph == 1)(lambda: get_wop(2))

        recv(bl_v.at[their_head + 2], bl_relay_slots[2])
        recv(bl_v.at[their_head + 3], bl_relay_slots[3])

        @pl.when(ph >= 2)
        def _():
            for k in range(4):
                recv(theirs_at(k), x_relay_slots[k])
            for k in range(4):
                x_relays[k].wait_send()

        project_heads(2)

    @pl.when(is_first)
    def _():
        for n in range(0, width, step):
            add_squares(n, x_v[:, n:n + step])

    square = jnp.sum(sq_v[...], axis=1, keepdims=True)
    scale_rows = lax.rsqrt(square * (1.0 / width) + 1e-05)

    stream = x_v[...]

    def project(weights):
        return (jnp.dot(stream, weights, preferred_element_type=jnp.float32) * scale_rows).astype(jnp.bfloat16)

    def own_blocks(kind, h, first, count):
        return kv_v.at[h, kind, pl.ds((3 + first) * BLK, count * BLK), :]

    def begin(when, chosen):
        @pl.when(when)
        def _():
            for made in chosen:
                made.start()

        pending.extend((made, when) for made in chosen)

    def ahead(kind, heads):
        return [
            copy(own_blocks(kind, h, 1, 1), kv_v.at[h, kind, pl.ds(0, BLK), :], halo_slots[h][2 * kind + 1], next2)
            for h in heads
        ]

    def start_keys(heads):
        begin(has_next1, [
            copy(own_blocks(0, h, 0, 2), kv_v.at[h, 0, pl.ds(BLK, 2 * BLK), :], halo_slots[h][0], next1) for h in heads
        ])
        begin(has_next2 & high, ahead(0, heads))

    def start_values():
        direct, around = [], []
        for h in range(4):
            for b, slot in enumerate((halo_slots[h][2], late_slots[h])):
                direct.append(copy(own_blocks(1, h, b, 1), kv_v.at[h, 1, pl.ds((b + 1) * BLK, BLK), :], slot, next1))
                around.append(
                    copy(own_blocks(1, h, b, 1), rel_v.at[h, pl.ds(b * BLK, BLK), :], rel_slots[h][b], helper_of(p))
                )
        begin(has_next1 & high, around[2:] + direct[:2])
        begin(has_next1 & low & jnp.logical_not(is_first), around)
        begin(has_next1 & is_first, direct)
        begin(has_next2 & low, [
            copy(own_blocks(1, h, 1, 1), far_v.at[h], far_slots[h], far_chip) for h in range(4)
        ])
        begin(has_next2 & high, ahead(1, (0,)))

    for kind in (0, 1):
        made = project(jnp.concatenate([wkv_v[kind], wkv_v[2 + kind]], axis=1))
        for h in range(4):
            kv_v[h, kind, 3 * BLK:5 * BLK, :] = made[:, h * HEAD:(h + 1) * HEAD]
        if kind == 0:
            start_keys((0,))
    start_values()
    start_keys((1, 2, 3))
    made = project(jnp.concatenate([wq_v[0], wq_v[1]], axis=1))
    for h in range(4):
        q_v[h] = made[:, h * HEAD:(h + 1) * HEAD]

    bls_slots = [next(slots) for _ in range(4)]
    factor = math.log2(math.e) / math.sqrt(HEAD)

    def scored(h, i, keys, first):
        query = q_v[h, i * BLK:(i + 1) * BLK, :]
        scores = lax.dot_general(query, keys, (((1,), (1,)), ((), ())), preferred_element_type=jnp.float32)
        return scores * factor + bias_v[i, :, first:first + keys.shape[0]]

    def mix(weights, values):
        return jnp.dot(weights.astype(jnp.bfloat16), values, preferred_element_type=jnp.float32)

    near = ((0, 3 * BLK, 4 * BLK, 3 * BLK), (1, 3 * BLK, 5 * BLK, 2 * BLK))
    far = ((0, 0, 3 * BLK, 0), (1, BLK, 3 * BLK, 0))
    for h in range(4):
        scores = [scored(h, i, kv_v[h, 0, lo:hi, :], first) for i, lo, hi, first in near]
        tops = [jnp.max(part, axis=1, keepdims=True) for part in scores]
        weights = [jnp.exp2(part - top) for part, top in zip(scores, tops)]
        sums = [jnp.sum(part, axis=1, keepdims=True) for part in weights]
        for (i, lo, hi, _), part, top, total in zip(near, weights, tops, sums):
            rows = slice(i * BLK, (i + 1) * BLK)
            mix_v[h, rows, :] = mix(part, kv_v[h, 1, lo:hi, :])
            top_v[h, rows, :] = jnp.broadcast_to(top, (BLK, HEAD))
            sum_v[h, rows, :] = jnp.broadcast_to(total, (BLK, HEAD))

    for h in range(4):
        run(has_last1 & low, lambda h=h: recv(kv_v.at[h, 0, pl.ds(BLK, 2 * BLK), :], halo_slots[h][0]))
        send(kv_v.at[h, 0, pl.ds(2 * BLK, BLK), :], kv_v.at[h, 0, pl.ds(0, BLK), :], halo_slots[h][1], next1,
             low & has_last1 & has_next1)
    for h in range(4):
        run(has_last1 & high, lambda h=h: recv(kv_v.at[h, 0, pl.ds(BLK, 2 * BLK), :], halo_slots[h][0]))
        run(has_last1, lambda h=h: recv(kv_v.at[h, 1, pl.ds(BLK, BLK), :], halo_slots[h][2]))
        run(has_last1, lambda h=h: recv(kv_v.at[h, 1, pl.ds(2 * BLK, BLK), :], late_slots[h]))
        for kind in range(2):
            run(has_last2, lambda h=h, kind=kind: recv(kv_v.at[h, kind, pl.ds(0, BLK), :], halo_slots[h][2 * kind + 1]))
        scores = [scored(h, i, kv_v[h, 0, lo:hi, :], first) for i, lo, hi, first in far]
        before = [top_v[h, i * BLK:(i + 1) * BLK, :] for i in range(2)]
        tops = [jnp.maximum(jnp.max(part, axis=1, keepdims=True), old) for part, old in zip(scores, before)]
        weights = [
            jnp.exp2(part - jnp.concatenate([top] * (part.shape[1] // HEAD), axis=1)) for part, top in zip(scores, tops)
        ]
        sums = [jnp.sum(part, axis=1, keepdims=True) for part in weights]
        mixed = [mix(part, kv_v[h, 1, lo:hi, :]) for part, (_, lo, hi, _) in zip(weights, far)]
        for i in range(2):
            rows = slice(i * BLK, (i + 1) * BLK)
            shrink = jnp.exp2(before[i] - tops[i])
            total = sum_v[h, rows, :] * shrink + sums[i]
            blo_v[h, rows, :] = ((mix_v[h, rows, :] * shrink + mixed[i]) / total).astype(jnp.bfloat16)
        blended_last = copy(blo_v.at[h], bl_v.at[4 * j + h], bl_slots[h], ph_next)
        pl.when(ph + 1 < phases)(blended_last.start)
        if h < 3:
            pending.append((blended_last, ph + 1 < phases))
        send(blo_v.at[h, theirs, :], bls_v.at[h], bls_slots[h], sibling)

    pl.when(goes_late)(lambda: go(ph + RING - 1))

    for h in range(4):
        recv(bls_v.at[h], bls_slots[h])
    own = jnp.concatenate([blo_v[h, mine, :] for h in range(4)], axis=1)
    other = jnp.concatenate([bls_v[h] for h in range(4)], axis=1)
    for n in range(0, width, step):
        first = wo_v[pl.ds(4 * j, 4), :, n:n + step].reshape(4 * HEAD, step)
        second = wo_v[pl.ds(4 * (1 - j), 4), :, n:n + step].reshape(4 * HEAD, step)
        update = jnp.dot(own, first, preferred_element_type=jnp.float32)
        update = update + jnp.dot(other, second, preferred_element_type=jnp.float32)
        out_ref[:, n:n + step] = (x_v[mine, n:n + step].astype(jnp.float32) + update).astype(jnp.bfloat16)
    pl.when(ph + 1 < phases)(blended_last.wait_send)
    for k in range(4):
        send(out_ref.at[:, pl.ds(k * piece, piece)], mine_at(k), x_prev_slots[k], ph_next2, res_out)

    pl.when(late_help)(help_halo)
    for made, when in pending + rel_copies + far_copies:
        if when is None:
            made.wait_send()
        else:
            pl.when(when)(made.wait_send)

    @pl.when(ph > 0)
    def _():
        for made in relays + bl_relays:
            made.wait_send()


def solution(mesh):
    phases, devices = mesh.shape["phase"], mesh.shape["ctx"]
    chips = devices // 2

    def local(inputs, segment_ids, w_query, w_keyval, w_out):
        width = inputs.shape[2]
        rows_dev = w_keyval.shape[1]
        seg = jnp.broadcast_to(segment_ids.astype(jnp.float32), (8, BLK))
        any_space = pl.BlockSpec(memory_space=pl.ANY)
        n_slots = 144
        made = pl.pallas_call(
            functools.partial(kernel, phases, chips),
            out_shape=jax.ShapeDtypeStruct((BLK, width), jnp.bfloat16),
            in_specs=[any_space] * 5,
            out_specs=pl.BlockSpec(memory_space=pltpu.VMEM),
            scratch_shapes=[
                pltpu.VMEM((2 * BLK, width), jnp.bfloat16),
                pltpu.VMEM((2 * BLK, width), jnp.float32),
                pltpu.VMEM((2, width, 2 * HEAD), jnp.bfloat16),
                pltpu.VMEM((4, width, 2 * HEAD), jnp.bfloat16),
                pltpu.VMEM((8, HEAD, width), jnp.bfloat16),
                pltpu.VMEM((8, HEAD, width), jnp.bfloat16),
                pltpu.VMEM((4, 2 * BLK, HEAD), jnp.bfloat16),
                pltpu.VMEM((4, 2, 5 * BLK, HEAD), jnp.bfloat16),
                pltpu.VMEM((8, 2 * BLK, HEAD), jnp.bfloat16),
                pltpu.VMEM((4, 2 * BLK, HEAD), jnp.bfloat16),
                pltpu.VMEM((4, BLK, HEAD), jnp.bfloat16),
                pltpu.VMEM((5, 8, BLK), jnp.float32),
                pltpu.VMEM((2, BLK, 4 * BLK), jnp.float32),
                pltpu.VMEM((4, 2 * BLK, HEAD), jnp.bfloat16),
                pltpu.VMEM((4, BLK, HEAD), jnp.bfloat16),
                pltpu.VMEM((2 * BLK, HEAD), jnp.float32),
                pltpu.VMEM((4, 2 * BLK, HEAD), jnp.float32),
                pltpu.VMEM((4, 2 * BLK, HEAD), jnp.float32),
                pltpu.VMEM((4, 2 * BLK, HEAD), jnp.float32),
                pltpu.SemaphoreType.DMA((n_slots,)),
                pltpu.SemaphoreType.DMA((n_slots,)),
                pltpu.SemaphoreType.DMA((16,)),
                pltpu.SemaphoreType.REGULAR,
            ],
            compiler_params=pltpu.CompilerParams(
                collective_id=0, has_side_effects=True, vmem_limit_bytes=56 * 1024 * 1024
            ),
        )(
            inputs.reshape(BLK, width), seg, w_query.reshape(width, -1),
            w_keyval.reshape(rows_dev, -1), w_out.reshape(8, HEAD, width),
        )
        return made.reshape(1, 1, BLK, width)

    placed = (
        P(None, "ctx", None),
        P(None, "ctx"),
        P("phase", None, None),
        P("phase", "ctx", None),
        P("phase", None, None),
    )
    return jax.shard_map(
        local, mesh=mesh, in_specs=placed, out_specs=P("phase", None, "ctx", None), check_vma=False
    )
```

```python
import functools
import math

import jax
import jax.numpy as jnp
from jax import lax
from jax.experimental import pallas as pl
from jax.experimental.pallas import tpu as pltpu
from jax.sharding import PartitionSpec as P

MESH = pl.DeviceIdType.MESH
HEAD = 128
BLK = 128
RING = 4


def kernel(
    phases, chips, x_in, seg_in, wq_in, wkv_in, wo_in, out_ref,
    x_v, acc, wq_v, wkv_v, wo_v, wop_v, q_v, kv_v, bl_v, blo_v, bls_v, seg_v, bias_v, rel_v, far_v, via_v, sq_v, mix_v, top_v, sum_v,
    ssem, rsem, lsem, go_sem,
):
    width = x_v.shape[1]
    rows_dev = wkv_in.shape[0]
    rows_chip = 2 * rows_dev
    ph = lax.axis_index("phase")
    c = lax.axis_index("ctx")
    p = c // 2
    j = c % 2
    y = p // RING
    z = p % RING
    sib = c + 1 - 2 * j

    def at(phase, chip):
        return {"phase": phase, "ctx": chip * 2 + j}

    sibling = {"phase": ph, "ctx": sib}

    def chip_at(dy, dz):
        return ((y + dy + RING) % RING) * RING + (z + dz + RING) % RING

    y_next, y_prev = at(ph, chip_at(1, 0)), at(ph, chip_at(-1, 0))
    z_next, z_prev = at(ph, chip_at(0, 1)), at(ph, chip_at(0, -1))
    next1, next2 = at(ph, jnp.minimum(p + 1, chips - 1)), at(ph, jnp.minimum(p + 2, chips - 1))
    last1, last2 = at(ph, jnp.maximum(p - 1, 0)), at(ph, jnp.maximum(p - 2, 0))
    ph_next, ph_prev = at(jnp.minimum(ph + 1, phases - 1), p), at(jnp.maximum(ph - 1, 0), p)
    goer = jnp.where(ph < RING + 2, jnp.maximum(ph - RING + 1, 0), ph - RING)
    has_next1, has_next2 = p + 1 < chips, p + 2 < chips
    has_last1, has_last2 = p >= 1, p >= 2
    is_first, is_last = ph == 0, ph == phases - 1
    has_under = ph >= RING
    goes_late, goes_early = (ph == 1) | (ph == 2), (ph == 2) | (ph == 3)
    early_help, late_help = ph == 2 * RING - 1, (ph % RING < RING - 1)
    has_helper, has_helped = ph > 0, ph != RING - 1
    helper = jnp.where(ph == RING, 2 * RING - 1, jnp.maximum(ph - 1, 0))
    helped = jnp.where(early_help, RING, jnp.minimum(ph + 1, phases - 1))
    row_end = z == RING - 1
    helper_chip = jnp.where(row_end, jnp.minimum(p + RING, chips - 1), p)
    helped_chip = jnp.where(row_end, jnp.maximum(p - RING, 0), p)
    helped_to1, helped_to2 = jnp.minimum(helped_chip + 1, chips - 1), jnp.minimum(helped_chip + 2, chips - 1)
    has_helped = has_helped & (jnp.logical_not(row_end) | (p >= RING))
    helped1, helped2 = has_helped & (helped_chip + 1 < chips), has_helped & (helped_chip + 2 < chips)

    def helper_of(chip):
        chip = jnp.maximum(chip, 0)
        return at(helper, jnp.where(chip % RING == RING - 1, jnp.minimum(chip + RING, chips - 1), chip))

    res_out, res_in = ph + 2 < phases, ph >= 2
    ph_next2, ph_prev2 = at(jnp.minimum(ph + 2, phases - 1), p), at(jnp.maximum(ph - 2, 0), p)
    low, high = ph < RING, ph >= RING
    def far_of(chip):
        chip = jnp.clip(chip, 0, chips - 1)
        crossing = chip % RING >= 2
        row = jnp.minimum(chip // RING + jnp.where(crossing, 1, 0), RING - 1)
        return at(jnp.minimum(ph + RING, phases - 1), row * RING + (chip % RING + RING - 1) % RING)

    far_chip, far_back = far_of(p), far_of(p - 2)
    far_z = (z + 1) % RING
    far_row = y - jnp.where(far_z >= 2, 1, 0)
    far_from, far_phase = jnp.maximum(far_row, 0) * RING + far_z, jnp.maximum(ph - RING, 0)
    far_to = jnp.minimum(far_from + 2, chips - 1)
    does_far = high & (far_row >= 0) & (far_from + 2 < chips)
    turn_out, turn_in = ph == RING - 1, ph == RING

    barrier = pltpu.get_barrier_semaphore()
    for device in (sibling, y_next, y_prev, z_next, z_prev):
        pl.semaphore_signal(barrier, inc=1, device_id=device, device_id_type=MESH)
    count = jnp.int32(5)
    for device, there in (
        (next1, has_next1), (next2, has_next2), (last1, has_last1), (last2, has_last2),
        (ph_next, ph + 1 < phases), (ph_prev, ph > 0), (at(goer, p), has_under), (at(ph + RING - 1, p), goes_late), (at(jnp.minimum(ph + RING, phases - 1), p), goes_early),
        (far_chip, low & has_next2), (far_back, low & has_last2),
        (at(far_phase, far_from), does_far), (at(far_phase, far_to), does_far),
        (helper_of(p), has_helper & has_next1), (at(helped, helped_chip), helped1),
        (at(helped, helped_to1), helped1), (at(helped, helped_to2), helped2),
        (helper_of(p - 1), has_helper & has_last1), (helper_of(p - 2), has_helper & has_last2),
        (ph_next2, res_out), (ph_prev2, res_in), (at(RING - 1, p), is_first), (at(0, p), turn_out),
        (at(jnp.minimum(ph + 1, phases - 1), chip_at(0, -1)), turn_out),
        (at(jnp.maximum(ph - 1, 0), chip_at(0, 1)), turn_in),
    ):
        @pl.when(there)
        def _(device=device):
            pl.semaphore_signal(barrier, inc=1, device_id=device, device_id_type=MESH)

        count = count + there.astype(jnp.int32)
    pl.semaphore_wait(barrier, count)

    pending = []
    slots = iter(range(ssem.shape[0]))

    def copy(src, dst, slot, device):
        return pltpu.make_async_remote_copy(
            src_ref=src, dst_ref=dst, send_sem=ssem.at[slot], recv_sem=rsem.at[slot],
            device_id=device, device_id_type=MESH,
        )

    def send(src, dst, slot, device, when=None):
        made = copy(src, dst, slot, device)
        if when is None:
            made.start()
        else:
            pl.when(when)(made.start)
        pending.append((made, when))
        return made

    def recv(dst, slot):
        copy(dst, dst, slot, sibling).wait_recv()

    def run(when, body):
        pl.when(when)(body)

    local = []

    def load(src, dst):
        made = pltpu.make_async_copy(src, dst, lsem.at[len(local)])
        made.start()
        local.append(made)
        return made

    def columns(core, tile):
        start = core * 4 * HEAD + (tile // 2) * 2 * HEAD + (tile % 2) * 8 * HEAD
        return pl.ds(pl.multiple_of(start, 2 * HEAD), 2 * HEAD)

    own_rows = pl.ds(pl.multiple_of(c * rows_dev, rows_dev), rows_dev)
    shard_loads = [load(wkv_in.at[:, columns(j, t)], wkv_v.at[t, own_rows, :]) for t in range(4)]
    seg_v[3 + j] = jnp.broadcast_to(seg_in[...].astype(jnp.float32), seg_v.shape[1:])
    mine = pl.ds(pl.multiple_of(j * BLK, BLK), BLK)
    theirs = pl.ds(pl.multiple_of((1 - j) * BLK, BLK), BLK)
    wq_loads = [
        load(wq_in.at[:, pl.ds(pl.multiple_of(j * 4 * HEAD + t * 2 * HEAD, 2 * HEAD), 2 * HEAD)], wq_v.at[t])
        for t in range(2)
    ]
    wo_load = load(wo_in, wo_v)

    halo_slots = [[next(slots) for _ in range(4)] for _ in range(4)]
    rel_slots = [[next(slots), next(slots)] for _ in range(4)]
    late_slots = [next(slots) for _ in range(4)]
    far_slots = [next(slots) for _ in range(4)]
    helped_high = helped >= RING
    rel_copies = []
    for h in range(4):
        needed = helped1 & (True if h > 0 else jnp.logical_not(helped_high))
        for b, slot in enumerate((halo_slots[h][2], late_slots[h])):
            rel_copies.append((copy(rel_v.at[h, pl.ds(b * BLK, BLK), :], kv_v.at[h, 1, pl.ds((b + 1) * BLK, BLK), :],
                                    slot, at(helped, helped_to1)), needed))
    for h in range(1, 4):
        rel_copies.append((copy(rel_v.at[h, pl.ds(BLK, BLK), :], kv_v.at[h, 1, pl.ds(0, BLK), :], halo_slots[h][3],
                                at(helped, helped_to2)), helped2 & helped_high))
    far_copies = [
        (copy(far_v.at[h], kv_v.at[h, 1, pl.ds(0, BLK), :], halo_slots[h][3], at(far_phase, far_to)), does_far)
        for h in range(4)
    ]

    def help_halo():
        for h in range(4):
            @pl.when(rel_copies[2 * h][1])
            def _(h=h):
                for b in range(2):
                    recv(rel_v.at[h, pl.ds(b * BLK, BLK), :], rel_slots[h][b])
                    rel_copies[2 * h + b][0].start()

            if h > 0:
                pl.when(rel_copies[h + 7][1])(rel_copies[h + 7][0].start)

    def help_far():
        for h in range(4):
            recv(far_v.at[h], far_slots[h])
            far_copies[h][0].start()

    sib_rows = pl.ds(pl.multiple_of(sib * rows_dev, rows_dev), rows_dev)
    shard_slots = [next(slots) for _ in range(4)]
    seg_slots = [next(slots) for _ in range(3)]

    for t in range(4):
        send(wkv_in.at[:, columns(1 - j, t)], wkv_v.at[t, own_rows, :], shard_slots[t], sibling)
    send(seg_v.at[3 + j], seg_v.at[3 + j], seg_slots[0], sibling)

    wop_slots = [next(slots) for _ in range(4)]

    def send_wop(when, devices):
        for k in range(4):
            send(wo_in.at[4 * j + k], wop_v.at[4 * j + k], wop_slots[k], devices[k // 2],
                 when & jnp.logical_not(is_first) if k == 3 else when)

    via_slots = [next(slots), next(slots)]
    via_mid = copy(via_v, via_v, via_slots[1], at(2, p))
    via_end = copy(via_v, wop_v.at[4 * j + 3], wop_slots[3], at(1, p))

    def pass_via(slot, made):
        recv(via_v, slot)
        made.start()

    send(wo_in.at[4 * j + 3], via_v, via_slots[0], at(RING - 1, p), is_first)
    send_wop((ph + 1 < phases) & jnp.logical_not(turn_out), (ph_next, ph_next))
    x_slot = next(slots)
    x_prev_slots = [next(slots) for _ in range(4)]
    x_relay_slots = [next(slots) for _ in range(4)]
    x_load = pltpu.make_async_copy(x_in, x_v.at[mine], lsem.at[len(local)])
    x_direct = copy(x_in, x_v.at[mine], x_slot, sibling)

    @pl.when(ph < 2)
    def _():
        x_load.start()
        x_direct.start()

    for made in shard_loads:
        made.wait()
    for t in range(4):
        recv(wkv_v.at[t, sib_rows, :], shard_slots[t])

    def slab(chip, first, count_):
        return wkv_v.at[pl.ds(first, count_), pl.ds(pl.multiple_of(chip * rows_chip, rows_chip), rows_chip), :]

    sets = []
    for s in range(2):
        sets.append(dict(
            tile=2 * s,
            prim=(y_next, y_prev) if s == 0 else (z_next, z_prev),
            sec=(z_next, z_prev) if s == 0 else (y_next, y_prev),
            chip=(lambda a, b: chip_at(a, b)) if s == 0 else (lambda a, b: chip_at(b, a)),
            pslot=[next(slots) for _ in range(4)],
            sslot={dp: [next(slots) for _ in range(4)] for dp in (0, -1, 1, 2)},
        ))

    def ring_send(g, ring, slot, dp):
        piece = slab(g["chip"](dp, 0), g["tile"], 2)
        send(piece, piece, slot[0], ring[0])
        send(piece, piece, slot[1], ring[1])

    def ring_forward(g, ring, slot, before, after):
        piece = slab(before, g["tile"], 2)
        recv(piece, slot[0])
        half = slab(before, g["tile"], 1)
        send(half, half, slot[2], ring[0])
        piece = slab(after, g["tile"], 2)
        recv(piece, slot[1])
        half = slab(after, g["tile"] + 1, 1)
        send(half, half, slot[3], ring[1])

    def ring_end(g, slot, far):
        recv(slab(far, g["tile"], 1), slot[2])
        recv(slab(far, g["tile"] + 1, 1), slot[3])

    recv(seg_v.at[4 - j], seg_slots[0])
    send(seg_v.at[pl.ds(3, 2)], seg_v.at[pl.ds(1, 2)], seg_slots[1], next1, has_next1)
    send(seg_v.at[4], seg_v.at[0], seg_slots[2], next2, has_next2)

    @pl.when(jnp.logical_not(has_last1))
    def _():
        seg_v[1:3] = jnp.full((2,) + seg_v.shape[1:], -1.0, jnp.float32)
        kv_v[:, :, BLK:3 * BLK, :] = jnp.zeros((4, 2, 2 * BLK, HEAD), jnp.bfloat16)

    @pl.when(jnp.logical_not(has_last2))
    def _():
        seg_v[0] = jnp.full(seg_v.shape[1:], -1.0, jnp.float32)
        kv_v[:, :, 0:BLK, :] = jnp.zeros((4, 2, BLK, HEAD), jnp.bfloat16)

    pl.when(does_far & (ph < RING + 2))(help_far)
    pl.when(has_under)(lambda: pl.semaphore_wait(go_sem, 1))
    for g in sets:
        ring_send(g, g["prim"], g["pslot"], 0)
        ring_send(g, g["sec"], g["sslot"][0], 0)
    run(has_last1, lambda: recv(seg_v.at[pl.ds(1, 2)], seg_slots[1]))
    run(has_last2, lambda: recv(seg_v.at[0], seg_slots[2]))

    row_id = lax.broadcasted_iota(jnp.int32, (BLK, BLK), 0)
    col_id = lax.broadcasted_iota(jnp.int32, (BLK, BLK), 1)
    causal = col_id <= row_id
    for i in range(2):
        asking = jnp.transpose(jnp.broadcast_to(seg_v[3 + i, 0:1, :], (BLK, BLK)))
        for b in range(4):
            asked = jnp.broadcast_to(seg_v[i + b, 0:1, :], (BLK, BLK))
            ok = asking == asked
            if b == 3:
                ok = ok & causal
            bias_v[i, :, b * BLK:(b + 1) * BLK] = jnp.where(ok, 0.0, -1e30).astype(jnp.float32)

    for g in sets:
        ring_forward(g, g["prim"], g["pslot"], g["chip"](-1, 0), g["chip"](1, 0))
        ring_send(g, g["sec"], g["sslot"][-1], -1)
        ring_send(g, g["sec"], g["sslot"][1], 1)
    for g in sets:
        ring_forward(g, g["sec"], g["sslot"][0], g["chip"](0, -1), g["chip"](0, 1))
    pl.when(turn_out)(lambda: pass_via(via_slots[0], via_mid))
    for g in sets:
        ring_end(g, g["pslot"], g["chip"](2, 0))
        ring_send(g, g["sec"], g["sslot"][2], 2)
    for dp in (-1, 1, 2):
        for g in sets:
            ring_forward(g, g["sec"], g["sslot"][dp], g["chip"](dp, -1), g["chip"](dp, 1))

    pl.when(ph == 2)(lambda: pass_via(via_slots[1], via_end))
    for dp in (0, -1, 1, 2):
        for g in sets:
            ring_end(g, g["sslot"][dp], g["chip"](dp, 2))
    for made in wq_loads:
        made.wait()
    wo_load.wait()

    def go(phase):
        pl.semaphore_signal(go_sem, inc=1, device_id=at(jnp.minimum(phase, phases - 1), p), device_id_type=MESH)

    piece = width // 4

    def mine_at(k):
        return x_v.at[mine, pl.ds(k * piece, piece)]

    def theirs_at(k):
        return x_v.at[theirs, pl.ds(k * piece, piece)]

    pl.when(goes_early)(lambda: go(ph + RING))
    pl.when(does_far & (ph >= RING + 2))(help_far)
    pl.when(early_help)(help_halo)
    send_wop(turn_out, (ph_next, at(jnp.minimum(ph + 1, phases - 1), chip_at(0, -1))))

    wop_relay = [next(slots) for _ in range(4)]
    relays = []
    for k in range(4):
        relays.append(copy(wop_v.at[4 * j + k], wop_v.at[4 * j + k], wop_relay[k], sibling))
    x_relays = [copy(mine_at(k), mine_at(k), x_relay_slots[k], sibling) for k in range(4)]

    def take_wop(first):
        for k in (first, first + 1):
            recv(wop_v.at[4 * j + k], wop_slots[k])
            relays[k].start()

    def get_wop(first):
        for k in (first, first + 1):
            recv(wop_v.at[4 * (1 - j) + k], wop_relay[k])

    pl.when(ph > 0)(lambda: take_wop(0))
    pl.when(ph > 1)(lambda: take_wop(2))
    pl.when(ph > 0)(lambda: get_wop(0))
    pl.when(ph > 1)(lambda: get_wop(2))

    @pl.when(ph < 2)
    def _():
        x_load.wait()
        x_direct.wait_send()
        recv(x_v.at[theirs], x_slot)

    bl_slots = [next(slots) for _ in range(4)]
    bl_relay_slots = [next(slots) for _ in range(4)]
    bl_relays = [copy(bl_v.at[4 * j + h], bl_v.at[4 * j + h], bl_relay_slots[h], sibling) for h in range(4)]
    step = 512 if width % 512 == 0 else width

    def add_squares(n, rounded):
        wide = rounded.astype(jnp.float32)
        wide = wide * wide
        lanes = wide[:, :HEAD]
        for m in range(HEAD, step, HEAD):
            lanes = lanes + wide[:, m:m + HEAD]
        sq_v[...] = lanes if n == 0 else sq_v[...] + lanes


    @pl.when(ph > 0)
    def _():
        mine_head, their_head = 4 * j, 4 * (1 - j)
        def take(h):
            recv(bl_v.at[mine_head + h], bl_slots[h])
            bl_relays[h].start()

        def project_heads(first):
            heads = [mine_head + first, mine_head + first + 1, their_head + first, their_head + first + 1]
            lhs = jnp.concatenate([bl_v[head] for head in heads], axis=1)
            for n in range(0, width, step):
                rhs = jnp.concatenate([wop_v[head, :, n:n + step] for head in heads], axis=0)
                part = jnp.dot(lhs, rhs, preferred_element_type=jnp.float32)
                if first == 0:
                    acc[:, n:n + step] = part
                else:
                    total = x_v[:, n:n + step].astype(jnp.float32) + (acc[:, n:n + step] + part)
                    total = total.astype(jnp.bfloat16)
                    x_v[:, n:n + step] = total
                    add_squares(n, total)

        take(0)
        take(1)

        @pl.when(ph >= 2)
        def _():
            for k in range(4):
                recv(mine_at(k), x_prev_slots[k])
                x_relays[k].start()

        pl.when(ph == 1)(lambda: take_wop(2))
        recv(bl_v.at[their_head], bl_relay_slots[0])
        recv(bl_v.at[their_head + 1], bl_relay_slots[1])
        take(2)
        project_heads(0)
        take(3)
        pl.when(ph == 1)(lambda: get_wop(2))

        recv(bl_v.at[their_head + 2], bl_relay_slots[2])
        recv(bl_v.at[their_head + 3], bl_relay_slots[3])

        @pl.when(ph >= 2)
        def _():
            for k in range(4):
                recv(theirs_at(k), x_relay_slots[k])
            for k in range(4):
                x_relays[k].wait_send()

        project_heads(2)

    @pl.when(is_first)
    def _():
        for n in range(0, width, step):
            add_squares(n, x_v[:, n:n + step])

    square = jnp.sum(sq_v[...], axis=1, keepdims=True)
    scale_rows = lax.rsqrt(square * (1.0 / width) + 1e-05)

    stream = x_v[...]

    def project(weights):
        return (jnp.dot(stream, weights, preferred_element_type=jnp.float32) * scale_rows).astype(jnp.bfloat16)

    def own_blocks(kind, h, first, count):
        return kv_v.at[h, kind, pl.ds((3 + first) * BLK, count * BLK), :]

    def begin(when, chosen):
        @pl.when(when)
        def _():
            for made in chosen:
                made.start()

        pending.extend((made, when) for made in chosen)

    def ahead(kind, heads):
        return [
            copy(own_blocks(kind, h, 1, 1), kv_v.at[h, kind, pl.ds(0, BLK), :], halo_slots[h][2 * kind + 1], next2)
            for h in heads
        ]

    def start_keys(heads):
        begin(has_next1, [
            copy(own_blocks(0, h, 0, 2), kv_v.at[h, 0, pl.ds(BLK, 2 * BLK), :], halo_slots[h][0], next1) for h in heads
        ])
        begin(has_next2 & high, ahead(0, heads))

    def start_values():
        direct, around = [], []
        for h in range(4):
            for b, slot in enumerate((halo_slots[h][2], late_slots[h])):
                direct.append(copy(own_blocks(1, h, b, 1), kv_v.at[h, 1, pl.ds((b + 1) * BLK, BLK), :], slot, next1))
                around.append(
                    copy(own_blocks(1, h, b, 1), rel_v.at[h, pl.ds(b * BLK, BLK), :], rel_slots[h][b], helper_of(p))
                )
        begin(has_next1 & high, around[2:] + direct[:2])
        begin(has_next1 & low & jnp.logical_not(is_first), around)
        begin(has_next1 & is_first, direct)
        begin(has_next2 & low, [
            copy(own_blocks(1, h, 1, 1), far_v.at[h], far_slots[h], far_chip) for h in range(4)
        ])
        begin(has_next2 & high, ahead(1, (0,)))

    for kind in (0, 1):
        made = project(jnp.concatenate([wkv_v[kind], wkv_v[2 + kind]], axis=1))
        for h in range(4):
            kv_v[h, kind, 3 * BLK:5 * BLK, :] = made[:, h * HEAD:(h + 1) * HEAD]
        if kind == 0:
            start_keys((0,))
    start_values()
    start_keys((1, 2, 3))
    made = project(jnp.concatenate([wq_v[0], wq_v[1]], axis=1))
    for h in range(4):
        q_v[h] = made[:, h * HEAD:(h + 1) * HEAD]

    bls_slots = [next(slots) for _ in range(4)]
    factor = math.log2(math.e) / math.sqrt(HEAD)

    def scored(h, i, keys, first):
        query = q_v[h, i * BLK:(i + 1) * BLK, :]
        scores = lax.dot_general(query, keys, (((1,), (1,)), ((), ())), preferred_element_type=jnp.float32)
        return scores * factor + bias_v[i, :, first:first + keys.shape[0]]

    def mix(weights, values):
        return jnp.dot(weights.astype(jnp.bfloat16), values, preferred_element_type=jnp.float32)

    near = ((0, 3 * BLK, 4 * BLK, 3 * BLK), (1, 3 * BLK, 5 * BLK, 2 * BLK))
    far = ((0, 0, 3 * BLK, 0), (1, BLK, 3 * BLK, 0))
    for h in range(4):
        scores = [scored(h, i, kv_v[h, 0, lo:hi, :], first) for i, lo, hi, first in near]
        tops = [jnp.max(part, axis=1, keepdims=True) for part in scores]
        weights = [jnp.exp2(part - top) for part, top in zip(scores, tops)]
        sums = [jnp.sum(part, axis=1, keepdims=True) for part in weights]
        for (i, lo, hi, _), part, top, total in zip(near, weights, tops, sums):
            rows = slice(i * BLK, (i + 1) * BLK)
            mix_v[h, rows, :] = mix(part, kv_v[h, 1, lo:hi, :])
            top_v[h, rows, :] = jnp.broadcast_to(top, (BLK, HEAD))
            sum_v[h, rows, :] = jnp.broadcast_to(total, (BLK, HEAD))

    for h in range(4):
        run(has_last1 & low, lambda h=h: recv(kv_v.at[h, 0, pl.ds(BLK, 2 * BLK), :], halo_slots[h][0]))
        send(kv_v.at[h, 0, pl.ds(2 * BLK, BLK), :], kv_v.at[h, 0, pl.ds(0, BLK), :], halo_slots[h][1], next1,
             low & has_last1 & has_next1)
    for h in range(4):
        run(has_last1 & high, lambda h=h: recv(kv_v.at[h, 0, pl.ds(BLK, 2 * BLK), :], halo_slots[h][0]))
        run(has_last1, lambda h=h: recv(kv_v.at[h, 1, pl.ds(BLK, BLK), :], halo_slots[h][2]))
        run(has_last1, lambda h=h: recv(kv_v.at[h, 1, pl.ds(2 * BLK, BLK), :], late_slots[h]))
        for kind in range(2):
            run(has_last2, lambda h=h, kind=kind: recv(kv_v.at[h, kind, pl.ds(0, BLK), :], halo_slots[h][2 * kind + 1]))
        scores = [scored(h, i, kv_v[h, 0, lo:hi, :], first) for i, lo, hi, first in far]
        before = [top_v[h, i * BLK:(i + 1) * BLK, :] for i in range(2)]
        tops = [jnp.maximum(jnp.max(part, axis=1, keepdims=True), old) for part, old in zip(scores, before)]
        weights = [
            jnp.exp2(part - jnp.concatenate([top] * (part.shape[1] // HEAD), axis=1)) for part, top in zip(scores, tops)
        ]
        sums = [jnp.sum(part, axis=1, keepdims=True) for part in weights]
        mixed = [mix(part, kv_v[h, 1, lo:hi, :]) for part, (_, lo, hi, _) in zip(weights, far)]
        for i in range(2):
            rows = slice(i * BLK, (i + 1) * BLK)
            shrink = jnp.exp2(before[i] - tops[i])
            total = sum_v[h, rows, :] * shrink + sums[i]
            blo_v[h, rows, :] = ((mix_v[h, rows, :] * shrink + mixed[i]) / total).astype(jnp.bfloat16)
        blended_last = copy(blo_v.at[h], bl_v.at[4 * j + h], bl_slots[h], ph_next)
        pl.when(ph + 1 < phases)(blended_last.start)
        if h < 3:
            pending.append((blended_last, ph + 1 < phases))
        send(blo_v.at[h, theirs, :], bls_v.at[h], bls_slots[h], sibling)

    pl.when(goes_late)(lambda: go(ph + RING - 1))

    for h in range(4):
        recv(bls_v.at[h], bls_slots[h])
    own = jnp.concatenate([blo_v[h, mine, :] for h in range(4)], axis=1)
    other = jnp.concatenate([bls_v[h] for h in range(4)], axis=1)
    for n in range(0, width, step):
        first = wo_v[pl.ds(4 * j, 4), :, n:n + step].reshape(4 * HEAD, step)
        second = wo_v[pl.ds(4 * (1 - j), 4), :, n:n + step].reshape(4 * HEAD, step)
        update = jnp.dot(own, first, preferred_element_type=jnp.float32)
        update = update + jnp.dot(other, second, preferred_element_type=jnp.float32)
        out_ref[:, n:n + step] = (x_v[mine, n:n + step].astype(jnp.float32) + update).astype(jnp.bfloat16)
    pl.when(ph + 1 < phases)(blended_last.wait_send)
    for k in range(4):
        send(out_ref.at[:, pl.ds(k * piece, piece)], mine_at(k), x_prev_slots[k], ph_next2, res_out)

    pl.when(late_help)(help_halo)
    for made, when in pending + rel_copies + far_copies + [(via_mid, turn_out), (via_end, ph == 2)]:
        if when is None:
            made.wait_send()
        else:
            pl.when(when)(made.wait_send)

    @pl.when(ph > 0)
    def _():
        for made in relays + bl_relays:
            made.wait_send()


def solution(mesh):
    phases, devices = mesh.shape["phase"], mesh.shape["ctx"]
    chips = devices // 2

    def local(inputs, segment_ids, w_query, w_keyval, w_out):
        width = inputs.shape[2]
        rows_dev = w_keyval.shape[1]
        any_space = pl.BlockSpec(memory_space=pl.ANY)
        n_slots = 144
        made = pl.pallas_call(
            functools.partial(kernel, phases, chips),
            out_shape=jax.ShapeDtypeStruct((BLK, width), jnp.bfloat16),
            in_specs=[any_space, pl.BlockSpec(memory_space=pltpu.VMEM)] + [any_space] * 3,
            out_specs=pl.BlockSpec(memory_space=pltpu.VMEM),
            scratch_shapes=[
                pltpu.VMEM((2 * BLK, width), jnp.bfloat16),
                pltpu.VMEM((2 * BLK, width), jnp.float32),
                pltpu.VMEM((2, width, 2 * HEAD), jnp.bfloat16),
                pltpu.VMEM((4, width, 2 * HEAD), jnp.bfloat16),
                pltpu.VMEM((8, HEAD, width), jnp.bfloat16),
                pltpu.VMEM((8, HEAD, width), jnp.bfloat16),
                pltpu.VMEM((4, 2 * BLK, HEAD), jnp.bfloat16),
                pltpu.VMEM((4, 2, 5 * BLK, HEAD), jnp.bfloat16),
                pltpu.VMEM((8, 2 * BLK, HEAD), jnp.bfloat16),
                pltpu.VMEM((4, 2 * BLK, HEAD), jnp.bfloat16),
                pltpu.VMEM((4, BLK, HEAD), jnp.bfloat16),
                pltpu.VMEM((5, 8, BLK), jnp.float32),
                pltpu.VMEM((2, BLK, 4 * BLK), jnp.float32),
                pltpu.VMEM((4, 2 * BLK, HEAD), jnp.bfloat16),
                pltpu.VMEM((4, BLK, HEAD), jnp.bfloat16),
                pltpu.VMEM((HEAD, width), jnp.bfloat16),
                pltpu.VMEM((2 * BLK, HEAD), jnp.float32),
                pltpu.VMEM((4, 2 * BLK, HEAD), jnp.float32),
                pltpu.VMEM((4, 2 * BLK, HEAD), jnp.float32),
                pltpu.VMEM((4, 2 * BLK, HEAD), jnp.float32),
                pltpu.SemaphoreType.DMA((n_slots,)),
                pltpu.SemaphoreType.DMA((n_slots,)),
                pltpu.SemaphoreType.DMA((16,)),
                pltpu.SemaphoreType.REGULAR,
            ],
            compiler_params=pltpu.CompilerParams(
                collective_id=0, has_side_effects=True, vmem_limit_bytes=56 * 1024 * 1024
            ),
        )(
            inputs.reshape(BLK, width), segment_ids, w_query.reshape(width, -1),
            w_keyval.reshape(rows_dev, -1), w_out.reshape(8, HEAD, width),
        )
        return made.reshape(1, 1, BLK, width)

    placed = (
        P(None, "ctx", None),
        P(None, "ctx"),
        P("phase", None, None),
        P("phase", "ctx", None),
        P("phase", None, None),
    )
    return jax.shard_map(
        local, mesh=mesh, in_specs=placed, out_specs=P("phase", None, "ctx", None), check_vma=False
    )
```

```python
import functools
import math

import jax
import jax.numpy as jnp
from jax import lax
from jax.experimental import pallas as pl
from jax.experimental.pallas import tpu as pltpu
from jax.sharding import PartitionSpec as P

MESH = pl.DeviceIdType.MESH
HEAD = 128
BLK = 128
RING = 4


def kernel(
    phases, chips, x_in, seg_in, wq_in, wkv_in, wo_in, out_ref,
    x_v, acc, wq_v, wkv_v, wo_v, wop_v, q_v, kv_v, bl_v, blo_v, bls_v, seg_v, bias_v, rel_v, far_v, via_v, res_v, sq_v, mix_v, top_v, sum_v,
    ssem, rsem, lsem, go_sem,
):
    width = x_v.shape[1]
    rows_dev = wkv_in.shape[0]
    rows_chip = 2 * rows_dev
    ph = lax.axis_index("phase")
    c = lax.axis_index("ctx")
    p = c // 2
    j = c % 2
    y = p // RING
    z = p % RING
    sib = c + 1 - 2 * j

    def at(phase, chip):
        return {"phase": phase, "ctx": chip * 2 + j}

    sibling = {"phase": ph, "ctx": sib}

    def chip_at(dy, dz):
        return ((y + dy + RING) % RING) * RING + (z + dz + RING) % RING

    y_next, y_prev = at(ph, chip_at(1, 0)), at(ph, chip_at(-1, 0))
    z_next, z_prev = at(ph, chip_at(0, 1)), at(ph, chip_at(0, -1))
    next1, next2 = at(ph, jnp.minimum(p + 1, chips - 1)), at(ph, jnp.minimum(p + 2, chips - 1))
    last1, last2 = at(ph, jnp.maximum(p - 1, 0)), at(ph, jnp.maximum(p - 2, 0))
    ph_next, ph_prev = at(jnp.minimum(ph + 1, phases - 1), p), at(jnp.maximum(ph - 1, 0), p)
    goer = jnp.where(ph < RING + 2, jnp.maximum(ph - RING + 1, 0), ph - RING)
    has_next1, has_next2 = p + 1 < chips, p + 2 < chips
    has_last1, has_last2 = p >= 1, p >= 2
    is_first, is_last = ph == 0, ph == phases - 1
    has_under = ph >= RING
    goes_late, goes_early = (ph == 1) | (ph == 2), (ph == 2) | (ph == 3)
    early_help, late_help = ph == 2 * RING - 1, (ph % RING < RING - 1)
    has_helper, has_helped = ph > 0, ph != RING - 1
    helper = jnp.where(ph == RING, 2 * RING - 1, jnp.maximum(ph - 1, 0))
    helped = jnp.where(early_help, RING, jnp.minimum(ph + 1, phases - 1))
    row_end = z == RING - 1
    helper_chip = jnp.where(row_end, jnp.minimum(p + RING, chips - 1), p)
    helped_chip = jnp.where(row_end, jnp.maximum(p - RING, 0), p)
    helped_to1, helped_to2 = jnp.minimum(helped_chip + 1, chips - 1), jnp.minimum(helped_chip + 2, chips - 1)
    has_helped = has_helped & (jnp.logical_not(row_end) | (p >= RING))
    helped1, helped2 = has_helped & (helped_chip + 1 < chips), has_helped & (helped_chip + 2 < chips)

    def helper_of(chip):
        chip = jnp.maximum(chip, 0)
        return at(helper, jnp.where(chip % RING == RING - 1, jnp.minimum(chip + RING, chips - 1), chip))

    res_out, res_in = ph + 2 < phases, ph >= 2
    res_even = res_out & (ph % RING == 0)
    res_direct = res_out & (ph % RING != 0)
    res_via = jnp.minimum(ph + RING - 1, phases - 1)
    passes = ph % RING == RING - 1
    pass_from = jnp.maximum(ph - RING + 1, 0)
    pass_to = jnp.minimum(pass_from + 2, phases - 1)
    res_back = jnp.minimum(ph + 1, phases - 1)
    res_around = ph % RING == 2
    ph_next2, ph_prev2 = at(jnp.minimum(ph + 2, phases - 1), p), at(jnp.maximum(ph - 2, 0), p)
    low, high = ph < RING, ph >= RING
    def far_of(chip):
        chip = jnp.clip(chip, 0, chips - 1)
        crossing = chip % RING >= 2
        row = jnp.minimum(chip // RING + jnp.where(crossing, 1, 0), RING - 1)
        return at(jnp.minimum(ph + RING, phases - 1), row * RING + (chip % RING + RING - 1) % RING)

    far_chip, far_back = far_of(p), far_of(p - 2)
    far_z = (z + 1) % RING
    far_row = y - jnp.where(far_z >= 2, 1, 0)
    far_from, far_phase = jnp.maximum(far_row, 0) * RING + far_z, jnp.maximum(ph - RING, 0)
    far_to = jnp.minimum(far_from + 2, chips - 1)
    does_far = high & (far_row >= 0) & (far_from + 2 < chips)
    turn_out, turn_in = ph == RING - 1, ph == RING

    barrier = pltpu.get_barrier_semaphore()
    for device in (sibling, y_next, y_prev, z_next, z_prev):
        pl.semaphore_signal(barrier, inc=1, device_id=device, device_id_type=MESH)
    count = jnp.int32(5)
    for device, there in (
        (next1, has_next1), (next2, has_next2), (last1, has_last1), (last2, has_last2),
        (ph_next, ph + 1 < phases), (ph_prev, ph > 0), (at(goer, p), has_under), (at(ph + RING - 1, p), goes_late), (at(jnp.minimum(ph + RING, phases - 1), p), goes_early),
        (far_chip, low & has_next2), (far_back, low & has_last2),
        (at(far_phase, far_from), does_far), (at(far_phase, far_to), does_far),
        (helper_of(p), has_helper & has_next1), (at(helped, helped_chip), helped1),
        (at(helped, helped_to1), helped1), (at(helped, helped_to2), helped2),
        (helper_of(p - 1), has_helper & has_last1), (helper_of(p - 2), has_helper & has_last2),
        (ph_next2, res_direct), (ph_prev2, res_in & jnp.logical_not(res_around)),
        (at(res_via, p), res_even), (at(pass_from, p), passes), (at(pass_to, p), passes),
        (at(res_back, p), res_around), (at(RING - 1, p), is_first), (at(0, p), turn_out),
        (at(jnp.minimum(ph + 1, phases - 1), chip_at(0, -1)), turn_out),
        (at(jnp.maximum(ph - 1, 0), chip_at(0, 1)), turn_in),
    ):
        @pl.when(there)
        def _(device=device):
            pl.semaphore_signal(barrier, inc=1, device_id=device, device_id_type=MESH)

        count = count + there.astype(jnp.int32)
    pl.semaphore_wait(barrier, count)

    pending = []
    slots = iter(range(ssem.shape[0]))

    def copy(src, dst, slot, device):
        return pltpu.make_async_remote_copy(
            src_ref=src, dst_ref=dst, send_sem=ssem.at[slot], recv_sem=rsem.at[slot],
            device_id=device, device_id_type=MESH,
        )

    def send(src, dst, slot, device, when=None):
        made = copy(src, dst, slot, device)
        if when is None:
            made.start()
        else:
            pl.when(when)(made.start)
        pending.append((made, when))
        return made

    def recv(dst, slot):
        copy(dst, dst, slot, sibling).wait_recv()

    def run(when, body):
        pl.when(when)(body)

    local = []

    def load(src, dst):
        made = pltpu.make_async_copy(src, dst, lsem.at[len(local)])
        made.start()
        local.append(made)
        return made

    def columns(core, tile):
        start = core * 4 * HEAD + (tile // 2) * 2 * HEAD + (tile % 2) * 8 * HEAD
        return pl.ds(pl.multiple_of(start, 2 * HEAD), 2 * HEAD)

    own_rows = pl.ds(pl.multiple_of(c * rows_dev, rows_dev), rows_dev)
    shard_loads = [load(wkv_in.at[:, columns(j, t)], wkv_v.at[t, own_rows, :]) for t in range(4)]
    seg_v[3 + j] = jnp.broadcast_to(seg_in[...].astype(jnp.float32), seg_v.shape[1:])
    mine = pl.ds(pl.multiple_of(j * BLK, BLK), BLK)
    theirs = pl.ds(pl.multiple_of((1 - j) * BLK, BLK), BLK)
    wq_loads = [
        load(wq_in.at[:, pl.ds(pl.multiple_of(j * 4 * HEAD + t * 2 * HEAD, 2 * HEAD), 2 * HEAD)], wq_v.at[t])
        for t in range(2)
    ]
    wo_load = load(wo_in, wo_v)

    halo_slots = [[next(slots) for _ in range(4)] for _ in range(4)]
    rel_slots = [[next(slots), next(slots)] for _ in range(4)]
    late_slots = [next(slots) for _ in range(4)]
    far_slots = [next(slots) for _ in range(4)]
    helped_high = helped >= RING
    rel_copies = []
    for h in range(4):
        needed = helped1 & (True if h > 0 else jnp.logical_not(helped_high))
        for b, slot in enumerate((halo_slots[h][2], late_slots[h])):
            rel_copies.append((copy(rel_v.at[h, pl.ds(b * BLK, BLK), :], kv_v.at[h, 1, pl.ds((b + 1) * BLK, BLK), :],
                                    slot, at(helped, helped_to1)), needed))
    for h in range(1, 4):
        rel_copies.append((copy(rel_v.at[h, pl.ds(BLK, BLK), :], kv_v.at[h, 1, pl.ds(0, BLK), :], halo_slots[h][3],
                                at(helped, helped_to2)), helped2 & helped_high))
    far_copies = [
        (copy(far_v.at[h], kv_v.at[h, 1, pl.ds(0, BLK), :], halo_slots[h][3], at(far_phase, far_to)), does_far)
        for h in range(4)
    ]

    def help_halo():
        for h in range(4):
            @pl.when(rel_copies[2 * h][1])
            def _(h=h):
                for b in range(2):
                    recv(rel_v.at[h, pl.ds(b * BLK, BLK), :], rel_slots[h][b])
                    rel_copies[2 * h + b][0].start()

            if h > 0:
                pl.when(rel_copies[h + 7][1])(rel_copies[h + 7][0].start)

    def help_far():
        for h in range(4):
            recv(far_v.at[h], far_slots[h])
            far_copies[h][0].start()

    sib_rows = pl.ds(pl.multiple_of(sib * rows_dev, rows_dev), rows_dev)
    shard_slots = [next(slots) for _ in range(4)]
    seg_slots = [next(slots) for _ in range(3)]

    for t in range(4):
        send(wkv_in.at[:, columns(1 - j, t)], wkv_v.at[t, own_rows, :], shard_slots[t], sibling)
    send(seg_v.at[3 + j], seg_v.at[3 + j], seg_slots[0], sibling)

    wop_slots = [next(slots) for _ in range(4)]

    def send_wop(when, devices):
        for k in range(4):
            send(wo_in.at[4 * j + k], wop_v.at[4 * j + k], wop_slots[k], devices[k // 2],
                 when & jnp.logical_not(is_first) if k == 3 else when)

    via_slots = [next(slots), next(slots)]
    via_mid = copy(via_v, via_v, via_slots[1], at(2, p))
    via_end = copy(via_v, wop_v.at[4 * j + 3], wop_slots[3], at(1, p))

    def pass_via(slot, made):
        recv(via_v, slot)
        made.start()

    send(wo_in.at[4 * j + 3], via_v, via_slots[0], at(RING - 1, p), is_first)
    send_wop((ph + 1 < phases) & jnp.logical_not(turn_out), (ph_next, ph_next))
    x_slot = next(slots)
    x_prev_slots = [next(slots) for _ in range(4)]
    x_relay_slots = [next(slots) for _ in range(4)]
    res_slots = [next(slots) for _ in range(4)]
    x_load = pltpu.make_async_copy(x_in, x_v.at[mine], lsem.at[len(local)])
    x_direct = copy(x_in, x_v.at[mine], x_slot, sibling)

    @pl.when(ph < 2)
    def _():
        x_load.start()
        x_direct.start()

    for made in shard_loads:
        made.wait()
    for t in range(4):
        recv(wkv_v.at[t, sib_rows, :], shard_slots[t])

    def slab(chip, first, count_):
        return wkv_v.at[pl.ds(first, count_), pl.ds(pl.multiple_of(chip * rows_chip, rows_chip), rows_chip), :]

    sets = []
    for s in range(2):
        sets.append(dict(
            tile=2 * s,
            prim=(y_next, y_prev) if s == 0 else (z_next, z_prev),
            sec=(z_next, z_prev) if s == 0 else (y_next, y_prev),
            chip=(lambda a, b: chip_at(a, b)) if s == 0 else (lambda a, b: chip_at(b, a)),
            pslot=[next(slots) for _ in range(4)],
            sslot={dp: [next(slots) for _ in range(4)] for dp in (0, -1, 1, 2)},
        ))

    def ring_send(g, ring, slot, dp):
        piece = slab(g["chip"](dp, 0), g["tile"], 2)
        send(piece, piece, slot[0], ring[0])
        send(piece, piece, slot[1], ring[1])

    def ring_forward(g, ring, slot, before, after):
        piece = slab(before, g["tile"], 2)
        recv(piece, slot[0])
        half = slab(before, g["tile"], 1)
        send(half, half, slot[2], ring[0])
        piece = slab(after, g["tile"], 2)
        recv(piece, slot[1])
        half = slab(after, g["tile"] + 1, 1)
        send(half, half, slot[3], ring[1])

    def ring_end(g, slot, far):
        recv(slab(far, g["tile"], 1), slot[2])
        recv(slab(far, g["tile"] + 1, 1), slot[3])

    recv(seg_v.at[4 - j], seg_slots[0])
    send(seg_v.at[pl.ds(3, 2)], seg_v.at[pl.ds(1, 2)], seg_slots[1], next1, has_next1)
    send(seg_v.at[4], seg_v.at[0], seg_slots[2], next2, has_next2)

    @pl.when(jnp.logical_not(has_last1))
    def _():
        seg_v[1:3] = jnp.full((2,) + seg_v.shape[1:], -1.0, jnp.float32)
        kv_v[:, :, BLK:3 * BLK, :] = jnp.zeros((4, 2, 2 * BLK, HEAD), jnp.bfloat16)

    @pl.when(jnp.logical_not(has_last2))
    def _():
        seg_v[0] = jnp.full(seg_v.shape[1:], -1.0, jnp.float32)
        kv_v[:, :, 0:BLK, :] = jnp.zeros((4, 2, BLK, HEAD), jnp.bfloat16)

    pl.when(does_far & (ph < RING + 2))(help_far)
    pl.when(has_under)(lambda: pl.semaphore_wait(go_sem, 1))
    for g in sets:
        ring_send(g, g["prim"], g["pslot"], 0)
        ring_send(g, g["sec"], g["sslot"][0], 0)
    run(has_last1, lambda: recv(seg_v.at[pl.ds(1, 2)], seg_slots[1]))
    run(has_last2, lambda: recv(seg_v.at[0], seg_slots[2]))

    row_id = lax.broadcasted_iota(jnp.int32, (BLK, BLK), 0)
    col_id = lax.broadcasted_iota(jnp.int32, (BLK, BLK), 1)
    causal = col_id <= row_id
    for i in range(2):
        asking = jnp.transpose(jnp.broadcast_to(seg_v[3 + i, 0:1, :], (BLK, BLK)))
        for b in range(4):
            asked = jnp.broadcast_to(seg_v[i + b, 0:1, :], (BLK, BLK))
            ok = asking == asked
            if b == 3:
                ok = ok & causal
            bias_v[i, :, b * BLK:(b + 1) * BLK] = jnp.where(ok, 0.0, -1e30).astype(jnp.float32)

    for g in sets:
        ring_forward(g, g["prim"], g["pslot"], g["chip"](-1, 0), g["chip"](1, 0))
        ring_send(g, g["sec"], g["sslot"][-1], -1)
        ring_send(g, g["sec"], g["sslot"][1], 1)
    for g in sets:
        ring_forward(g, g["sec"], g["sslot"][0], g["chip"](0, -1), g["chip"](0, 1))
    pl.when(turn_out)(lambda: pass_via(via_slots[0], via_mid))
    for g in sets:
        ring_end(g, g["pslot"], g["chip"](2, 0))
        ring_send(g, g["sec"], g["sslot"][2], 2)
    for dp in (-1, 1, 2):
        for g in sets:
            ring_forward(g, g["sec"], g["sslot"][dp], g["chip"](dp, -1), g["chip"](dp, 1))

    pl.when(ph == 2)(lambda: pass_via(via_slots[1], via_end))
    for dp in (0, -1, 1, 2):
        for g in sets:
            ring_end(g, g["sslot"][dp], g["chip"](dp, 2))
    for made in wq_loads:
        made.wait()
    wo_load.wait()

    def go(phase):
        pl.semaphore_signal(go_sem, inc=1, device_id=at(jnp.minimum(phase, phases - 1), p), device_id_type=MESH)

    piece = width // 4

    def mine_at(k):
        return x_v.at[mine, pl.ds(k * piece, piece)]

    def theirs_at(k):
        return x_v.at[theirs, pl.ds(k * piece, piece)]

    res_copies = [
        copy(res_v.at[:, pl.ds(k * piece, piece)], mine_at(k), x_prev_slots[k], at(pass_to, p)) for k in range(4)
    ]

    def pass_residual():
        for k in range(4):
            recv(res_v.at[:, pl.ds(k * piece, piece)], res_slots[k])
            res_copies[k].start()

    pl.when(goes_early)(lambda: go(ph + RING))
    pl.when(does_far & (ph >= RING + 2))(help_far)
    pl.when(early_help)(help_halo)
    send_wop(turn_out, (ph_next, at(jnp.minimum(ph + 1, phases - 1), chip_at(0, -1))))

    wop_relay = [next(slots) for _ in range(4)]
    relays = []
    for k in range(4):
        relays.append(copy(wop_v.at[4 * j + k], wop_v.at[4 * j + k], wop_relay[k], sibling))
    x_relays = [copy(mine_at(k), mine_at(k), x_relay_slots[k], sibling) for k in range(4)]

    def take_wop(first):
        for k in (first, first + 1):
            recv(wop_v.at[4 * j + k], wop_slots[k])
            relays[k].start()

    def get_wop(first):
        for k in (first, first + 1):
            recv(wop_v.at[4 * (1 - j) + k], wop_relay[k])

    pl.when(ph > 0)(lambda: take_wop(0))
    pl.when(ph > 1)(lambda: take_wop(2))
    pl.when(ph > 0)(lambda: get_wop(0))
    pl.when(ph > 1)(lambda: get_wop(2))

    @pl.when(ph < 2)
    def _():
        x_load.wait()
        x_direct.wait_send()
        recv(x_v.at[theirs], x_slot)

    pl.when(passes)(pass_residual)
    bl_slots = [next(slots) for _ in range(4)]
    bl_relay_slots = [next(slots) for _ in range(4)]
    bl_relays = [copy(bl_v.at[4 * j + h], bl_v.at[4 * j + h], bl_relay_slots[h], sibling) for h in range(4)]
    step = 512 if width % 512 == 0 else width

    def add_squares(n, rounded):
        wide = rounded.astype(jnp.float32)
        wide = wide * wide
        lanes = wide[:, :HEAD]
        for m in range(HEAD, step, HEAD):
            lanes = lanes + wide[:, m:m + HEAD]
        sq_v[...] = lanes if n == 0 else sq_v[...] + lanes


    @pl.when(ph > 0)
    def _():
        mine_head, their_head = 4 * j, 4 * (1 - j)
        def take(h):
            recv(bl_v.at[mine_head + h], bl_slots[h])
            bl_relays[h].start()

        def project_heads(first):
            heads = [mine_head + first, mine_head + first + 1, their_head + first, their_head + first + 1]
            lhs = jnp.concatenate([bl_v[head] for head in heads], axis=1)
            for n in range(0, width, step):
                rhs = jnp.concatenate([wop_v[head, :, n:n + step] for head in heads], axis=0)
                part = jnp.dot(lhs, rhs, preferred_element_type=jnp.float32)
                if first == 0:
                    acc[:, n:n + step] = part
                else:
                    total = x_v[:, n:n + step].astype(jnp.float32) + (acc[:, n:n + step] + part)
                    total = total.astype(jnp.bfloat16)
                    x_v[:, n:n + step] = total
                    add_squares(n, total)

        take(0)
        take(1)

        @pl.when(ph >= 2)
        def _():
            for k in range(4):
                recv(mine_at(k), x_prev_slots[k])
                x_relays[k].start()

        pl.when(ph == 1)(lambda: take_wop(2))
        recv(bl_v.at[their_head], bl_relay_slots[0])
        recv(bl_v.at[their_head + 1], bl_relay_slots[1])
        take(2)
        project_heads(0)
        take(3)
        pl.when(ph == 1)(lambda: get_wop(2))

        recv(bl_v.at[their_head + 2], bl_relay_slots[2])
        recv(bl_v.at[their_head + 3], bl_relay_slots[3])

        @pl.when(ph >= 2)
        def _():
            for k in range(4):
                recv(theirs_at(k), x_relay_slots[k])
            for k in range(4):
                x_relays[k].wait_send()

        project_heads(2)

    @pl.when(is_first)
    def _():
        for n in range(0, width, step):
            add_squares(n, x_v[:, n:n + step])

    square = jnp.sum(sq_v[...], axis=1, keepdims=True)
    scale_rows = lax.rsqrt(square * (1.0 / width) + 1e-05)

    stream = x_v[...]

    def project(weights):
        return (jnp.dot(stream, weights, preferred_element_type=jnp.float32) * scale_rows).astype(jnp.bfloat16)

    def own_blocks(kind, h, first, count):
        return kv_v.at[h, kind, pl.ds((3 + first) * BLK, count * BLK), :]

    def begin(when, chosen):
        @pl.when(when)
        def _():
            for made in chosen:
                made.start()

        pending.extend((made, when) for made in chosen)

    def ahead(kind, heads):
        return [
            copy(own_blocks(kind, h, 1, 1), kv_v.at[h, kind, pl.ds(0, BLK), :], halo_slots[h][2 * kind + 1], next2)
            for h in heads
        ]

    def start_keys(heads):
        begin(has_next1, [
            copy(own_blocks(0, h, 0, 2), kv_v.at[h, 0, pl.ds(BLK, 2 * BLK), :], halo_slots[h][0], next1) for h in heads
        ])
        begin(has_next2 & high, ahead(0, heads))

    def start_values():
        direct, around = [], []
        for h in range(4):
            for b, slot in enumerate((halo_slots[h][2], late_slots[h])):
                direct.append(copy(own_blocks(1, h, b, 1), kv_v.at[h, 1, pl.ds((b + 1) * BLK, BLK), :], slot, next1))
                around.append(
                    copy(own_blocks(1, h, b, 1), rel_v.at[h, pl.ds(b * BLK, BLK), :], rel_slots[h][b], helper_of(p))
                )
        begin(has_next1 & high, around[2:] + direct[:2])
        begin(has_next1 & low & jnp.logical_not(is_first), around)
        begin(has_next1 & is_first, direct)
        begin(has_next2 & low, [
            copy(own_blocks(1, h, 1, 1), far_v.at[h], far_slots[h], far_chip) for h in range(4)
        ])
        begin(has_next2 & high, ahead(1, (0,)))

    for kind in (0, 1):
        made = project(jnp.concatenate([wkv_v[kind], wkv_v[2 + kind]], axis=1))
        for h in range(4):
            kv_v[h, kind, 3 * BLK:5 * BLK, :] = made[:, h * HEAD:(h + 1) * HEAD]
        if kind == 0:
            start_keys((0,))
    start_values()
    start_keys((1, 2, 3))
    made = project(jnp.concatenate([wq_v[0], wq_v[1]], axis=1))
    for h in range(4):
        q_v[h] = made[:, h * HEAD:(h + 1) * HEAD]

    bls_slots = [next(slots) for _ in range(4)]
    factor = math.log2(math.e) / math.sqrt(HEAD)

    def scored(h, i, keys, first):
        query = q_v[h, i * BLK:(i + 1) * BLK, :]
        scores = lax.dot_general(query, keys, (((1,), (1,)), ((), ())), preferred_element_type=jnp.float32)
        return scores * factor + bias_v[i, :, first:first + keys.shape[0]]

    def mix(weights, values):
        return jnp.dot(weights.astype(jnp.bfloat16), values, preferred_element_type=jnp.float32)

    near = ((0, 3 * BLK, 4 * BLK, 3 * BLK), (1, 3 * BLK, 5 * BLK, 2 * BLK))
    far = ((0, 0, 3 * BLK, 0), (1, BLK, 3 * BLK, 0))
    for h in range(4):
        scores = [scored(h, i, kv_v[h, 0, lo:hi, :], first) for i, lo, hi, first in near]
        tops = [jnp.max(part, axis=1, keepdims=True) for part in scores]
        weights = [jnp.exp2(part - top) for part, top in zip(scores, tops)]
        sums = [jnp.sum(part, axis=1, keepdims=True) for part in weights]
        for (i, lo, hi, _), part, top, total in zip(near, weights, tops, sums):
            rows = slice(i * BLK, (i + 1) * BLK)
            mix_v[h, rows, :] = mix(part, kv_v[h, 1, lo:hi, :])
            top_v[h, rows, :] = jnp.broadcast_to(top, (BLK, HEAD))
            sum_v[h, rows, :] = jnp.broadcast_to(total, (BLK, HEAD))

    for h in range(4):
        run(has_last1 & low, lambda h=h: recv(kv_v.at[h, 0, pl.ds(BLK, 2 * BLK), :], halo_slots[h][0]))
        send(kv_v.at[h, 0, pl.ds(2 * BLK, BLK), :], kv_v.at[h, 0, pl.ds(0, BLK), :], halo_slots[h][1], next1,
             low & has_last1 & has_next1)
    for h in range(4):
        run(has_last1 & high, lambda h=h: recv(kv_v.at[h, 0, pl.ds(BLK, 2 * BLK), :], halo_slots[h][0]))
        run(has_last1, lambda h=h: recv(kv_v.at[h, 1, pl.ds(BLK, BLK), :], halo_slots[h][2]))
        run(has_last1, lambda h=h: recv(kv_v.at[h, 1, pl.ds(2 * BLK, BLK), :], late_slots[h]))
        for kind in range(2):
            run(has_last2, lambda h=h, kind=kind: recv(kv_v.at[h, kind, pl.ds(0, BLK), :], halo_slots[h][2 * kind + 1]))
        scores = [scored(h, i, kv_v[h, 0, lo:hi, :], first) for i, lo, hi, first in far]
        before = [top_v[h, i * BLK:(i + 1) * BLK, :] for i in range(2)]
        tops = [jnp.maximum(jnp.max(part, axis=1, keepdims=True), old) for part, old in zip(scores, before)]
        weights = [
            jnp.exp2(part - jnp.concatenate([top] * (part.shape[1] // HEAD), axis=1)) for part, top in zip(scores, tops)
        ]
        sums = [jnp.sum(part, axis=1, keepdims=True) for part in weights]
        mixed = [mix(part, kv_v[h, 1, lo:hi, :]) for part, (_, lo, hi, _) in zip(weights, far)]
        for i in range(2):
            rows = slice(i * BLK, (i + 1) * BLK)
            shrink = jnp.exp2(before[i] - tops[i])
            total = sum_v[h, rows, :] * shrink + sums[i]
            blo_v[h, rows, :] = ((mix_v[h, rows, :] * shrink + mixed[i]) / total).astype(jnp.bfloat16)
        blended_last = copy(blo_v.at[h], bl_v.at[4 * j + h], bl_slots[h], ph_next)
        pl.when(ph + 1 < phases)(blended_last.start)
        if h < 3:
            pending.append((blended_last, ph + 1 < phases))
        send(blo_v.at[h, theirs, :], bls_v.at[h], bls_slots[h], sibling)

    pl.when(goes_late)(lambda: go(ph + RING - 1))

    for h in range(4):
        recv(bls_v.at[h], bls_slots[h])
    own = jnp.concatenate([blo_v[h, mine, :] for h in range(4)], axis=1)
    other = jnp.concatenate([bls_v[h] for h in range(4)], axis=1)
    for n in range(0, width, step):
        first = wo_v[pl.ds(4 * j, 4), :, n:n + step].reshape(4 * HEAD, step)
        second = wo_v[pl.ds(4 * (1 - j), 4), :, n:n + step].reshape(4 * HEAD, step)
        update = jnp.dot(own, first, preferred_element_type=jnp.float32)
        update = update + jnp.dot(other, second, preferred_element_type=jnp.float32)
        out_ref[:, n:n + step] = (x_v[mine, n:n + step].astype(jnp.float32) + update).astype(jnp.bfloat16)
    pl.when(ph + 1 < phases)(blended_last.wait_send)
    for k in range(4):
        part = out_ref.at[:, pl.ds(k * piece, piece)]
        send(part, mine_at(k), x_prev_slots[k], ph_next2, res_direct)
        send(part, res_v.at[:, pl.ds(k * piece, piece)], res_slots[k], at(res_via, p), res_even)

    pl.when(late_help)(help_halo)
    for made, when in pending + rel_copies + far_copies + [(via_mid, turn_out), (via_end, ph == 2)] + [(made, passes) for made in res_copies]:
        if when is None:
            made.wait_send()
        else:
            pl.when(when)(made.wait_send)

    @pl.when(ph > 0)
    def _():
        for made in relays + bl_relays:
            made.wait_send()


def solution(mesh):
    phases, devices = mesh.shape["phase"], mesh.shape["ctx"]
    chips = devices // 2

    def local(inputs, segment_ids, w_query, w_keyval, w_out):
        width = inputs.shape[2]
        rows_dev = w_keyval.shape[1]
        any_space = pl.BlockSpec(memory_space=pl.ANY)
        n_slots = 144
        made = pl.pallas_call(
            functools.partial(kernel, phases, chips),
            out_shape=jax.ShapeDtypeStruct((BLK, width), jnp.bfloat16),
            in_specs=[any_space, pl.BlockSpec(memory_space=pltpu.VMEM)] + [any_space] * 3,
            out_specs=pl.BlockSpec(memory_space=pltpu.VMEM),
            scratch_shapes=[
                pltpu.VMEM((2 * BLK, width), jnp.bfloat16),
                pltpu.VMEM((2 * BLK, width), jnp.float32),
                pltpu.VMEM((2, width, 2 * HEAD), jnp.bfloat16),
                pltpu.VMEM((4, width, 2 * HEAD), jnp.bfloat16),
                pltpu.VMEM((8, HEAD, width), jnp.bfloat16),
                pltpu.VMEM((8, HEAD, width), jnp.bfloat16),
                pltpu.VMEM((4, 2 * BLK, HEAD), jnp.bfloat16),
                pltpu.VMEM((4, 2, 5 * BLK, HEAD), jnp.bfloat16),
                pltpu.VMEM((8, 2 * BLK, HEAD), jnp.bfloat16),
                pltpu.VMEM((4, 2 * BLK, HEAD), jnp.bfloat16),
                pltpu.VMEM((4, BLK, HEAD), jnp.bfloat16),
                pltpu.VMEM((5, 8, BLK), jnp.float32),
                pltpu.VMEM((2, BLK, 4 * BLK), jnp.float32),
                pltpu.VMEM((4, 2 * BLK, HEAD), jnp.bfloat16),
                pltpu.VMEM((4, BLK, HEAD), jnp.bfloat16),
                pltpu.VMEM((HEAD, width), jnp.bfloat16),
                pltpu.VMEM((BLK, width), jnp.bfloat16),
                pltpu.VMEM((2 * BLK, HEAD), jnp.float32),
                pltpu.VMEM((4, 2 * BLK, HEAD), jnp.float32),
                pltpu.VMEM((4, 2 * BLK, HEAD), jnp.float32),
                pltpu.VMEM((4, 2 * BLK, HEAD), jnp.float32),
                pltpu.SemaphoreType.DMA((n_slots,)),
                pltpu.SemaphoreType.DMA((n_slots,)),
                pltpu.SemaphoreType.DMA((16,)),
                pltpu.SemaphoreType.REGULAR,
            ],
            compiler_params=pltpu.CompilerParams(
                collective_id=0, has_side_effects=True, vmem_limit_bytes=56 * 1024 * 1024
            ),
        )(
            inputs.reshape(BLK, width), segment_ids, w_query.reshape(width, -1),
            w_keyval.reshape(rows_dev, -1), w_out.reshape(8, HEAD, width),
        )
        return made.reshape(1, 1, BLK, width)

    placed = (
        P(None, "ctx", None),
        P(None, "ctx"),
        P("phase", None, None),
        P("phase", "ctx", None),
        P("phase", None, None),
    )
    return jax.shard_map(
        local, mesh=mesh, in_specs=placed, out_specs=P("phase", None, "ctx", None), check_vma=False
    )
```

```python
import functools
import math

import jax
import jax.numpy as jnp
from jax import lax
from jax.experimental import pallas as pl
from jax.experimental.pallas import tpu as pltpu
from jax.sharding import PartitionSpec as P

MESH = pl.DeviceIdType.MESH
HEAD = 128
BLK = 128
RING = 4


def kernel(
    phases, chips, x_in, seg_in, wq_in, wkv_in, wo_in, out_ref,
    x_v, acc, wq_v, wkv_v, wo_v, wop_v, q_v, kv_v, bl_v, blo_v, bls_v, seg_v, bias_v, rel_v, far_v, via_v, res_v, sq_v, mix_v, top_v, sum_v,
    ssem, rsem, lsem, go_sem,
):
    width = x_v.shape[1]
    rows_dev = wkv_in.shape[0]
    rows_chip = 2 * rows_dev
    ph = lax.axis_index("phase")
    c = lax.axis_index("ctx")
    p = c // 2
    j = c % 2
    y = p // RING
    z = p % RING
    sib = c + 1 - 2 * j

    def at(phase, chip):
        return {"phase": phase, "ctx": chip * 2 + j}

    sibling = {"phase": ph, "ctx": sib}

    def chip_at(dy, dz):
        return ((y + dy + RING) % RING) * RING + (z + dz + RING) % RING

    y_next, y_prev = at(ph, chip_at(1, 0)), at(ph, chip_at(-1, 0))
    z_next, z_prev = at(ph, chip_at(0, 1)), at(ph, chip_at(0, -1))
    next1, next2 = at(ph, jnp.minimum(p + 1, chips - 1)), at(ph, jnp.minimum(p + 2, chips - 1))
    last1, last2 = at(ph, jnp.maximum(p - 1, 0)), at(ph, jnp.maximum(p - 2, 0))
    ph_next, ph_prev = at(jnp.minimum(ph + 1, phases - 1), p), at(jnp.maximum(ph - 1, 0), p)
    goer = jnp.where(ph < RING + 2, jnp.maximum(ph - RING + 1, 0), ph - RING)
    has_next1, has_next2 = p + 1 < chips, p + 2 < chips
    has_last1, has_last2 = p >= 1, p >= 2
    is_first, is_last = ph == 0, ph == phases - 1
    has_under = ph >= RING
    goes_late, goes_early = (ph == 1) | (ph == 2), (ph == 2) | (ph == 3)
    early_help, late_help = ph == 2 * RING - 1, (ph % RING < RING - 1)
    has_helper, has_helped = ph > 0, ph != RING - 1
    helper = jnp.where(ph == RING, 2 * RING - 1, jnp.maximum(ph - 1, 0))
    helped = jnp.where(early_help, RING, jnp.minimum(ph + 1, phases - 1))
    row_end = z == RING - 1
    helper_chip = jnp.where(row_end, jnp.minimum(p + RING, chips - 1), p)
    helped_chip = jnp.where(row_end, jnp.maximum(p - RING, 0), p)
    helped_to1, helped_to2 = jnp.minimum(helped_chip + 1, chips - 1), jnp.minimum(helped_chip + 2, chips - 1)
    has_helped = has_helped & (jnp.logical_not(row_end) | (p >= RING))
    helped1, helped2 = has_helped & (helped_chip + 1 < chips), has_helped & (helped_chip + 2 < chips)

    def helper_of(chip):
        chip = jnp.maximum(chip, 0)
        return at(helper, jnp.where(chip % RING == RING - 1, jnp.minimum(chip + RING, chips - 1), chip))

    res_out, res_in = ph + 2 < phases, ph >= 2
    res_even = res_out & (ph % RING == 0)
    res_direct = res_out & (ph % RING != 0)
    res_via = jnp.minimum(ph + RING - 1, phases - 1)
    passes = ph % RING == RING - 1
    pass_from = jnp.maximum(ph - RING + 1, 0)
    pass_to = jnp.minimum(pass_from + 2, phases - 1)
    res_back = jnp.minimum(ph + 1, phases - 1)
    res_around = ph % RING == 2
    ph_next2, ph_prev2 = at(jnp.minimum(ph + 2, phases - 1), p), at(jnp.maximum(ph - 2, 0), p)
    low, high = ph < RING, ph >= RING
    def far_of(chip):
        chip = jnp.clip(chip, 0, chips - 1)
        crossing = chip % RING >= 2
        row = jnp.minimum(chip // RING + jnp.where(crossing, 1, 0), RING - 1)
        return at(jnp.minimum(ph + RING, phases - 1), row * RING + (chip % RING + RING - 1) % RING)

    far_chip, far_back = far_of(p), far_of(p - 2)
    far_z = (z + 1) % RING
    far_row = y - jnp.where(far_z >= 2, 1, 0)
    far_from, far_phase = jnp.maximum(far_row, 0) * RING + far_z, jnp.maximum(ph - RING, 0)
    far_to = jnp.minimum(far_from + 2, chips - 1)
    does_far = high & (far_row >= 0) & (far_from + 2 < chips)
    turn_out, turn_in = ph == RING - 1, ph == RING

    barrier = pltpu.get_barrier_semaphore()
    for device in (sibling, y_next, y_prev, z_next, z_prev):
        pl.semaphore_signal(barrier, inc=1, device_id=device, device_id_type=MESH)
    count = jnp.int32(5)
    for device, there in (
        (next1, has_next1), (next2, has_next2), (last1, has_last1), (last2, has_last2),
        (ph_next, ph + 1 < phases), (ph_prev, ph > 0), (at(goer, p), has_under), (at(ph + RING - 1, p), goes_late), (at(jnp.minimum(ph + RING, phases - 1), p), goes_early),
        (far_chip, low & has_next2), (far_back, low & has_last2),
        (at(far_phase, far_from), does_far), (at(far_phase, far_to), does_far),
        (helper_of(p), has_helper & has_next1), (at(helped, helped_chip), helped1),
        (at(helped, helped_to1), helped1), (at(helped, helped_to2), helped2),
        (helper_of(p - 1), has_helper & has_last1), (helper_of(p - 2), has_helper & has_last2),
        (ph_next2, res_direct), (ph_prev2, res_in & jnp.logical_not(res_around)),
        (at(res_via, p), res_even), (at(pass_from, p), passes), (at(pass_to, p), passes),
        (at(res_back, p), res_around), (at(RING - 1, p), is_first), (at(0, p), turn_out),
        (at(jnp.minimum(ph + 1, phases - 1), chip_at(0, -1)), turn_out),
        (at(jnp.maximum(ph - 1, 0), chip_at(0, 1)), turn_in),
    ):
        @pl.when(there)
        def _(device=device):
            pl.semaphore_signal(barrier, inc=1, device_id=device, device_id_type=MESH)

        count = count + there.astype(jnp.int32)
    pl.semaphore_wait(barrier, count)

    pending = []
    slots = iter(range(ssem.shape[0]))

    def copy(src, dst, slot, device):
        return pltpu.make_async_remote_copy(
            src_ref=src, dst_ref=dst, send_sem=ssem.at[slot], recv_sem=rsem.at[slot],
            device_id=device, device_id_type=MESH,
        )

    def send(src, dst, slot, device, when=None):
        made = copy(src, dst, slot, device)
        if when is None:
            made.start()
        else:
            pl.when(when)(made.start)
        pending.append((made, when))
        return made

    def recv(dst, slot):
        copy(dst, dst, slot, sibling).wait_recv()

    def run(when, body):
        pl.when(when)(body)

    local = []

    def load(src, dst):
        made = pltpu.make_async_copy(src, dst, lsem.at[len(local)])
        made.start()
        local.append(made)
        return made

    def columns(core, tile):
        start = core * 4 * HEAD + (tile // 2) * 2 * HEAD + (tile % 2) * 8 * HEAD
        return pl.ds(pl.multiple_of(start, 2 * HEAD), 2 * HEAD)

    own_rows = pl.ds(pl.multiple_of(c * rows_dev, rows_dev), rows_dev)
    shard_loads = [load(wkv_in.at[:, columns(j, t)], wkv_v.at[t, own_rows, :]) for t in range(4)]
    seg_v[3 + j] = jnp.broadcast_to(seg_in[...].astype(jnp.float32), seg_v.shape[1:])
    mine = pl.ds(pl.multiple_of(j * BLK, BLK), BLK)
    theirs = pl.ds(pl.multiple_of((1 - j) * BLK, BLK), BLK)
    wq_loads = [
        load(wq_in.at[:, pl.ds(pl.multiple_of(j * 4 * HEAD + t * 2 * HEAD, 2 * HEAD), 2 * HEAD)], wq_v.at[t])
        for t in range(2)
    ]
    wo_load = load(wo_in, wo_v)

    halo_slots = [[next(slots) for _ in range(4)] for _ in range(4)]
    rel_slots = [[next(slots), next(slots)] for _ in range(4)]
    late_slots = [next(slots) for _ in range(4)]
    far_slots = [next(slots) for _ in range(4)]
    helped_high = helped >= RING
    rel_copies = []
    for h in range(4):
        needed = helped1 & (True if h > 0 else jnp.logical_not(helped_high))
        for b, slot in enumerate((halo_slots[h][2], late_slots[h])):
            rel_copies.append((copy(rel_v.at[h, pl.ds(b * BLK, BLK), :], kv_v.at[h, 1, pl.ds((b + 1) * BLK, BLK), :],
                                    slot, at(helped, helped_to1)), needed))
    for h in range(1, 4):
        rel_copies.append((copy(rel_v.at[h, pl.ds(BLK, BLK), :], kv_v.at[h, 1, pl.ds(0, BLK), :], halo_slots[h][3],
                                at(helped, helped_to2)), helped2 & helped_high))
    far_copies = [
        (copy(far_v.at[h], kv_v.at[h, 1, pl.ds(0, BLK), :], halo_slots[h][3], at(far_phase, far_to)), does_far)
        for h in range(4)
    ]

    def help_halo():
        for h in range(4):
            @pl.when(rel_copies[2 * h][1])
            def _(h=h):
                for b in range(2):
                    recv(rel_v.at[h, pl.ds(b * BLK, BLK), :], rel_slots[h][b])
                    rel_copies[2 * h + b][0].start()

            if h > 0:
                pl.when(rel_copies[h + 7][1])(rel_copies[h + 7][0].start)

    def help_far():
        for h in range(4):
            recv(far_v.at[h], far_slots[h])
            far_copies[h][0].start()

    sib_rows = pl.ds(pl.multiple_of(sib * rows_dev, rows_dev), rows_dev)
    shard_slots = [next(slots) for _ in range(4)]
    seg_slots = [next(slots) for _ in range(3)]

    for t in range(4):
        send(wkv_in.at[:, columns(1 - j, t)], wkv_v.at[t, own_rows, :], shard_slots[t], sibling)
    send(seg_v.at[3 + j], seg_v.at[3 + j], seg_slots[0], sibling)

    wop_slots = [next(slots) for _ in range(4)]

    def send_wop(when, devices):
        for k in range(4):
            send(wo_in.at[4 * j + k], wop_v.at[4 * j + k], wop_slots[k], devices[k // 2],
                 when & jnp.logical_not(is_first) if k == 3 else when)

    via_slots = [next(slots), next(slots)]
    via_mid = copy(via_v, via_v, via_slots[1], at(2, p))
    via_end = copy(via_v, wop_v.at[4 * j + 3], wop_slots[3], at(1, p))

    def pass_via(slot, made):
        recv(via_v, slot)
        made.start()

    send(wo_in.at[4 * j + 3], via_v, via_slots[0], at(RING - 1, p), is_first)
    send_wop((ph + 1 < phases) & jnp.logical_not(turn_out), (ph_next, ph_next))
    x_slot = next(slots)
    x_prev_slots = [next(slots) for _ in range(4)]
    x_relay_slots = [next(slots) for _ in range(4)]
    res_slots = [next(slots) for _ in range(4)]
    x_load = pltpu.make_async_copy(x_in, x_v.at[mine], lsem.at[len(local)])
    x_direct = copy(x_in, x_v.at[mine], x_slot, sibling)

    @pl.when(ph < 2)
    def _():
        x_load.start()
        x_direct.start()

    for made in shard_loads:
        made.wait()
    for t in range(4):
        recv(wkv_v.at[t, sib_rows, :], shard_slots[t])

    def slab(chip, first, count_):
        return wkv_v.at[pl.ds(first, count_), pl.ds(pl.multiple_of(chip * rows_chip, rows_chip), rows_chip), :]

    sets = []
    for s in range(2):
        sets.append(dict(
            tile=2 * s,
            prim=(y_next, y_prev) if s == 0 else (z_next, z_prev),
            sec=(z_next, z_prev) if s == 0 else (y_next, y_prev),
            chip=(lambda a, b: chip_at(a, b)) if s == 0 else (lambda a, b: chip_at(b, a)),
            pslot=[next(slots) for _ in range(4)],
            sslot={dp: [next(slots) for _ in range(4)] for dp in (0, -1, 1, 2)},
        ))

    def ring_send(g, ring, slot, dp):
        piece = slab(g["chip"](dp, 0), g["tile"], 2)
        send(piece, piece, slot[0], ring[0])
        send(piece, piece, slot[1], ring[1])

    def ring_forward(g, ring, slot, before, after):
        piece = slab(before, g["tile"], 2)
        recv(piece, slot[0])
        half = slab(before, g["tile"], 1)
        send(half, half, slot[2], ring[0])
        piece = slab(after, g["tile"], 2)
        recv(piece, slot[1])
        half = slab(after, g["tile"] + 1, 1)
        send(half, half, slot[3], ring[1])

    def ring_end(g, slot, far):
        recv(slab(far, g["tile"], 1), slot[2])
        recv(slab(far, g["tile"] + 1, 1), slot[3])

    recv(seg_v.at[4 - j], seg_slots[0])
    send(seg_v.at[pl.ds(3, 2)], seg_v.at[pl.ds(1, 2)], seg_slots[1], next1, has_next1)
    send(seg_v.at[4], seg_v.at[0], seg_slots[2], next2, has_next2)

    @pl.when(jnp.logical_not(has_last1))
    def _():
        seg_v[1:3] = jnp.full((2,) + seg_v.shape[1:], -1.0, jnp.float32)
        kv_v[:, :, BLK:3 * BLK, :] = jnp.zeros((4, 2, 2 * BLK, HEAD), jnp.bfloat16)

    @pl.when(jnp.logical_not(has_last2))
    def _():
        seg_v[0] = jnp.full(seg_v.shape[1:], -1.0, jnp.float32)
        kv_v[:, :, 0:BLK, :] = jnp.zeros((4, 2, BLK, HEAD), jnp.bfloat16)

    pl.when(does_far & (ph < RING + 2))(help_far)
    pl.when(has_under)(lambda: pl.semaphore_wait(go_sem, 1))
    for g in sets:
        ring_send(g, g["prim"], g["pslot"], 0)
        ring_send(g, g["sec"], g["sslot"][0], 0)
    run(has_last1, lambda: recv(seg_v.at[pl.ds(1, 2)], seg_slots[1]))
    run(has_last2, lambda: recv(seg_v.at[0], seg_slots[2]))

    row_id = lax.broadcasted_iota(jnp.int32, (BLK, BLK), 0)
    col_id = lax.broadcasted_iota(jnp.int32, (BLK, BLK), 1)
    causal = col_id <= row_id
    for i in range(2):
        asking = jnp.transpose(jnp.broadcast_to(seg_v[3 + i, 0:1, :], (BLK, BLK)))
        for b in range(4):
            asked = jnp.broadcast_to(seg_v[i + b, 0:1, :], (BLK, BLK))
            ok = asking == asked
            if b == 3:
                ok = ok & causal
            bias_v[i, :, b * BLK:(b + 1) * BLK] = jnp.where(ok, 0.0, -1e30).astype(jnp.float32)

    for g in sets:
        ring_forward(g, g["prim"], g["pslot"], g["chip"](-1, 0), g["chip"](1, 0))
        ring_send(g, g["sec"], g["sslot"][-1], -1)
        ring_send(g, g["sec"], g["sslot"][1], 1)
    for g in sets:
        ring_forward(g, g["sec"], g["sslot"][0], g["chip"](0, -1), g["chip"](0, 1))
    pl.when(turn_out)(lambda: pass_via(via_slots[0], via_mid))
    for g in sets:
        ring_end(g, g["pslot"], g["chip"](2, 0))
        ring_send(g, g["sec"], g["sslot"][2], 2)
    for dp in (-1, 1, 2):
        for g in sets:
            ring_forward(g, g["sec"], g["sslot"][dp], g["chip"](dp, -1), g["chip"](dp, 1))

    pl.when(ph == 2)(lambda: pass_via(via_slots[1], via_end))
    for dp in (0, -1, 1, 2):
        for g in sets:
            ring_end(g, g["sslot"][dp], g["chip"](dp, 2))
    for made in wq_loads:
        made.wait()
    wo_load.wait()

    def go(phase):
        pl.semaphore_signal(go_sem, inc=1, device_id=at(jnp.minimum(phase, phases - 1), p), device_id_type=MESH)

    piece = width // 4

    def mine_at(k):
        return x_v.at[mine, pl.ds(k * piece, piece)]

    def theirs_at(k):
        return x_v.at[theirs, pl.ds(k * piece, piece)]

    res_copies = [
        copy(res_v.at[:, pl.ds(k * piece, piece)], mine_at(k), x_prev_slots[k], at(pass_to, p)) for k in range(4)
    ]

    def pass_residual():
        for k in range(4):
            recv(res_v.at[:, pl.ds(k * piece, piece)], res_slots[k])
            res_copies[k].start()

    pl.when(goes_early)(lambda: go(ph + RING))
    pl.when(does_far & (ph >= RING + 2))(help_far)
    pl.when(early_help)(help_halo)
    send_wop(turn_out, (ph_next, at(jnp.minimum(ph + 1, phases - 1), chip_at(0, -1))))

    wop_relay = [next(slots) for _ in range(4)]
    relays = []
    for k in range(4):
        relays.append(copy(wop_v.at[4 * j + k], wop_v.at[4 * j + k], wop_relay[k], sibling))
    x_relays = [copy(mine_at(k), mine_at(k), x_relay_slots[k], sibling) for k in range(4)]

    def take_wop(first):
        for k in (first, first + 1):
            recv(wop_v.at[4 * j + k], wop_slots[k])
            relays[k].start()

    def get_wop(first):
        for k in (first, first + 1):
            recv(wop_v.at[4 * (1 - j) + k], wop_relay[k])

    pl.when(ph > 0)(lambda: take_wop(0))
    pl.when(ph > 1)(lambda: take_wop(2))
    pl.when(ph > 0)(lambda: get_wop(0))
    pl.when(ph > 1)(lambda: get_wop(2))

    @pl.when(ph < 2)
    def _():
        x_load.wait()
        x_direct.wait_send()
        recv(x_v.at[theirs], x_slot)

    pl.when(passes)(pass_residual)
    bl_slots = [next(slots) for _ in range(4)]
    bl_relay_slots = [next(slots) for _ in range(4)]
    bl_relays = [copy(bl_v.at[4 * j + h], bl_v.at[4 * j + h], bl_relay_slots[h], sibling) for h in range(4)]
    step = 512 if width % 512 == 0 else width

    def add_squares(n, rounded):
        wide = rounded.astype(jnp.float32)
        wide = wide * wide
        lanes = wide[:, :HEAD]
        for m in range(HEAD, step, HEAD):
            lanes = lanes + wide[:, m:m + HEAD]
        sq_v[...] = lanes if n == 0 else sq_v[...] + lanes


    @pl.when(ph > 0)
    def _():
        mine_head, their_head = 4 * j, 4 * (1 - j)
        def take(h):
            recv(bl_v.at[mine_head + h], bl_slots[h])
            bl_relays[h].start()

        def project_heads(first):
            heads = [mine_head + first, mine_head + first + 1, their_head + first, their_head + first + 1]
            lhs = jnp.concatenate([bl_v[head] for head in heads], axis=1)
            for n in range(0, width, step):
                rhs = jnp.concatenate([wop_v[head, :, n:n + step] for head in heads], axis=0)
                part = jnp.dot(lhs, rhs, preferred_element_type=jnp.float32)
                if first == 0:
                    acc[:, n:n + step] = part
                else:
                    total = x_v[:, n:n + step].astype(jnp.float32) + (acc[:, n:n + step] + part)
                    total = total.astype(jnp.bfloat16)
                    x_v[:, n:n + step] = total
                    add_squares(n, total)

        take(0)
        take(1)

        @pl.when(ph >= 2)
        def _():
            for k in range(4):
                recv(mine_at(k), x_prev_slots[k])
                x_relays[k].start()

        pl.when(ph == 1)(lambda: take_wop(2))
        recv(bl_v.at[their_head], bl_relay_slots[0])
        recv(bl_v.at[their_head + 1], bl_relay_slots[1])
        take(2)
        project_heads(0)
        take(3)
        pl.when(ph == 1)(lambda: get_wop(2))

        recv(bl_v.at[their_head + 2], bl_relay_slots[2])
        recv(bl_v.at[their_head + 3], bl_relay_slots[3])

        @pl.when(ph >= 2)
        def _():
            for k in range(4):
                recv(theirs_at(k), x_relay_slots[k])
            for k in range(4):
                x_relays[k].wait_send()

        project_heads(2)

    @pl.when(is_first)
    def _():
        for n in range(0, width, step):
            add_squares(n, x_v[:, n:n + step])

    square = jnp.sum(sq_v[...], axis=1, keepdims=True)
    scale_rows = lax.rsqrt(square * (1.0 / width) + 1e-05)

    stream = x_v[...]

    def project(weights):
        return (jnp.dot(stream, weights, preferred_element_type=jnp.float32) * scale_rows).astype(jnp.bfloat16)

    def own_blocks(kind, h, first, count):
        return kv_v.at[h, kind, pl.ds((3 + first) * BLK, count * BLK), :]

    def begin(when, chosen):
        @pl.when(when)
        def _():
            for made in chosen:
                made.start()

        pending.extend((made, when) for made in chosen)

    def ahead(kind, heads):
        return [
            copy(own_blocks(kind, h, 1, 1), kv_v.at[h, kind, pl.ds(0, BLK), :], halo_slots[h][2 * kind + 1], next2)
            for h in heads
        ]

    def start_keys(heads):
        begin(has_next1, [
            copy(own_blocks(0, h, 0, 2), kv_v.at[h, 0, pl.ds(BLK, 2 * BLK), :], halo_slots[h][0], next1) for h in heads
        ])
        begin(has_next2 & high, ahead(0, heads))

    def start_values():
        direct, around = [], []
        for h in range(4):
            for b, slot in enumerate((halo_slots[h][2], late_slots[h])):
                direct.append(copy(own_blocks(1, h, b, 1), kv_v.at[h, 1, pl.ds((b + 1) * BLK, BLK), :], slot, next1))
                around.append(
                    copy(own_blocks(1, h, b, 1), rel_v.at[h, pl.ds(b * BLK, BLK), :], rel_slots[h][b], helper_of(p))
                )
        begin(has_next1 & high, around[2:] + direct[:2])
        begin(has_next1 & low & jnp.logical_not(is_first), around)
        begin(has_next1 & is_first, direct)
        begin(has_next2 & low, [
            copy(own_blocks(1, h, 1, 1), far_v.at[h], far_slots[h], far_chip) for h in range(4)
        ])
        begin(has_next2 & high, ahead(1, (0,)))

    for kind in (0, 1):
        made = project(jnp.concatenate([wkv_v[kind], wkv_v[2 + kind]], axis=1))
        for h in range(4):
            kv_v[h, kind, 3 * BLK:5 * BLK, :] = made[:, h * HEAD:(h + 1) * HEAD]
        if kind == 0:
            start_keys((0,))
    start_values()
    start_keys((1, 2, 3))
    made = project(jnp.concatenate([wq_v[0], wq_v[1]], axis=1))
    for h in range(4):
        q_v[h] = made[:, h * HEAD:(h + 1) * HEAD]

    bls_slots = [next(slots) for _ in range(4)]
    factor = math.log2(math.e) / math.sqrt(HEAD)

    def scored(h, i, keys, first):
        query = q_v[h, i * BLK:(i + 1) * BLK, :]
        scores = lax.dot_general(query, keys, (((1,), (1,)), ((), ())), preferred_element_type=jnp.float32)
        return scores * factor + bias_v[i, :, first:first + keys.shape[0]]

    def mix(weights, values):
        return jnp.dot(weights.astype(jnp.bfloat16), values, preferred_element_type=jnp.float32)

    near = ((0, 3 * BLK, 4 * BLK, 3 * BLK), (1, 3 * BLK, 5 * BLK, 2 * BLK))
    far = ((0, 0, 3 * BLK, 0), (1, BLK, 3 * BLK, 0))
    for h in range(4):
        scores = [scored(h, i, kv_v[h, 0, lo:hi, :], first) for i, lo, hi, first in near]
        tops = [jnp.max(part, axis=1, keepdims=True) for part in scores]
        weights = [jnp.exp2(part - top) for part, top in zip(scores, tops)]
        sums = [jnp.sum(part, axis=1, keepdims=True) for part in weights]
        for (i, lo, hi, _), part, top, total in zip(near, weights, tops, sums):
            rows = slice(i * BLK, (i + 1) * BLK)
            mix_v[h, rows, :] = mix(part, kv_v[h, 1, lo:hi, :])
            top_v[h, rows, :] = jnp.broadcast_to(top, (BLK, HEAD))
            sum_v[h, rows, :] = jnp.broadcast_to(total, (BLK, HEAD))

    for h in range(4):
        run(has_last1 & low, lambda h=h: recv(kv_v.at[h, 0, pl.ds(BLK, 2 * BLK), :], halo_slots[h][0]))
        send(kv_v.at[h, 0, pl.ds(2 * BLK, BLK), :], kv_v.at[h, 0, pl.ds(0, BLK), :], halo_slots[h][1], next1,
             low & has_last1 & has_next1)
    for h in range(4):
        run(has_last1 & high, lambda h=h: recv(kv_v.at[h, 0, pl.ds(BLK, 2 * BLK), :], halo_slots[h][0]))
        run(has_last1, lambda h=h: recv(kv_v.at[h, 1, pl.ds(BLK, BLK), :], halo_slots[h][2]))
        run(has_last1, lambda h=h: recv(kv_v.at[h, 1, pl.ds(2 * BLK, BLK), :], late_slots[h]))
        for kind in range(2):
            run(has_last2, lambda h=h, kind=kind: recv(kv_v.at[h, kind, pl.ds(0, BLK), :], halo_slots[h][2 * kind + 1]))
        scores = [scored(h, i, kv_v[h, 0, lo:hi, :], first) for i, lo, hi, first in far]
        before = [top_v[h, i * BLK:(i + 1) * BLK, :] for i in range(2)]
        tops = [jnp.maximum(jnp.max(part, axis=1, keepdims=True), old) for part, old in zip(scores, before)]
        weights = [
            jnp.exp2(part - jnp.concatenate([top] * (part.shape[1] // HEAD), axis=1)) for part, top in zip(scores, tops)
        ]
        sums = [jnp.sum(part, axis=1, keepdims=True) for part in weights]
        mixed = [mix(part, kv_v[h, 1, lo:hi, :]) for part, (_, lo, hi, _) in zip(weights, far)]
        for i in range(2):
            rows = slice(i * BLK, (i + 1) * BLK)
            shrink = jnp.exp2(before[i] - tops[i])
            total = sum_v[h, rows, :] * shrink + sums[i]
            blo_v[h, rows, :] = ((mix_v[h, rows, :] * shrink + mixed[i]) / total).astype(jnp.bfloat16)
        blended_last = copy(blo_v.at[h], bl_v.at[4 * j + h], bl_slots[h], ph_next)
        pl.when(ph + 1 < phases)(blended_last.start)
        if h < 3:
            pending.append((blended_last, ph + 1 < phases))
        send(blo_v.at[h, theirs, :], bls_v.at[h], bls_slots[h], sibling)

    pl.when(goes_late)(lambda: go(ph + RING - 1))

    for h in range(4):
        recv(bls_v.at[h], bls_slots[h])
    own = jnp.concatenate([blo_v[h, mine, :] for h in range(4)], axis=1)
    other = jnp.concatenate([bls_v[h] for h in range(4)], axis=1)
    for n in range(0, width, step):
        first = wo_v[pl.ds(4 * j, 4), :, n:n + step].reshape(4 * HEAD, step)
        second = wo_v[pl.ds(4 * (1 - j), 4), :, n:n + step].reshape(4 * HEAD, step)
        update = jnp.dot(own, first, preferred_element_type=jnp.float32)
        update = update + jnp.dot(other, second, preferred_element_type=jnp.float32)
        out_ref[:, n:n + step] = (x_v[mine, n:n + step].astype(jnp.float32) + update).astype(jnp.bfloat16)
    pl.when((ph + 1 < phases) & (ph % 2 == 0))(blended_last.wait_send)
    for k in range(4):
        part = out_ref.at[:, pl.ds(k * piece, piece)]
        send(part, mine_at(k), x_prev_slots[k], ph_next2, res_direct)
        send(part, res_v.at[:, pl.ds(k * piece, piece)], res_slots[k], at(res_via, p), res_even)

    pl.when((ph + 1 < phases) & (ph % 2 == 1))(blended_last.wait_send)
    pl.when(late_help)(help_halo)
    for made, when in pending + rel_copies + far_copies + [(via_mid, turn_out), (via_end, ph == 2)] + [(made, passes) for made in res_copies]:
        if when is None:
            made.wait_send()
        else:
            pl.when(when)(made.wait_send)

    @pl.when(ph > 0)
    def _():
        for made in relays + bl_relays:
            made.wait_send()


def solution(mesh):
    phases, devices = mesh.shape["phase"], mesh.shape["ctx"]
    chips = devices // 2

    def local(inputs, segment_ids, w_query, w_keyval, w_out):
        width = inputs.shape[2]
        rows_dev = w_keyval.shape[1]
        any_space = pl.BlockSpec(memory_space=pl.ANY)
        n_slots = 144
        made = pl.pallas_call(
            functools.partial(kernel, phases, chips),
            out_shape=jax.ShapeDtypeStruct((BLK, width), jnp.bfloat16),
            in_specs=[any_space, pl.BlockSpec(memory_space=pltpu.VMEM)] + [any_space] * 3,
            out_specs=pl.BlockSpec(memory_space=pltpu.VMEM),
            scratch_shapes=[
                pltpu.VMEM((2 * BLK, width), jnp.bfloat16),
                pltpu.VMEM((2 * BLK, width), jnp.float32),
                pltpu.VMEM((2, width, 2 * HEAD), jnp.bfloat16),
                pltpu.VMEM((4, width, 2 * HEAD), jnp.bfloat16),
                pltpu.VMEM((8, HEAD, width), jnp.bfloat16),
                pltpu.VMEM((8, HEAD, width), jnp.bfloat16),
                pltpu.VMEM((4, 2 * BLK, HEAD), jnp.bfloat16),
                pltpu.VMEM((4, 2, 5 * BLK, HEAD), jnp.bfloat16),
                pltpu.VMEM((8, 2 * BLK, HEAD), jnp.bfloat16),
                pltpu.VMEM((4, 2 * BLK, HEAD), jnp.bfloat16),
                pltpu.VMEM((4, BLK, HEAD), jnp.bfloat16),
                pltpu.VMEM((5, 8, BLK), jnp.float32),
                pltpu.VMEM((2, BLK, 4 * BLK), jnp.float32),
                pltpu.VMEM((4, 2 * BLK, HEAD), jnp.bfloat16),
                pltpu.VMEM((4, BLK, HEAD), jnp.bfloat16),
                pltpu.VMEM((HEAD, width), jnp.bfloat16),
                pltpu.VMEM((BLK, width), jnp.bfloat16),
                pltpu.VMEM((2 * BLK, HEAD), jnp.float32),
                pltpu.VMEM((4, 2 * BLK, HEAD), jnp.float32),
                pltpu.VMEM((4, 2 * BLK, HEAD), jnp.float32),
                pltpu.VMEM((4, 2 * BLK, HEAD), jnp.float32),
                pltpu.SemaphoreType.DMA((n_slots,)),
                pltpu.SemaphoreType.DMA((n_slots,)),
                pltpu.SemaphoreType.DMA((16,)),
                pltpu.SemaphoreType.REGULAR,
            ],
            compiler_params=pltpu.CompilerParams(
                collective_id=0, has_side_effects=True, vmem_limit_bytes=56 * 1024 * 1024
            ),
        )(
            inputs.reshape(BLK, width), segment_ids, w_query.reshape(width, -1),
            w_keyval.reshape(rows_dev, -1), w_out.reshape(8, HEAD, width),
        )
        return made.reshape(1, 1, BLK, width)

    placed = (
        P(None, "ctx", None),
        P(None, "ctx"),
        P("phase", None, None),
        P("phase", "ctx", None),
        P("phase", None, None),
    )
    return jax.shard_map(
        local, mesh=mesh, in_specs=placed, out_specs=P("phase", None, "ctx", None), check_vma=False
    )
```
